32 devices in a mesh: row: 8 (over z, x), col: 4 (over y, core).
Axes of the slice: x: 2, y: 2, z: 4, core: 2. Of those that a mesh axis runs over, the one named last changes fastest.
Arguments:
- object_field: float32 [2, 3072, 1536], P(None, 'row', 'col'), may hold values from -6 to 6
- probe: float32 [2, 256, 256], replicated, may hold values from -5 to 5
- amplitudes: float32 [4096, 2048], P('row', 'col'), may hold values from 0.2 to 3
- offsets: int32 [16, 8, 2], P('row', 'col'), may hold values from 0 to 128, as said below
Outputs:
- updated_object: float32 [2, 3072, 1536], P(None, 'row', 'col')
The draws below stay inside these ranges and needn't reach their ends.
Inputs may be any that keep to these rules, and one draw needn't show every extreme that they name: Both offsets of every scan position lie in 0 to 128, and each end of that range is taken in every draw.
All inputs are finite; a program needn't handle non-finite values.
Results may differ from the reference program's by a relative error of at most 0.0003.
Values sent between devices are 32-bit elements; how exact they have to be, the bound alone decides.
No kernel may reach another device: no remote copies, remote signals or barrier semaphores. Data moves between devices by JAX's collectives and lax.ppermute only.
A program may use at most 64 MiB of HBM per device.

```python
import math
import jax
import jax.numpy as jnp
from jax import lax

TILE = 384
WIN = 256
MARGIN = 96
ITERS = 2
PITCH = 192
SCAN_ROWS = 16
SCAN_COLS = 8
OBJ_ROWS = 3072
OBJ_COLS = 1536
AMP_ROWS = 4096
AMP_COLS = 2048


def draw_offsets(key, part):
    top = 2 * MARGIN + TILE - PITCH - WIN
    values = jax.random.randint(key, (SCAN_ROWS, SCAN_COLS, 2), 0, top + 1)
    values = values.at[0, 0, 0].set(0).at[0, 0, 1].set(top)
    values = values.at[SCAN_ROWS - 1, SCAN_COLS - 1, 0].set(top).at[SCAN_ROWS - 1, SCAN_COLS - 1, 1].set(0)
    return values.astype(jnp.int32)


def level_of(stream_key, dims, pieces, smallest, high):
    gain, own = 1.0, jax.random.fold_in(stream_key, 6)
    for axis_at, blocks in pieces:
        draws = jnp.exp(jax.random.uniform(jax.random.fold_in(own, axis_at), (blocks,), jnp.float32, smallest / len(pieces), high / len(pieces)))
        gain = gain * jnp.repeat(draws, dims[axis_at] // blocks).reshape([-1 if axis == axis_at else 1 for axis in range(len(dims))])
    return gain


def normal_values(own_key, extent, deviation, reach, shards=(), held_as=jnp.bfloat16):
    result = deviation * jax.random.normal(own_key, extent, jnp.float32)
    if shards:
        result = result * level_of(own_key, extent, shards, -0.22, 0.18)
    return jnp.clip(result, -reach, reach).astype(held_as)


def setup_inputs(seed: int = 0) -> dict:
    arg_keys = jax.random.split(jax.random.key(seed), 5)
    object_field = normal_values(arg_keys[0], (2, OBJ_ROWS, OBJ_COLS), 1.0, 6.0, ((1, 8), (2, 4)), jnp.float32)
    probe = normal_values(arg_keys[1], (2, WIN, WIN), 0.7, 5.0, (), jnp.float32)
    amplitudes = jnp.clip(jnp.exp(math.log(3.0) - 2.7080502 * jax.random.uniform(arg_keys[2], (AMP_ROWS, AMP_COLS), jnp.float32) ** level_of(arg_keys[2], (AMP_ROWS, AMP_COLS), ((0, 8), (1, 4)), -0.2, 0.2)), 0.2, 3.0)
    offsets = draw_offsets(jax.random.fold_in(arg_keys[4], 71), 0)
    return {"object_field": object_field, "probe": probe, "amplitudes": amplitudes, "offsets": offsets}


step_size = 0.3
tv_weight = 0.2
tv_smooth = 0.1
amp_floor = 0.5

def tv_from_extended(extended):
    base = extended[:, :-1, :-1]
    diff_down = extended[:, 1:, :-1] - base
    diff_right = extended[:, :-1, 1:] - base
    scale = jnp.sqrt(lax.optimization_barrier(jnp.sum(diff_down * diff_down + diff_right * diff_right, axis=0)) + tv_smooth)
    flow_down = diff_down / scale
    flow_right = diff_right / scale
    return flow_down[:, :-1, 1:] - flow_down[:, 1:, 1:] + flow_right[:, 1:, :-1] - flow_right[:, 1:, 1:]

def window_gradient(window, probe, amp):
    probe_c = probe[0] + 1j * probe[1]
    field = probe_c * (window[0] + 1j * window[1])
    spectrum = jnp.fft.fft2(field, norm='ortho')
    magnitude = jnp.abs(spectrum)
    misfit = spectrum * (1.0 - amp / jnp.maximum(magnitude, amp_floor))
    back = jnp.fft.ifft2(misfit, norm='ortho')
    grad = jnp.conj(probe_c) * back
    return jnp.stack([jnp.real(grad), jnp.imag(grad)])

def reference(object_field, probe, amplitudes, offsets):
    amp_tiles = amplitudes.reshape(SCAN_ROWS, WIN, SCAN_COLS, WIN).transpose(0, 2, 1, 3).reshape(-1, WIN, WIN)
    offset_list = offsets.reshape(-1, 2)
    numbers = jnp.arange(SCAN_ROWS * SCAN_COLS, dtype=jnp.int32)
    obj = object_field
    zero = jnp.int32(0)
    for step in range(ITERS):
        padded = jnp.pad(obj, ((0, 0), (MARGIN, MARGIN), (MARGIN, MARGIN)))

        def visit(canvas, item):
            number, offset, amp = item
            start_row = (number // SCAN_COLS * PITCH + offset[0]).astype(jnp.int32)
            start_col = (number % SCAN_COLS * PITCH + offset[1]).astype(jnp.int32)
            window = lax.dynamic_slice(padded, (zero, start_row, start_col), (2, WIN, WIN))
            grad = window_gradient(window, probe, amp)
            piece = lax.dynamic_slice(canvas, (zero, start_row, start_col), (2, WIN, WIN))
            canvas = lax.dynamic_update_slice(canvas, piece + grad, (zero, start_row, start_col))
            return (canvas, None)
        canvas, _ = lax.scan(visit, jnp.zeros_like(padded), (numbers, offset_list, amp_tiles))
        grad = canvas[:, MARGIN:MARGIN + OBJ_ROWS, MARGIN:MARGIN + OBJ_COLS]
        edged = jnp.pad(obj, ((0, 0), (1, 1), (1, 1)))
        obj = obj - step_size * (grad + tv_weight * tv_from_extended(edged))
    return obj
```

```python
import functools
import math

import jax
import jax.numpy as jnp
import numpy as np
from jax import lax
from jax.experimental import pallas as pl
from jax.experimental.pallas import tpu as pltpu
from jax.sharding import PartitionSpec as P

WIN = 256
HALF = 128
MARGIN = 96
LANE = 128

step_size = 0.3
tv_weight = 0.2
tv_smooth = 0.1
amp_floor = 0.5

F32 = jnp.float32
BF16 = jnp.bfloat16


def tables():
    counter = np.arange(HALF)
    angle = (counter[:, None] * counter[None, :] % HALF) * (2.0 * math.pi / HALF)
    cosine = np.cos(angle) / math.sqrt(WIN)
    sine = np.sin(angle) / math.sqrt(WIN)
    first = np.block([[cosine, sine], [-sine, cosine]])
    second = np.block([[cosine, -sine], [sine, cosine]])
    parts = []
    for table in (first, second):
        table = table.astype(np.float32)
        high = table.astype(jnp.bfloat16)
        low = (table - high.astype(np.float32)).astype(jnp.bfloat16)
        parts += [high, low]
    turn = counter * (2.0 * math.pi / WIN)
    rows = np.stack([np.cos(turn), np.sin(turn)])
    by_row = np.broadcast_to(rows[:, :, None], (2, HALF, HALF))
    by_lane = np.broadcast_to(rows[:, None, :], (2, HALF, HALF))
    twiddle = np.concatenate([by_row, by_lane]).astype(np.float32)
    order = np.zeros((WIN, WIN), np.float32)
    for parity in range(2):
        order[2 * counter + parity, parity * HALF + counter] = 1.0
    return np.stack(parts), twiddle, order.astype(jnp.bfloat16)


def split(value):
    high = value.astype(BF16)
    return high, (value - high.astype(F32)).astype(BF16)


def mul(left, right):
    return jnp.dot(left, right, preferred_element_type=F32)


def vmem(count):
    return [pl.BlockSpec(memory_space=pltpu.VMEM)] * count


def prepare_kernel(off_ref, probe_ref, amp_ref, order_ref, probes_ref, amps_ref, parts_ref):
    order = order_ref[...]
    for i in range(2):
        for j in range(2):
            row = off_ref[i, j, 0]
            col = off_ref[i, j, 1] + (32 if j == 0 else 96)
            for channel in range(2):
                turned = pltpu.roll(probe_ref[channel], row, 0)
                probes_ref[2 * i + j, channel] = pltpu.roll(turned, col, 1)
            amp = amp_ref[i * WIN : (i + 1) * WIN, j * WIN : (j + 1) * WIN]
            high, rest = split(amp)
            middle, low = split(amp - high.astype(F32) - rest.astype(F32))
            sorted_lanes = mul(high, order) + mul(rest, order) + mul(middle, order)
            for q in range(2):
                parts_ref[...] = sorted_lanes[:, q * HALF : (q + 1) * HALF]
                for p in range(2):
                    at = q * WIN + p * HALF
                    amps_ref[2 * i + j, at : at + HALF, :] = parts_ref[pl.ds(p, HALF, stride=2), :]


def prepare(offsets, probe, amplitudes, order):
    return pl.pallas_call(
        prepare_kernel,
        out_shape=(
            jax.ShapeDtypeStruct((4, 2, WIN, WIN), F32),
            jax.ShapeDtypeStruct((4, 2 * WIN, HALF), F32),
        ),
        in_specs=[pl.BlockSpec(memory_space=pltpu.SMEM)] + vmem(3),
        out_specs=tuple(vmem(2)),
        scratch_shapes=[pltpu.VMEM((WIN, HALF), F32)],
        cost_estimate=pl.CostEstimate(flops=400_000_000, bytes_accessed=6_000_000, transcendentals=0),
        name="prepare",
    )(offsets, probe, amplitudes, order)


def windows_kernel(i, plan, acc_at, outs, off_ref, tab_ref, tw_ref, probes_ref, amps_ref, *refs):
    operands = sum(len(part) for part in plan)
    ins, refs = refs[:operands], refs[operands:]
    carried = ()
    if acc_at is not None:
        carried, refs = refs[:3], refs[3:]
    out_refs, refs = refs[: 3 * len(outs)], refs[3 * len(outs) :]
    reg, can, gh, gl, hh, hl, wide, tall = refs
    spans = ((0, LANE), (LANE, 4 * LANE), (4 * LANE, 5 * LANE))

    which = 0
    for part, (lo, hi) in zip(plan, spans):
        row = 0
        for first, rows in part:
            for channel in range(2):
                reg[channel, row : row + rows, lo:hi] = ins[which][channel, first : first + rows, :]
            row += rows
            which += 1

    can[...] = jnp.zeros_like(can)
    if acc_at is not None:
        for ref, (lo, hi) in zip(carried, spans):
            for channel in range(2):
                can[channel, acc_at : acc_at + 192, lo:hi] = ref[channel]

    def variation(step, _):
        base = pl.multiple_of(MARGIN - 8 + step * 32, 8)
        flows = []
        power = tv_smooth
        for channel in range(2):
            block = reg[channel, pl.ds(base, 48), :]
            down = pltpu.roll(block, 47, 0) - block
            right = pltpu.roll(block, 5 * LANE - 1, 1) - block
            power = power + down * down + right * right
            flows.append((down, right))
        inverse = lax.rsqrt(power)
        for channel in range(2):
            down, right = flows[channel]
            down = down * inverse
            right = right * inverse
            change = pltpu.roll(down, 1, 0) - down + pltpu.roll(right, 1, 1) - right
            at = pl.multiple_of(base + 8, 8)
            here = (channel, pl.ds(at, 32), slice(LANE, 4 * LANE))
            can[here] = can[here] + tv_weight * change[8:40, LANE : 4 * LANE]
        return 0

    lax.fori_loop(0, 6, variation, 0)

    row_iota = lax.broadcasted_iota(jnp.int32, (HALF, HALF), 0)
    lane_iota = lax.broadcasted_iota(jnp.int32, (HALF, HALF), 1)
    first_h, first_l, second_h, second_l = (tab_ref[n] for n in range(4))

    def store_split(high_ref, low_ref, at, value):
        high, low = split(value)
        high_ref[at] = high
        low_ref[at] = low

    def window(j, _):
        row_start = off_ref[i, j, 0]
        col_start = off_ref[i, j, 1] + 32 + 64 * j
        in_row = row_iota >= row_start

        def lanes(cb):
            return pl.ds(pl.multiple_of((j + cb) * LANE, LANE), LANE)

        number = 2 * i + j
        for cb in range(2):
            in_col = lane_iota + cb * LANE >= col_start
            field = []
            for rb in range(2):
                value = []
                for channel in range(2):
                    near = reg[channel, rb * HALF : (rb + 1) * HALF, lanes(cb)]
                    far = reg[channel, rb * HALF : (rb + 1) * HALF, lanes(cb + 2)]
                    picked = jnp.where(in_col, near, far)
                    if rb == 0:
                        near = reg[channel, WIN : WIN + HALF, lanes(cb)]
                        far = reg[channel, WIN : WIN + HALF, lanes(cb + 2)]
                        picked = jnp.where(in_row, picked, jnp.where(in_col, near, far))
                    value.append(picked)
                box = (slice(rb * HALF, (rb + 1) * HALF), slice(cb * LANE, (cb + 1) * LANE))
                p_re = probes_ref[(number, 0) + box]
                p_im = probes_ref[(number, 1) + box]
                field.append((p_re * value[0] - p_im * value[1], p_re * value[1] + p_im * value[0]))
            (re0, im0), (re1, im1) = field
            even = slice(cb * LANE, (cb + 1) * LANE)
            odd = slice(WIN + cb * LANE, WIN + (cb + 1) * LANE)
            store_split(gh, gl, (slice(0, HALF), even), re0 + re1)
            store_split(gh, gl, (slice(HALF, WIN), even), im0 + im1)
            d_re = re0 - re1
            d_im = im0 - im1
            tw_c, tw_s = tw_ref[0], tw_ref[1]
            store_split(gh, gl, (slice(0, HALF), odd), d_re * tw_c + d_im * tw_s)
            store_split(gh, gl, (slice(HALF, WIN), odd), d_im * tw_c - d_re * tw_s)
        g_h = gh[...]
        wide[...] = mul(first_h, g_h) + mul(first_h, gl[...]) + mul(first_l, g_h)

        tl_c, tl_s = tw_ref[2], tw_ref[3]
        re_l, im_l = slice(0, HALF), slice(HALF, WIN)
        for p in range(2):
            c0 = slice(p * WIN, p * WIN + LANE)
            c1 = slice(p * WIN + LANE, (p + 1) * WIN)
            re0, re1 = wide[:HALF, c0], wide[:HALF, c1]
            im0, im1 = wide[HALF:, c0], wide[HALF:, c1]
            rows = slice(p * HALF, (p + 1) * HALF)
            store_split(hh, hl, (rows, re_l), re0 + re1)
            store_split(hh, hl, (rows, im_l), im0 + im1)
            d_re = re0 - re1
            d_im = im0 - im1
            rows = slice(WIN + p * HALF, WIN + (p + 1) * HALF)
            store_split(hh, hl, (rows, re_l), d_re * tl_c + d_im * tl_s)
            store_split(hh, hl, (rows, im_l), d_im * tl_c - d_re * tl_s)
        h_h = hh[...]
        tall[...] = mul(h_h, second_h) + mul(hl[...], second_h) + mul(h_h, second_l)

        for n in range(4):
            rows = slice(n * HALF, (n + 1) * HALF)
            re, im = tall[rows, re_l], tall[rows, im_l]
            power = jnp.maximum(re * re + im * im, amp_floor * amp_floor)
            keeping = 1.0 - amps_ref[number, rows, :] * lax.rsqrt(power)
            store_split(hh, hl, (rows, re_l), re * keeping)
            store_split(hh, hl, (rows, im_l), im * keeping)
        h_h = hh[...]
        tall[...] = mul(h_h, first_h) + mul(hl[...], first_h) + mul(h_h, first_l)

        for p in range(2):
            rows = slice(p * HALF, (p + 1) * HALF)
            u_re, u_im = tall[rows, re_l], tall[rows, im_l]
            rows = slice(WIN + p * HALF, WIN + (p + 1) * HALF)
            v_re, v_im = tall[rows, re_l], tall[rows, im_l]
            w_re = v_re * tl_c - v_im * tl_s
            w_im = v_im * tl_c + v_re * tl_s
            c0 = slice(p * WIN, p * WIN + LANE)
            c1 = slice(p * WIN + LANE, (p + 1) * WIN)
            store_split(gh, gl, (re_l, c0), u_re + w_re)
            store_split(gh, gl, (re_l, c1), u_re - w_re)
            store_split(gh, gl, (im_l, c0), u_im + w_im)
            store_split(gh, gl, (im_l, c1), u_im - w_im)
        g_h = gh[...]
        wide[...] = mul(second_h, g_h) + mul(second_h, gl[...]) + mul(second_l, g_h)

        tw_c, tw_s = tw_ref[0], tw_ref[1]
        for cb in range(2):
            in_col = lane_iota + cb * LANE >= col_start
            c0 = slice(cb * LANE, (cb + 1) * LANE)
            c1 = slice(WIN + cb * LANE, WIN + (cb + 1) * LANE)
            u_re, u_im = wide[:HALF, c0], wide[HALF:, c0]
            v_re, v_im = wide[:HALF, c1], wide[HALF:, c1]
            w_re = v_re * tw_c - v_im * tw_s
            w_im = v_im * tw_c + v_re * tw_s
            for rb in range(2):
                b_re = u_re + w_re if rb == 0 else u_re - w_re
                b_im = u_im + w_im if rb == 0 else u_im - w_im
                box = (slice(rb * HALF, (rb + 1) * HALF), c0)
                p_re = probes_ref[(number, 0) + box]
                p_im = probes_ref[(number, 1) + box]
                grads = (p_re * b_re + p_im * b_im, p_re * b_im - p_im * b_re)
                for channel in range(2):
                    grad = grads[channel]
                    targets = [(rb * HALF, grad)]
                    if rb == 0:
                        targets = [
                            (0, jnp.where(in_row, grad, 0.0)),
                            (WIN, jnp.where(in_row, 0.0, grad)),
                        ]
                    for at, piece in targets:
                        here = (channel, slice(at, at + HALF), lanes(cb))
                        can[here] = can[here] + jnp.where(in_col, piece, 0.0)
                        here = (channel, slice(at, at + HALF), lanes(cb + 2))
                        can[here] = can[here] + jnp.where(in_col, 0.0, piece)
        return 0

    lax.fori_loop(0, 2, window, 0)

    which = 0
    for first, rows in outs:
        for lo, hi in spans:
            for channel in range(2):
                out_refs[which][channel] = can[channel, first : first + rows, lo:hi]
            which += 1


def windows(i, consts, parts, carried, acc_at, outs):
    offsets, table, twiddle, probes, amps = consts
    plan = tuple(tuple((first, rows) for _, first, rows in part) for part in parts)
    operands = [array for part in parts for array, _, _ in part]
    extra = list(carried) if carried is not None else []
    own = parts[1][0][0].shape[-1]
    assert own == 3 * LANE
    shapes = []
    for _, rows in outs:
        for width in (LANE, own, LANE):
            shapes.append(jax.ShapeDtypeStruct((2, rows, width), F32))
    return pl.pallas_call(
        functools.partial(windows_kernel, i, plan, acc_at, outs),
        out_shape=tuple(shapes),
        in_specs=[pl.BlockSpec(memory_space=pltpu.SMEM)] + vmem(4 + len(operands) + len(extra)),
        out_specs=tuple(vmem(len(shapes))),
        scratch_shapes=[
            pltpu.VMEM((2, own, 5 * LANE), F32),
            pltpu.VMEM((2, own, 5 * LANE), F32),
            pltpu.VMEM((WIN, 2 * WIN), BF16),
            pltpu.VMEM((WIN, 2 * WIN), BF16),
            pltpu.VMEM((2 * WIN, WIN), BF16),
            pltpu.VMEM((2 * WIN, WIN), BF16),
            pltpu.VMEM((WIN, 2 * WIN), F32),
            pltpu.VMEM((2 * WIN, WIN), F32),
        ],
        cost_estimate=pl.CostEstimate(flops=1_600_000_000, bytes_accessed=10_000_000, transcendentals=0),
        name=f"windows_{i}",
    )(offsets, table, twiddle, probes, amps, *operands, *extra)


def totals_kernel(outs, own_ref, left_ref, right_ref, *out_refs):
    for (first, rows), out in zip(outs, out_refs):
        span = slice(first, first + rows)
        for channel in range(2):
            out[channel, :, :LANE] = own_ref[channel, span, :LANE] + left_ref[channel, span, :]
            out[channel, :, LANE : 2 * LANE] = own_ref[channel, span, LANE : 2 * LANE]
            out[channel, :, 2 * LANE :] = own_ref[channel, span, 2 * LANE :] + right_ref[channel, span, :]


def totals(own, from_left, from_right, outs):
    return pl.pallas_call(
        functools.partial(totals_kernel, outs),
        out_shape=tuple(jax.ShapeDtypeStruct((2, rows, own.shape[2]), F32) for _, rows in outs),
        in_specs=vmem(3),
        out_specs=tuple(vmem(len(outs))),
        cost_estimate=pl.CostEstimate(flops=500_000, bytes_accessed=3_000_000, transcendentals=0),
        name="totals",
    )(own, from_left, from_right)


def update_kernel(pieces, guard, *refs):
    new, left, right = refs[-3:]
    ins = refs[:-3]
    row = 0
    for which, first, rows, grads, masked in pieces:
        for channel in range(2):
            total = None
            for grad, at in grads:
                term = ins[grad][channel, at : at + rows, :]
                total = term if total is None else total + term
            value = ins[which][channel, first : first + rows, :] - step_size * total
            if masked:
                value = jnp.where(guard(), value, 0.0)
            new[channel, row : row + rows, :] = value
            left[channel, row : row + rows, :] = value[:, :LANE]
            right[channel, row : row + rows, :] = value[:, 2 * LANE :]
        row += rows


def update(operands, pieces, guard):
    rows = sum(piece[2] for piece in pieces)
    shape = [jax.ShapeDtypeStruct((2, rows, width), F32) for width in (3 * LANE, LANE, LANE)]
    return pl.pallas_call(
        functools.partial(update_kernel, pieces, guard),
        out_shape=tuple(shape),
        in_specs=vmem(len(operands)),
        out_specs=tuple(vmem(3)),
        cost_estimate=pl.CostEstimate(flops=1_000_000, bytes_accessed=4_000_000, transcendentals=0),
        name="update",
    )(*operands)


def finish_kernel(top_ref, bottom_ref, mid_ref, low_ref, above_ref, below_ref, out_ref):
    for channel in range(2):
        above = mid_ref[channel, :MARGIN, :] + above_ref[channel]
        out_ref[channel, :MARGIN, :] = top_ref[channel, MARGIN:, :] - step_size * above
        out_ref[channel, MARGIN:288, :] = bottom_ref[channel, :192, :] - step_size * mid_ref[channel, MARGIN:, :]
        below = low_ref[channel] + below_ref[channel]
        out_ref[channel, 288:, :] = bottom_ref[channel, 192:288, :] - step_size * below


def finish(*operands):
    return pl.pallas_call(
        finish_kernel,
        out_shape=jax.ShapeDtypeStruct((2, 3 * LANE, 3 * LANE), F32),
        in_specs=vmem(len(operands)),
        out_specs=pl.BlockSpec(memory_space=pltpu.VMEM),
        cost_estimate=pl.CostEstimate(flops=1_000_000, bytes_accessed=4_000_000, transcendentals=0),
        name="finish",
    )(*operands)


def moved(block, axis, distance):
    devices = range(lax.axis_size(axis))
    route = [(n, n + distance) for n in devices if n + distance in devices]
    return lax.ppermute(block, axis, route)


def sideways(to_right, to_left):
    return moved(to_right, "col", 1), moved(to_left, "col", -1)


def on_device(table, twiddle, order, object_field, probe, amplitudes, offsets):
    tile = object_field.shape[1]
    last = tile - MARGIN
    band = 2 * MARGIN
    edge = tile - LANE
    obj = object_field

    top = moved(obj[:, last:, :], "row", 1)
    bottom = moved(obj[:, :MARGIN, :], "row", -1)
    left, right = sideways(obj[:, :, edge:], obj[:, :, :LANE])
    probes, amps = prepare(offsets, probe, amplitudes, order)
    consts = (offsets, table, twiddle, probes, amps)

    top_l, top_r = sideways(top[:, :, edge:], top[:, :, :LANE])
    parts = (
        [(top_l, 0, MARGIN), (left, 0, last)],
        [(top, 0, MARGIN), (obj, 0, last)],
        [(top_r, 0, MARGIN), (right, 0, last)],
    )
    lo_l, lo_o, lo_r, mid_l, mid_o, mid_r = windows(0, consts, parts, None, None, ((0, band), (band, band)))
    in_l, in_r = sideways(lo_r, lo_l)
    (top_sum,) = totals(lo_o, in_l, in_r, ((0, band),))
    from_below = moved(top_sum, "row", -1)

    bot_l, bot_r = sideways(bottom[:, :, edge:], bottom[:, :, :LANE])
    parts = (
        [(left, MARGIN, last), (bot_l, 0, MARGIN)],
        [(obj, MARGIN, last), (bottom, 0, MARGIN)],
        [(right, MARGIN, last), (bot_r, 0, MARGIN)],
    )
    hi_l, hi_o, hi_r = windows(1, consts, parts, (mid_l, mid_o, mid_r), 0, ((0, tile),))
    in_l, in_r = sideways(hi_r, hi_l)
    mid_sum, bot_sum = totals(hi_o, in_l, in_r, ((0, band), (band, band)))
    from_above = moved(bot_sum, "row", 1)

    def not_last():
        return lax.axis_index("row") < lax.axis_size("row") - 1

    def not_first():
        return lax.axis_index("row") > 0

    low, low_to_left, low_to_right = update(
        (obj, bottom, mid_sum, bot_sum, from_below),
        (
            (0, MARGIN, band, ((2, 0),), False),
            (0, last, MARGIN, ((3, 0), (4, 0)), False),
            (1, 0, MARGIN, ((3, MARGIN), (4, MARGIN)), True),
        ),
        not_last,
    )
    low_l, low_r = sideways(low_to_right, low_to_left)
    parts = ([(low_l, 0, tile)], [(low, 0, tile)], [(low_r, 0, tile)])
    mid_l, mid_o, mid_r, hi_l, hi_o, hi_r = windows(1, consts, parts, None, None, ((0, band), (band, band)))
    in_l, in_r = sideways(hi_r, hi_l)
    low_sum, over = totals(hi_o, in_l, in_r, ((0, MARGIN), (MARGIN, MARGIN)))
    last_above = moved(over, "row", 1)

    up, up_to_left, up_to_right = update(
        (top, obj, top_sum, from_above),
        (
            (0, 0, MARGIN, ((2, 0), (3, 0)), True),
            (1, 0, MARGIN, ((2, MARGIN), (3, MARGIN)), False),
        ),
        not_first,
    )
    up_l, up_r = sideways(up_to_right, up_to_left)
    parts = (
        [(up_l, 0, band), (low_l, 0, band)],
        [(up, 0, band), (low, 0, band)],
        [(up_r, 0, band), (low_r, 0, band)],
    )
    lo_l, lo_o, lo_r = windows(0, consts, parts, (mid_l, mid_o, mid_r), band, ((0, tile),))
    in_l, in_r = sideways(lo_r, lo_l)
    over, mid_sum = totals(lo_o, in_l, in_r, ((0, MARGIN), (MARGIN, last)))
    last_below = moved(over, "row", -1)
    return finish(up, low, mid_sum, low_sum, last_above, last_below)


def solution(mesh):
    table, twiddle, order = tables()
    body = jax.shard_map(
        on_device,
        mesh=mesh,
        in_specs=(P(), P(), P(), P(None, "row", "col"), P(), P("row", "col"), P("row", "col", None)),
        out_specs=P(None, "row", "col"),
        check_vma=False,
    )

    def step(object_field, probe, amplitudes, offsets):
        return body(table, twiddle, order, object_field, probe, amplitudes, offsets)

    return step
```

```python
import functools
import math

import jax
import jax.numpy as jnp
import numpy as np
from jax import lax
from jax.experimental import pallas as pl
from jax.experimental.pallas import tpu as pltpu
from jax.sharding import PartitionSpec as P

WIN = 256
HALF = 128
MARGIN = 96
LANE = 128
VMEM_LIMIT = 24 * 1024 * 1024

step_size = 0.3
tv_weight = 0.2
tv_smooth = 0.1
amp_floor = 0.5

F32 = jnp.float32
BF16 = jnp.bfloat16


def tables():
    counter = np.arange(HALF)
    angle = (counter[:, None] * counter[None, :] % HALF) * (2.0 * math.pi / HALF)
    cosine = np.cos(angle) / math.sqrt(WIN)
    sine = np.sin(angle) / math.sqrt(WIN)
    first = np.block([[cosine, sine], [-sine, cosine]])
    second = np.block([[cosine, -sine], [sine, cosine]])
    parts = []
    for table in (first, second):
        table = table.astype(np.float32)
        high = table.astype(jnp.bfloat16)
        low = (table - high.astype(np.float32)).astype(jnp.bfloat16)
        parts += [high, low]
    turn = counter * (2.0 * math.pi / WIN)
    rows = np.stack([np.cos(turn), np.sin(turn)])
    by_row = np.broadcast_to(rows[:, :, None], (2, HALF, HALF))
    by_lane = np.broadcast_to(rows[:, None, :], (2, HALF, HALF))
    twiddle = np.concatenate([by_row, by_lane]).astype(np.float32)
    order = np.zeros((WIN, WIN), np.float32)
    for parity in range(2):
        order[2 * counter + parity, parity * HALF + counter] = 1.0
    return np.stack(parts), twiddle, order.astype(jnp.bfloat16)


def split(value):
    high = value.astype(BF16)
    return high, (value - high.astype(F32)).astype(BF16)


def mul(left, right):
    return jnp.dot(left, right, preferred_element_type=F32)


def vmem(count):
    return [pl.BlockSpec(memory_space=pltpu.VMEM)] * count


def prepare_kernel(off_ref, probe_ref, amp_ref, order_ref, probes_ref, amps_ref, parts_ref):
    order = order_ref[...]
    for i in range(2):
        for j in range(2):
            row = off_ref[i, j, 0]
            col = off_ref[i, j, 1] + (32 if j == 0 else 96)
            for channel in range(2):
                turned = pltpu.roll(probe_ref[channel], row, 0)
                probes_ref[2 * i + j, channel] = pltpu.roll(turned, col, 1)
            amp = amp_ref[i * WIN : (i + 1) * WIN, j * WIN : (j + 1) * WIN]
            high, rest = split(amp)
            middle, low = split(amp - high.astype(F32) - rest.astype(F32))
            sorted_lanes = mul(high, order) + mul(rest, order) + mul(middle, order)
            for q in range(2):
                parts_ref[...] = sorted_lanes[:, q * HALF : (q + 1) * HALF]
                for p in range(2):
                    at = q * WIN + p * HALF
                    amps_ref[2 * i + j, at : at + HALF, :] = parts_ref[pl.ds(p, HALF, stride=2), :]


def prepare(offsets, probe, amplitudes, order):
    return pl.pallas_call(
        prepare_kernel,
        out_shape=(
            jax.ShapeDtypeStruct((4, 2, WIN, WIN), F32),
            jax.ShapeDtypeStruct((4, 2 * WIN, HALF), F32),
        ),
        in_specs=[pl.BlockSpec(memory_space=pltpu.SMEM)] + vmem(3),
        out_specs=tuple(vmem(2)),
        scratch_shapes=[pltpu.VMEM((WIN, HALF), F32)],
        cost_estimate=pl.CostEstimate(flops=400_000_000, bytes_accessed=6_000_000, transcendentals=0),
        compiler_params=pltpu.CompilerParams(vmem_limit_bytes=VMEM_LIMIT),
        name="prepare",
    )(offsets, probe, amplitudes, order)


def windows_kernel(i, plan, acc_at, outs, off_ref, tab_ref, tw_ref, probes_ref, amps_ref, *refs):
    operands = sum(len(part) for part in plan)
    ins, refs = refs[:operands], refs[operands:]
    carried = ()
    if acc_at is not None:
        carried, refs = refs[:3], refs[3:]
    out_refs, refs = refs[: 3 * len(outs)], refs[3 * len(outs) :]
    reg, can, gh, gl, hh, hl, wide, tall = refs
    spans = ((0, LANE), (LANE, 4 * LANE), (4 * LANE, 5 * LANE))

    which = 0
    for part, (lo, hi) in zip(plan, spans):
        row = 0
        for first, rows in part:
            for channel in range(2):
                reg[channel, row : row + rows, lo:hi] = ins[which][channel, first : first + rows, :]
            row += rows
            which += 1

    can[...] = jnp.zeros_like(can)
    if acc_at is not None:
        for ref, (lo, hi) in zip(carried, spans):
            for channel in range(2):
                can[channel, acc_at : acc_at + 192, lo:hi] = ref[channel]

    def variation(step, _):
        base = pl.multiple_of(MARGIN - 8 + step * 32, 8)
        flows = []
        power = tv_smooth
        for channel in range(2):
            block = reg[channel, pl.ds(base, 48), :]
            down = pltpu.roll(block, 47, 0) - block
            right = pltpu.roll(block, 5 * LANE - 1, 1) - block
            power = power + down * down + right * right
            flows.append((down, right))
        inverse = lax.rsqrt(power)
        for channel in range(2):
            down, right = flows[channel]
            down = down * inverse
            right = right * inverse
            change = pltpu.roll(down, 1, 0) - down + pltpu.roll(right, 1, 1) - right
            at = pl.multiple_of(base + 8, 8)
            here = (channel, pl.ds(at, 32), slice(LANE, 4 * LANE))
            can[here] = can[here] + tv_weight * change[8:40, LANE : 4 * LANE]
        return 0

    lax.fori_loop(0, 6, variation, 0)

    row_iota = lax.broadcasted_iota(jnp.int32, (HALF, HALF), 0)
    lane_iota = lax.broadcasted_iota(jnp.int32, (HALF, HALF), 1)
    first_h, first_l, second_h, second_l = (tab_ref[n] for n in range(4))

    def store_split(high_ref, low_ref, at, value):
        high, low = split(value)
        high_ref[at] = high
        low_ref[at] = low

    def window(j, _):
        row_start = off_ref[i, j, 0]
        col_start = off_ref[i, j, 1] + 32 + 64 * j
        in_row = row_iota >= row_start

        def lanes(cb):
            return pl.ds(pl.multiple_of((j + cb) * LANE, LANE), LANE)

        number = 2 * i + j
        for cb in range(2):
            in_col = lane_iota + cb * LANE >= col_start
            field = []
            for rb in range(2):
                value = []
                for channel in range(2):
                    near = reg[channel, rb * HALF : (rb + 1) * HALF, lanes(cb)]
                    far = reg[channel, rb * HALF : (rb + 1) * HALF, lanes(cb + 2)]
                    picked = jnp.where(in_col, near, far)
                    if rb == 0:
                        near = reg[channel, WIN : WIN + HALF, lanes(cb)]
                        far = reg[channel, WIN : WIN + HALF, lanes(cb + 2)]
                        picked = jnp.where(in_row, picked, jnp.where(in_col, near, far))
                    value.append(picked)
                box = (slice(rb * HALF, (rb + 1) * HALF), slice(cb * LANE, (cb + 1) * LANE))
                p_re = probes_ref[(number, 0) + box]
                p_im = probes_ref[(number, 1) + box]
                field.append((p_re * value[0] - p_im * value[1], p_re * value[1] + p_im * value[0]))
            (re0, im0), (re1, im1) = field
            even = slice(cb * LANE, (cb + 1) * LANE)
            odd = slice(WIN + cb * LANE, WIN + (cb + 1) * LANE)
            store_split(gh, gl, (slice(0, HALF), even), re0 + re1)
            store_split(gh, gl, (slice(HALF, WIN), even), im0 + im1)
            d_re = re0 - re1
            d_im = im0 - im1
            tw_c, tw_s = tw_ref[0], tw_ref[1]
            store_split(gh, gl, (slice(0, HALF), odd), d_re * tw_c + d_im * tw_s)
            store_split(gh, gl, (slice(HALF, WIN), odd), d_im * tw_c - d_re * tw_s)
        g_h = gh[...]
        wide[...] = mul(first_h, g_h) + mul(first_h, gl[...]) + mul(first_l, g_h)

        tl_c, tl_s = tw_ref[2], tw_ref[3]
        re_l, im_l = slice(0, HALF), slice(HALF, WIN)
        for p in range(2):
            c0 = slice(p * WIN, p * WIN + LANE)
            c1 = slice(p * WIN + LANE, (p + 1) * WIN)
            re0, re1 = wide[:HALF, c0], wide[:HALF, c1]
            im0, im1 = wide[HALF:, c0], wide[HALF:, c1]
            rows = slice(p * HALF, (p + 1) * HALF)
            store_split(hh, hl, (rows, re_l), re0 + re1)
            store_split(hh, hl, (rows, im_l), im0 + im1)
            d_re = re0 - re1
            d_im = im0 - im1
            rows = slice(WIN + p * HALF, WIN + (p + 1) * HALF)
            store_split(hh, hl, (rows, re_l), d_re * tl_c + d_im * tl_s)
            store_split(hh, hl, (rows, im_l), d_im * tl_c - d_re * tl_s)
        h_h = hh[...]
        tall[...] = mul(h_h, second_h) + mul(hl[...], second_h) + mul(h_h, second_l)

        for n in range(4):
            rows = slice(n * HALF, (n + 1) * HALF)
            re, im = tall[rows, re_l], tall[rows, im_l]
            power = jnp.maximum(re * re + im * im, amp_floor * amp_floor)
            keeping = 1.0 - amps_ref[number, rows, :] * lax.rsqrt(power)
            store_split(hh, hl, (rows, re_l), re * keeping)
            store_split(hh, hl, (rows, im_l), im * keeping)
        h_h = hh[...]
        tall[...] = mul(h_h, first_h) + mul(hl[...], first_h) + mul(h_h, first_l)

        for p in range(2):
            rows = slice(p * HALF, (p + 1) * HALF)
            u_re, u_im = tall[rows, re_l], tall[rows, im_l]
            rows = slice(WIN + p * HALF, WIN + (p + 1) * HALF)
            v_re, v_im = tall[rows, re_l], tall[rows, im_l]
            w_re = v_re * tl_c - v_im * tl_s
            w_im = v_im * tl_c + v_re * tl_s
            c0 = slice(p * WIN, p * WIN + LANE)
            c1 = slice(p * WIN + LANE, (p + 1) * WIN)
            store_split(gh, gl, (re_l, c0), u_re + w_re)
            store_split(gh, gl, (re_l, c1), u_re - w_re)
            store_split(gh, gl, (im_l, c0), u_im + w_im)
            store_split(gh, gl, (im_l, c1), u_im - w_im)
        g_h = gh[...]
        wide[...] = mul(second_h, g_h) + mul(second_h, gl[...]) + mul(second_l, g_h)

        tw_c, tw_s = tw_ref[0], tw_ref[1]
        for cb in range(2):
            in_col = lane_iota + cb * LANE >= col_start
            c0 = slice(cb * LANE, (cb + 1) * LANE)
            c1 = slice(WIN + cb * LANE, WIN + (cb + 1) * LANE)
            u_re, u_im = wide[:HALF, c0], wide[HALF:, c0]
            v_re, v_im = wide[:HALF, c1], wide[HALF:, c1]
            w_re = v_re * tw_c - v_im * tw_s
            w_im = v_im * tw_c + v_re * tw_s
            for rb in range(2):
                b_re = u_re + w_re if rb == 0 else u_re - w_re
                b_im = u_im + w_im if rb == 0 else u_im - w_im
                box = (slice(rb * HALF, (rb + 1) * HALF), c0)
                p_re = probes_ref[(number, 0) + box]
                p_im = probes_ref[(number, 1) + box]
                grads = (p_re * b_re + p_im * b_im, p_re * b_im - p_im * b_re)
                for channel in range(2):
                    grad = grads[channel]
                    targets = [(rb * HALF, grad)]
                    if rb == 0:
                        targets = [
                            (0, jnp.where(in_row, grad, 0.0)),
                            (WIN, jnp.where(in_row, 0.0, grad)),
                        ]
                    for at, piece in targets:
                        here = (channel, slice(at, at + HALF), lanes(cb))
                        can[here] = can[here] + jnp.where(in_col, piece, 0.0)
                        here = (channel, slice(at, at + HALF), lanes(cb + 2))
                        can[here] = can[here] + jnp.where(in_col, 0.0, piece)
        return 0

    lax.fori_loop(0, 2, window, 0)

    which = 0
    for first, rows in outs:
        for lo, hi in spans:
            for channel in range(2):
                out_refs[which][channel] = can[channel, first : first + rows, lo:hi]
            which += 1


def windows(i, consts, parts, carried, acc_at, outs):
    offsets, table, twiddle, probes, amps = consts
    plan = tuple(tuple((first, rows) for _, first, rows in part) for part in parts)
    operands = [array for part in parts for array, _, _ in part]
    extra = list(carried) if carried is not None else []
    own = parts[1][0][0].shape[-1]
    assert own == 3 * LANE
    shapes = []
    for _, rows in outs:
        for width in (LANE, own, LANE):
            shapes.append(jax.ShapeDtypeStruct((2, rows, width), F32))
    return pl.pallas_call(
        functools.partial(windows_kernel, i, plan, acc_at, outs),
        out_shape=tuple(shapes),
        in_specs=[pl.BlockSpec(memory_space=pltpu.SMEM)] + vmem(4 + len(operands) + len(extra)),
        out_specs=tuple(vmem(len(shapes))),
        scratch_shapes=[
            pltpu.VMEM((2, own, 5 * LANE), F32),
            pltpu.VMEM((2, own, 5 * LANE), F32),
            pltpu.VMEM((WIN, 2 * WIN), BF16),
            pltpu.VMEM((WIN, 2 * WIN), BF16),
            pltpu.VMEM((2 * WIN, WIN), BF16),
            pltpu.VMEM((2 * WIN, WIN), BF16),
            pltpu.VMEM((WIN, 2 * WIN), F32),
            pltpu.VMEM((2 * WIN, WIN), F32),
        ],
        cost_estimate=pl.CostEstimate(flops=1_600_000_000, bytes_accessed=10_000_000, transcendentals=0),
        compiler_params=pltpu.CompilerParams(vmem_limit_bytes=VMEM_LIMIT),
        name=f"windows_{i}",
    )(offsets, table, twiddle, probes, amps, *operands, *extra)


def totals_kernel(outs, own_ref, left_ref, right_ref, *out_refs):
    for (first, rows), out in zip(outs, out_refs):
        span = slice(first, first + rows)
        for channel in range(2):
            out[channel, :, :LANE] = own_ref[channel, span, :LANE] + left_ref[channel, span, :]
            out[channel, :, LANE : 2 * LANE] = own_ref[channel, span, LANE : 2 * LANE]
            out[channel, :, 2 * LANE :] = own_ref[channel, span, 2 * LANE :] + right_ref[channel, span, :]


def totals(own, from_left, from_right, outs):
    return pl.pallas_call(
        functools.partial(totals_kernel, outs),
        out_shape=tuple(jax.ShapeDtypeStruct((2, rows, own.shape[2]), F32) for _, rows in outs),
        in_specs=vmem(3),
        out_specs=tuple(vmem(len(outs))),
        cost_estimate=pl.CostEstimate(flops=500_000, bytes_accessed=3_000_000, transcendentals=0),
        compiler_params=pltpu.CompilerParams(vmem_limit_bytes=VMEM_LIMIT),
        name="totals",
    )(own, from_left, from_right)


def update_kernel(pieces, guard, *refs):
    new, left, right = refs[-3:]
    ins = refs[:-3]
    row = 0
    for which, first, rows, grads, masked in pieces:
        for channel in range(2):
            total = None
            for grad, at in grads:
                term = ins[grad][channel, at : at + rows, :]
                total = term if total is None else total + term
            value = ins[which][channel, first : first + rows, :] - step_size * total
            if masked:
                value = jnp.where(guard(), value, 0.0)
            new[channel, row : row + rows, :] = value
            left[channel, row : row + rows, :] = value[:, :LANE]
            right[channel, row : row + rows, :] = value[:, 2 * LANE :]
        row += rows


def update(operands, pieces, guard):
    rows = sum(piece[2] for piece in pieces)
    shape = [jax.ShapeDtypeStruct((2, rows, width), F32) for width in (3 * LANE, LANE, LANE)]
    return pl.pallas_call(
        functools.partial(update_kernel, pieces, guard),
        out_shape=tuple(shape),
        in_specs=vmem(len(operands)),
        out_specs=tuple(vmem(3)),
        cost_estimate=pl.CostEstimate(flops=1_000_000, bytes_accessed=4_000_000, transcendentals=0),
        compiler_params=pltpu.CompilerParams(vmem_limit_bytes=VMEM_LIMIT),
        name="update",
    )(*operands)


def finish_kernel(top_ref, bottom_ref, mid_ref, low_ref, above_ref, below_ref, out_ref):
    for channel in range(2):
        above = mid_ref[channel, :MARGIN, :] + above_ref[channel]
        out_ref[channel, :MARGIN, :] = top_ref[channel, MARGIN:, :] - step_size * above
        out_ref[channel, MARGIN:288, :] = bottom_ref[channel, :192, :] - step_size * mid_ref[channel, MARGIN:, :]
        below = low_ref[channel] + below_ref[channel]
        out_ref[channel, 288:, :] = bottom_ref[channel, 192:288, :] - step_size * below


def finish(*operands):
    return pl.pallas_call(
        finish_kernel,
        out_shape=jax.ShapeDtypeStruct((2, 3 * LANE, 3 * LANE), F32),
        in_specs=vmem(len(operands)),
        out_specs=pl.BlockSpec(memory_space=pltpu.VMEM),
        cost_estimate=pl.CostEstimate(flops=1_000_000, bytes_accessed=4_000_000, transcendentals=0),
        compiler_params=pltpu.CompilerParams(vmem_limit_bytes=VMEM_LIMIT),
        name="finish",
    )(*operands)


def moved(block, axis, distance):
    devices = range(lax.axis_size(axis))
    route = [(n, n + distance) for n in devices if n + distance in devices]
    return lax.ppermute(block, axis, route)


def sideways(to_right, to_left):
    return moved(to_right, "col", 1), moved(to_left, "col", -1)


def on_device(table, twiddle, order, object_field, probe, amplitudes, offsets):
    tile = object_field.shape[1]
    last = tile - MARGIN
    band = 2 * MARGIN
    edge = tile - LANE
    obj = object_field

    top = moved(obj[:, last:, :], "row", 1)
    bottom = moved(obj[:, :MARGIN, :], "row", -1)
    left, right = sideways(obj[:, :, edge:], obj[:, :, :LANE])
    probes, amps = prepare(offsets, probe, amplitudes, order)
    consts = (offsets, table, twiddle, probes, amps)

    top_l, top_r = sideways(top[:, :, edge:], top[:, :, :LANE])
    parts = (
        [(top_l, 0, MARGIN), (left, 0, last)],
        [(top, 0, MARGIN), (obj, 0, last)],
        [(top_r, 0, MARGIN), (right, 0, last)],
    )
    lo_l, lo_o, lo_r, mid_l, mid_o, mid_r = windows(0, consts, parts, None, None, ((0, band), (band, band)))
    in_l, in_r = sideways(lo_r, lo_l)
    (top_sum,) = totals(lo_o, in_l, in_r, ((0, band),))
    from_below = moved(top_sum, "row", -1)

    bot_l, bot_r = sideways(bottom[:, :, edge:], bottom[:, :, :LANE])
    parts = (
        [(left, MARGIN, last), (bot_l, 0, MARGIN)],
        [(obj, MARGIN, last), (bottom, 0, MARGIN)],
        [(right, MARGIN, last), (bot_r, 0, MARGIN)],
    )
    hi_l, hi_o, hi_r = windows(1, consts, parts, (mid_l, mid_o, mid_r), 0, ((0, tile),))
    in_l, in_r = sideways(hi_r, hi_l)
    mid_sum, bot_sum = totals(hi_o, in_l, in_r, ((0, band), (band, band)))
    from_above = moved(bot_sum, "row", 1)

    def not_last():
        return lax.axis_index("row") < lax.axis_size("row") - 1

    def not_first():
        return lax.axis_index("row") > 0

    low, low_to_left, low_to_right = update(
        (obj, bottom, mid_sum, bot_sum, from_below),
        (
            (0, MARGIN, band, ((2, 0),), False),
            (0, last, MARGIN, ((3, 0), (4, 0)), False),
            (1, 0, MARGIN, ((3, MARGIN), (4, MARGIN)), True),
        ),
        not_last,
    )
    low_l, low_r = sideways(low_to_right, low_to_left)
    parts = ([(low_l, 0, tile)], [(low, 0, tile)], [(low_r, 0, tile)])
    mid_l, mid_o, mid_r, hi_l, hi_o, hi_r = windows(1, consts, parts, None, None, ((0, band), (band, band)))
    in_l, in_r = sideways(hi_r, hi_l)
    low_sum, over = totals(hi_o, in_l, in_r, ((0, MARGIN), (MARGIN, MARGIN)))
    last_above = moved(over, "row", 1)

    up, up_to_left, up_to_right = update(
        (top, obj, top_sum, from_above),
        (
            (0, 0, MARGIN, ((2, 0), (3, 0)), True),
            (1, 0, MARGIN, ((2, MARGIN), (3, MARGIN)), False),
        ),
        not_first,
    )
    up_l, up_r = sideways(up_to_right, up_to_left)
    parts = (
        [(up_l, 0, band), (low_l, 0, band)],
        [(up, 0, band), (low, 0, band)],
        [(up_r, 0, band), (low_r, 0, band)],
    )
    lo_l, lo_o, lo_r = windows(0, consts, parts, (mid_l, mid_o, mid_r), band, ((0, tile),))
    in_l, in_r = sideways(lo_r, lo_l)
    over, mid_sum = totals(lo_o, in_l, in_r, ((0, MARGIN), (MARGIN, last)))
    last_below = moved(over, "row", -1)
    return finish(up, low, mid_sum, low_sum, last_above, last_below)


def solution(mesh):
    table, twiddle, order = tables()
    body = jax.shard_map(
        on_device,
        mesh=mesh,
        in_specs=(P(), P(), P(), P(None, "row", "col"), P(), P("row", "col"), P("row", "col", None)),
        out_specs=P(None, "row", "col"),
        check_vma=False,
    )

    def step(object_field, probe, amplitudes, offsets):
        return body(table, twiddle, order, object_field, probe, amplitudes, offsets)

    return step
```

```python
import functools
import math

import jax
import jax.numpy as jnp
import numpy as np
from jax import lax
from jax.experimental import pallas as pl
from jax.experimental.pallas import tpu as pltpu
from jax.sharding import PartitionSpec as P

WIN = 256
HALF = 128
MARGIN = 96
LANE = 128
VMEM_LIMIT = 24 * 1024 * 1024

step_size = 0.3
tv_weight = 0.2
tv_smooth = 0.1
amp_floor = 0.5

F32 = jnp.float32
BF16 = jnp.bfloat16


def tables():
    counter = np.arange(HALF)
    angle = (counter[:, None] * counter[None, :] % HALF) * (2.0 * math.pi / HALF)
    cosine = np.cos(angle) / math.sqrt(WIN)
    sine = np.sin(angle) / math.sqrt(WIN)
    first = np.block([[cosine, sine], [-sine, cosine]])
    second = np.block([[cosine, -sine], [sine, cosine]])
    parts = []
    for table in (first, second):
        table = table.astype(np.float32)
        high = table.astype(jnp.bfloat16)
        low = (table - high.astype(np.float32)).astype(jnp.bfloat16)
        parts += [high, low]
    turn = counter * (2.0 * math.pi / WIN)
    rows = np.stack([np.cos(turn), np.sin(turn)])
    by_row = np.broadcast_to(rows[:, :, None], (2, HALF, HALF))
    by_lane = np.broadcast_to(rows[:, None, :], (2, HALF, HALF))
    twiddle = np.concatenate([by_row, by_lane]).astype(np.float32)
    order = np.zeros((WIN, WIN), np.float32)
    for parity in range(2):
        order[2 * counter + parity, parity * HALF + counter] = 1.0
    return np.stack(parts), twiddle, order.astype(jnp.bfloat16)


def split(value):
    high = value.astype(BF16)
    return high, (value - high.astype(F32)).astype(BF16)


def has(side):
    if side == "above":
        return lax.axis_index("row") > 0
    if side == "below":
        return lax.axis_index("row") < lax.axis_size("row") - 1
    if side == "left":
        return lax.axis_index("col") > 0
    return lax.axis_index("col") < lax.axis_size("col") - 1


def kept(value, *sides):
    for side in sides:
        value = jnp.where(has(side), value, 0.0)
    return value


def mul(left, right):
    return jnp.dot(left, right, preferred_element_type=F32)


def vmem(count):
    return [pl.BlockSpec(memory_space=pltpu.VMEM)] * count


def prepare_kernel(off_ref, probe_ref, amp_ref, order_ref, probes_ref, amps_ref, parts_ref):
    order = order_ref[...]
    for i in range(2):
        for j in range(2):
            row = off_ref[i, j, 0]
            col = off_ref[i, j, 1] + (32 if j == 0 else 96)
            for channel in range(2):
                turned = pltpu.roll(probe_ref[channel], row, 0)
                probes_ref[2 * i + j, channel] = pltpu.roll(turned, col, 1)
            amp = amp_ref[i * WIN : (i + 1) * WIN, j * WIN : (j + 1) * WIN]
            high, rest = split(amp)
            middle, low = split(amp - high.astype(F32) - rest.astype(F32))
            sorted_lanes = mul(high, order) + mul(rest, order) + mul(middle, order)
            for q in range(2):
                parts_ref[...] = sorted_lanes[:, q * HALF : (q + 1) * HALF]
                for p in range(2):
                    at = q * WIN + p * HALF
                    amps_ref[2 * i + j, at : at + HALF, :] = parts_ref[pl.ds(p, HALF, stride=2), :]


def prepare(offsets, probe, amplitudes, order):
    return pl.pallas_call(
        prepare_kernel,
        out_shape=(
            jax.ShapeDtypeStruct((4, 2, WIN, WIN), F32),
            jax.ShapeDtypeStruct((4, 2 * WIN, HALF), F32),
        ),
        in_specs=[pl.BlockSpec(memory_space=pltpu.SMEM)] + vmem(3),
        out_specs=tuple(vmem(2)),
        scratch_shapes=[pltpu.VMEM((WIN, HALF), F32)],
        cost_estimate=pl.CostEstimate(flops=400_000_000, bytes_accessed=6_000_000, transcendentals=0),
        compiler_params=pltpu.CompilerParams(vmem_limit_bytes=VMEM_LIMIT),
        name="prepare",
    )(offsets, probe, amplitudes, order)


def windows_kernel(i, plan, acc_at, outs, off_ref, tab_ref, tw_ref, probes_ref, amps_ref, *refs):
    operands = sum(len(part) for part in plan)
    ins, refs = refs[:operands], refs[operands:]
    carried = ()
    if acc_at is not None:
        carried, refs = refs[:3], refs[3:]
    out_refs, refs = refs[: 3 * len(outs)], refs[3 * len(outs) :]
    reg, can, gh, gl, hh, hl, wide, tall = refs
    spans = ((0, LANE), (LANE, 4 * LANE), (4 * LANE, 5 * LANE))

    which = 0
    for part, (lo, hi) in zip(plan, spans):
        row = 0
        for first, rows, sides in part:
            for channel in range(2):
                reg[channel, row : row + rows, lo:hi] = kept(ins[which][channel, first : first + rows, :], *sides)
            row += rows
            which += 1

    can[...] = jnp.zeros_like(can)
    if acc_at is not None:
        for ref, (lo, hi) in zip(carried, spans):
            for channel in range(2):
                can[channel, acc_at : acc_at + 192, lo:hi] = ref[channel]

    def variation(step, _):
        base = pl.multiple_of(MARGIN - 8 + step * 32, 8)
        flows = []
        power = tv_smooth
        for channel in range(2):
            block = reg[channel, pl.ds(base, 48), :]
            down = pltpu.roll(block, 47, 0) - block
            right = pltpu.roll(block, 5 * LANE - 1, 1) - block
            power = power + down * down + right * right
            flows.append((down, right))
        inverse = lax.rsqrt(power)
        for channel in range(2):
            down, right = flows[channel]
            down = down * inverse
            right = right * inverse
            change = pltpu.roll(down, 1, 0) - down + pltpu.roll(right, 1, 1) - right
            at = pl.multiple_of(base + 8, 8)
            here = (channel, pl.ds(at, 32), slice(LANE, 4 * LANE))
            can[here] = can[here] + tv_weight * change[8:40, LANE : 4 * LANE]
        return 0

    lax.fori_loop(0, 6, variation, 0)

    row_iota = lax.broadcasted_iota(jnp.int32, (HALF, HALF), 0)
    lane_iota = lax.broadcasted_iota(jnp.int32, (HALF, HALF), 1)
    first_h, first_l, second_h, second_l = (tab_ref[n] for n in range(4))

    def store_split(high_ref, low_ref, at, value):
        high, low = split(value)
        high_ref[at] = high
        low_ref[at] = low

    def window(j, _):
        row_start = off_ref[i, j, 0]
        col_start = off_ref[i, j, 1] + 32 + 64 * j
        in_row = row_iota >= row_start

        def lanes(cb):
            return pl.ds(pl.multiple_of((j + cb) * LANE, LANE), LANE)

        number = 2 * i + j
        for cb in range(2):
            in_col = lane_iota + cb * LANE >= col_start
            field = []
            for rb in range(2):
                value = []
                for channel in range(2):
                    near = reg[channel, rb * HALF : (rb + 1) * HALF, lanes(cb)]
                    far = reg[channel, rb * HALF : (rb + 1) * HALF, lanes(cb + 2)]
                    picked = jnp.where(in_col, near, far)
                    if rb == 0:
                        near = reg[channel, WIN : WIN + HALF, lanes(cb)]
                        far = reg[channel, WIN : WIN + HALF, lanes(cb + 2)]
                        picked = jnp.where(in_row, picked, jnp.where(in_col, near, far))
                    value.append(picked)
                box = (slice(rb * HALF, (rb + 1) * HALF), slice(cb * LANE, (cb + 1) * LANE))
                p_re = probes_ref[(number, 0) + box]
                p_im = probes_ref[(number, 1) + box]
                field.append((p_re * value[0] - p_im * value[1], p_re * value[1] + p_im * value[0]))
            (re0, im0), (re1, im1) = field
            even = slice(cb * LANE, (cb + 1) * LANE)
            odd = slice(WIN + cb * LANE, WIN + (cb + 1) * LANE)
            store_split(gh, gl, (slice(0, HALF), even), re0 + re1)
            store_split(gh, gl, (slice(HALF, WIN), even), im0 + im1)
            d_re = re0 - re1
            d_im = im0 - im1
            tw_c, tw_s = tw_ref[0], tw_ref[1]
            store_split(gh, gl, (slice(0, HALF), odd), d_re * tw_c + d_im * tw_s)
            store_split(gh, gl, (slice(HALF, WIN), odd), d_im * tw_c - d_re * tw_s)
        g_h = gh[...]
        wide[...] = mul(first_h, g_h) + mul(first_h, gl[...]) + mul(first_l, g_h)

        tl_c, tl_s = tw_ref[2], tw_ref[3]
        re_l, im_l = slice(0, HALF), slice(HALF, WIN)
        for p in range(2):
            c0 = slice(p * WIN, p * WIN + LANE)
            c1 = slice(p * WIN + LANE, (p + 1) * WIN)
            re0, re1 = wide[:HALF, c0], wide[:HALF, c1]
            im0, im1 = wide[HALF:, c0], wide[HALF:, c1]
            rows = slice(p * HALF, (p + 1) * HALF)
            store_split(hh, hl, (rows, re_l), re0 + re1)
            store_split(hh, hl, (rows, im_l), im0 + im1)
            d_re = re0 - re1
            d_im = im0 - im1
            rows = slice(WIN + p * HALF, WIN + (p + 1) * HALF)
            store_split(hh, hl, (rows, re_l), d_re * tl_c + d_im * tl_s)
            store_split(hh, hl, (rows, im_l), d_im * tl_c - d_re * tl_s)
        h_h = hh[...]
        tall[...] = mul(h_h, second_h) + mul(hl[...], second_h) + mul(h_h, second_l)

        for n in range(4):
            rows = slice(n * HALF, (n + 1) * HALF)
            re, im = tall[rows, re_l], tall[rows, im_l]
            power = jnp.maximum(re * re + im * im, amp_floor * amp_floor)
            keeping = 1.0 - amps_ref[number, rows, :] * lax.rsqrt(power)
            store_split(hh, hl, (rows, re_l), re * keeping)
            store_split(hh, hl, (rows, im_l), im * keeping)
        h_h = hh[...]
        tall[...] = mul(h_h, first_h) + mul(hl[...], first_h) + mul(h_h, first_l)

        for p in range(2):
            rows = slice(p * HALF, (p + 1) * HALF)
            u_re, u_im = tall[rows, re_l], tall[rows, im_l]
            rows = slice(WIN + p * HALF, WIN + (p + 1) * HALF)
            v_re, v_im = tall[rows, re_l], tall[rows, im_l]
            w_re = v_re * tl_c - v_im * tl_s
            w_im = v_im * tl_c + v_re * tl_s
            c0 = slice(p * WIN, p * WIN + LANE)
            c1 = slice(p * WIN + LANE, (p + 1) * WIN)
            store_split(gh, gl, (re_l, c0), u_re + w_re)
            store_split(gh, gl, (re_l, c1), u_re - w_re)
            store_split(gh, gl, (im_l, c0), u_im + w_im)
            store_split(gh, gl, (im_l, c1), u_im - w_im)
        g_h = gh[...]
        wide[...] = mul(second_h, g_h) + mul(second_h, gl[...]) + mul(second_l, g_h)

        tw_c, tw_s = tw_ref[0], tw_ref[1]
        for cb in range(2):
            in_col = lane_iota + cb * LANE >= col_start
            c0 = slice(cb * LANE, (cb + 1) * LANE)
            c1 = slice(WIN + cb * LANE, WIN + (cb + 1) * LANE)
            u_re, u_im = wide[:HALF, c0], wide[HALF:, c0]
            v_re, v_im = wide[:HALF, c1], wide[HALF:, c1]
            w_re = v_re * tw_c - v_im * tw_s
            w_im = v_im * tw_c + v_re * tw_s
            for rb in range(2):
                b_re = u_re + w_re if rb == 0 else u_re - w_re
                b_im = u_im + w_im if rb == 0 else u_im - w_im
                box = (slice(rb * HALF, (rb + 1) * HALF), c0)
                p_re = probes_ref[(number, 0) + box]
                p_im = probes_ref[(number, 1) + box]
                grads = (p_re * b_re + p_im * b_im, p_re * b_im - p_im * b_re)
                for channel in range(2):
                    grad = grads[channel]
                    targets = [(rb * HALF, grad)]
                    if rb == 0:
                        targets = [
                            (0, jnp.where(in_row, grad, 0.0)),
                            (WIN, jnp.where(in_row, 0.0, grad)),
                        ]
                    for at, piece in targets:
                        here = (channel, slice(at, at + HALF), lanes(cb))
                        can[here] = can[here] + jnp.where(in_col, piece, 0.0)
                        here = (channel, slice(at, at + HALF), lanes(cb + 2))
                        can[here] = can[here] + jnp.where(in_col, 0.0, piece)
        return 0

    lax.fori_loop(0, 2, window, 0)

    which = 0
    for first, rows in outs:
        for lo, hi in spans:
            for channel in range(2):
                out_refs[which][channel] = can[channel, first : first + rows, lo:hi]
            which += 1


def windows(i, consts, parts, carried, acc_at, outs):
    offsets, table, twiddle, probes, amps = consts
    plan = tuple(
        tuple((piece[1], piece[2], piece[3:] + side) for piece in part)
        for part, side in zip(parts, (("left",), (), ("right",)))
    )
    operands = [piece[0] for part in parts for piece in part]
    extra = list(carried) if carried is not None else []
    own = parts[1][0][0].shape[-1]
    assert own == 3 * LANE
    shapes = []
    for _, rows in outs:
        for width in (LANE, own, LANE):
            shapes.append(jax.ShapeDtypeStruct((2, rows, width), F32))
    return pl.pallas_call(
        functools.partial(windows_kernel, i, plan, acc_at, outs),
        out_shape=tuple(shapes),
        in_specs=[pl.BlockSpec(memory_space=pltpu.SMEM)] + vmem(4 + len(operands) + len(extra)),
        out_specs=tuple(vmem(len(shapes))),
        scratch_shapes=[
            pltpu.VMEM((2, own, 5 * LANE), F32),
            pltpu.VMEM((2, own, 5 * LANE), F32),
            pltpu.VMEM((WIN, 2 * WIN), BF16),
            pltpu.VMEM((WIN, 2 * WIN), BF16),
            pltpu.VMEM((2 * WIN, WIN), BF16),
            pltpu.VMEM((2 * WIN, WIN), BF16),
            pltpu.VMEM((WIN, 2 * WIN), F32),
            pltpu.VMEM((2 * WIN, WIN), F32),
        ],
        cost_estimate=pl.CostEstimate(flops=1_600_000_000, bytes_accessed=10_000_000, transcendentals=0),
        compiler_params=pltpu.CompilerParams(vmem_limit_bytes=VMEM_LIMIT),
        name=f"windows_{i}",
    )(offsets, table, twiddle, probes, amps, *operands, *extra)


def totals_kernel(outs, own_ref, left_ref, right_ref, *out_refs):
    for (first, rows), out in zip(outs, out_refs):
        span = slice(first, first + rows)
        for channel in range(2):
            out[channel, :, :LANE] = own_ref[channel, span, :LANE] + kept(left_ref[channel, span, :], "left")
            out[channel, :, LANE : 2 * LANE] = own_ref[channel, span, LANE : 2 * LANE]
            out[channel, :, 2 * LANE :] = own_ref[channel, span, 2 * LANE :] + kept(right_ref[channel, span, :], "right")


def totals(own, from_left, from_right, outs):
    return pl.pallas_call(
        functools.partial(totals_kernel, outs),
        out_shape=tuple(jax.ShapeDtypeStruct((2, rows, own.shape[2]), F32) for _, rows in outs),
        in_specs=vmem(3),
        out_specs=tuple(vmem(len(outs))),
        cost_estimate=pl.CostEstimate(flops=500_000, bytes_accessed=3_000_000, transcendentals=0),
        compiler_params=pltpu.CompilerParams(vmem_limit_bytes=VMEM_LIMIT),
        name="totals",
    )(own, from_left, from_right)


def update_kernel(pieces, side, *refs):
    new, left, right = refs[-3:]
    ins = refs[:-3]
    row = 0
    for which, first, rows, grads, masked in pieces:
        for channel in range(2):
            total = None
            for grad, at in grads:
                term = ins[grad][channel, at : at + rows, :]
                if grad == len(ins) - 1:
                    term = kept(term, side)
                total = term if total is None else total + term
            value = ins[which][channel, first : first + rows, :] - step_size * total
            if masked:
                value = kept(value, side)
            new[channel, row : row + rows, :] = value
            left[channel, row : row + rows, :] = value[:, :LANE]
            right[channel, row : row + rows, :] = value[:, 2 * LANE :]
        row += rows


def update(operands, pieces, side):
    rows = sum(piece[2] for piece in pieces)
    shape = [jax.ShapeDtypeStruct((2, rows, width), F32) for width in (3 * LANE, LANE, LANE)]
    return pl.pallas_call(
        functools.partial(update_kernel, pieces, side),
        out_shape=tuple(shape),
        in_specs=vmem(len(operands)),
        out_specs=tuple(vmem(3)),
        cost_estimate=pl.CostEstimate(flops=1_000_000, bytes_accessed=4_000_000, transcendentals=0),
        compiler_params=pltpu.CompilerParams(vmem_limit_bytes=VMEM_LIMIT),
        name="update",
    )(*operands)


def finish_kernel(top_ref, bottom_ref, mid_ref, low_ref, above_ref, below_ref, out_ref):
    for channel in range(2):
        above = mid_ref[channel, :MARGIN, :] + kept(above_ref[channel], "above")
        out_ref[channel, :MARGIN, :] = top_ref[channel, MARGIN:, :] - step_size * above
        out_ref[channel, MARGIN:288, :] = bottom_ref[channel, :192, :] - step_size * mid_ref[channel, MARGIN:, :]
        below = low_ref[channel] + kept(below_ref[channel], "below")
        out_ref[channel, 288:, :] = bottom_ref[channel, 192:288, :] - step_size * below


def finish(*operands):
    return pl.pallas_call(
        finish_kernel,
        out_shape=jax.ShapeDtypeStruct((2, 3 * LANE, 3 * LANE), F32),
        in_specs=vmem(len(operands)),
        out_specs=pl.BlockSpec(memory_space=pltpu.VMEM),
        cost_estimate=pl.CostEstimate(flops=1_000_000, bytes_accessed=4_000_000, transcendentals=0),
        compiler_params=pltpu.CompilerParams(vmem_limit_bytes=VMEM_LIMIT),
        name="finish",
    )(*operands)


def moved(block, axis, distance):
    count = lax.axis_size(axis)
    return lax.ppermute(block, axis, [(n, (n + distance) % count) for n in range(count)])


def sideways(to_right, to_left):
    return moved(to_right, "col", 1), moved(to_left, "col", -1)


def on_device(table, twiddle, order, object_field, probe, amplitudes, offsets):
    tile = object_field.shape[1]
    last = tile - MARGIN
    band = 2 * MARGIN
    edge = tile - LANE
    obj = object_field

    top = moved(obj[:, last:, :], "row", 1)
    bottom = moved(obj[:, :MARGIN, :], "row", -1)
    left, right = sideways(obj[:, :, edge:], obj[:, :, :LANE])
    probes, amps = prepare(offsets, probe, amplitudes, order)
    consts = (offsets, table, twiddle, probes, amps)

    top_l, top_r = sideways(top[:, :, edge:], top[:, :, :LANE])
    parts = (
        [(top_l, 0, MARGIN, "above"), (left, 0, last)],
        [(top, 0, MARGIN, "above"), (obj, 0, last)],
        [(top_r, 0, MARGIN, "above"), (right, 0, last)],
    )
    lo_l, lo_o, lo_r, mid_l, mid_o, mid_r = windows(0, consts, parts, None, None, ((0, band), (band, band)))
    bottom, lo_l = lax.optimization_barrier((bottom, lo_l))
    in_l, in_r = sideways(lo_r, lo_l)
    (top_sum,) = totals(lo_o, in_l, in_r, ((0, band),))
    from_below = moved(top_sum, "row", -1)

    mid_o, top_sum = lax.optimization_barrier((mid_o, top_sum))
    bot_l, bot_r = sideways(bottom[:, :, edge:], bottom[:, :, :LANE])
    parts = (
        [(left, MARGIN, last), (bot_l, 0, MARGIN, "below")],
        [(obj, MARGIN, last), (bottom, 0, MARGIN, "below")],
        [(right, MARGIN, last), (bot_r, 0, MARGIN, "below")],
    )
    hi_l, hi_o, hi_r = windows(1, consts, parts, (mid_l, mid_o, mid_r), 0, ((0, tile),))
    in_l, in_r = sideways(hi_r, hi_l)
    mid_sum, bot_sum = totals(hi_o, in_l, in_r, ((0, band), (band, band)))
    from_above = moved(bot_sum, "row", 1)

    low, low_to_left, low_to_right = update(
        (obj, bottom, mid_sum, bot_sum, from_below),
        (
            (0, MARGIN, band, ((2, 0),), False),
            (0, last, MARGIN, ((3, 0), (4, 0)), False),
            (1, 0, MARGIN, ((3, MARGIN), (4, MARGIN)), True),
        ),
        "below",
    )
    low_l, low_r = sideways(low_to_right, low_to_left)
    parts = ([(low_l, 0, tile)], [(low, 0, tile)], [(low_r, 0, tile)])
    mid_l, mid_o, mid_r, hi_l, hi_o, hi_r = windows(1, consts, parts, None, None, ((0, band), (band, band)))
    in_l, in_r = sideways(hi_r, hi_l)
    low_sum, over = totals(hi_o, in_l, in_r, ((0, MARGIN), (MARGIN, MARGIN)))
    last_above = moved(over, "row", 1)

    up, up_to_left, up_to_right = update(
        (top, obj, top_sum, from_above),
        (
            (0, 0, MARGIN, ((2, 0), (3, 0)), True),
            (1, 0, MARGIN, ((2, MARGIN), (3, MARGIN)), False),
        ),
        "above",
    )
    up_l, up_r = sideways(up_to_right, up_to_left)
    parts = (
        [(up_l, 0, band), (low_l, 0, band)],
        [(up, 0, band), (low, 0, band)],
        [(up_r, 0, band), (low_r, 0, band)],
    )
    mid_o, over = lax.optimization_barrier((mid_o, over))
    lo_l, lo_o, lo_r = windows(0, consts, parts, (mid_l, mid_o, mid_r), band, ((0, tile),))
    in_l, in_r = sideways(lo_r, lo_l)
    over, mid_sum = totals(lo_o, in_l, in_r, ((0, MARGIN), (MARGIN, last)))
    last_below = moved(over, "row", -1)
    return finish(up, low, mid_sum, low_sum, last_above, last_below)


def solution(mesh):
    table, twiddle, order = tables()
    body = jax.shard_map(
        on_device,
        mesh=mesh,
        in_specs=(P(), P(), P(), P(None, "row", "col"), P(), P("row", "col"), P("row", "col", None)),
        out_specs=P(None, "row", "col"),
        check_vma=False,
    )

    def step(object_field, probe, amplitudes, offsets):
        return body(table, twiddle, order, object_field, probe, amplitudes, offsets)

    return step
```

```python
import functools
import math

import jax
import jax.numpy as jnp
import numpy as np
from jax import lax
from jax.experimental import pallas as pl
from jax.experimental.pallas import tpu as pltpu
from jax.sharding import PartitionSpec as P

WIN = 256
HALF = 128
MARGIN = 96
LANE = 128
VMEM_LIMIT = 24 * 1024 * 1024

step_size = 0.3
tv_weight = 0.2
tv_smooth = 0.1
amp_floor = 0.5

F32 = jnp.float32
BF16 = jnp.bfloat16


def tables():
    counter = np.arange(HALF)
    angle = (counter[:, None] * counter[None, :] % HALF) * (2.0 * math.pi / HALF)
    cosine = np.cos(angle) / math.sqrt(WIN)
    sine = np.sin(angle) / math.sqrt(WIN)
    first = np.block([[cosine, sine], [-sine, cosine]])
    second = np.block([[cosine, -sine], [sine, cosine]])
    parts = []
    for table in (first, second):
        table = table.astype(np.float32)
        high = table.astype(jnp.bfloat16)
        low = (table - high.astype(np.float32)).astype(jnp.bfloat16)
        parts += [high, low]
    turn = counter * (2.0 * math.pi / WIN)
    rows = np.stack([np.cos(turn), np.sin(turn)])
    by_row = np.broadcast_to(rows[:, :, None], (2, HALF, HALF))
    by_lane = np.broadcast_to(rows[:, None, :], (2, HALF, HALF))
    twiddle = np.concatenate([by_row, by_lane]).astype(np.float32)
    order = np.zeros((WIN, WIN), np.float32)
    for parity in range(2):
        order[2 * counter + parity, parity * HALF + counter] = 1.0
    return np.stack(parts), twiddle, order.astype(jnp.bfloat16)


def split(value):
    high = value.astype(BF16)
    return high, (value - high.astype(F32)).astype(BF16)


def has(side):
    if side == "above":
        return lax.axis_index("row") > 0
    if side == "below":
        return lax.axis_index("row") < lax.axis_size("row") - 1
    if side == "left":
        return lax.axis_index("col") > 0
    return lax.axis_index("col") < lax.axis_size("col") - 1


def kept(value, *sides):
    for side in sides:
        value = jnp.where(has(side), value, 0.0)
    return value


def mul(left, right):
    return jnp.dot(left, right, preferred_element_type=F32)


def vmem(count):
    return [pl.BlockSpec(memory_space=pltpu.VMEM)] * count


def prepare_kernel(off_ref, probe_ref, amp_ref, order_ref, probes_ref, amps_ref, parts_ref):
    order = order_ref[...]
    for i in range(2):
        for j in range(2):
            row = off_ref[i, j, 0]
            col = off_ref[i, j, 1] + (32 if j == 0 else 96)
            for channel in range(2):
                turned = pltpu.roll(probe_ref[channel], row, 0)
                probes_ref[2 * i + j, channel] = pltpu.roll(turned, col, 1)
            amp = amp_ref[i * WIN : (i + 1) * WIN, j * WIN : (j + 1) * WIN]
            high, rest = split(amp)
            middle, low = split(amp - high.astype(F32) - rest.astype(F32))
            sorted_lanes = mul(high, order) + mul(rest, order) + mul(middle, order)
            for q in range(2):
                parts_ref[...] = sorted_lanes[:, q * HALF : (q + 1) * HALF]
                for p in range(2):
                    at = q * WIN + p * HALF
                    amps_ref[2 * i + j, at : at + HALF, :] = parts_ref[pl.ds(p, HALF, stride=2), :]


def prepare(offsets, probe, amplitudes, order):
    return pl.pallas_call(
        prepare_kernel,
        out_shape=(
            jax.ShapeDtypeStruct((4, 2, WIN, WIN), F32),
            jax.ShapeDtypeStruct((4, 2 * WIN, HALF), F32),
        ),
        in_specs=[pl.BlockSpec(memory_space=pltpu.SMEM)] + vmem(3),
        out_specs=tuple(vmem(2)),
        scratch_shapes=[pltpu.VMEM((WIN, HALF), F32)],
        cost_estimate=pl.CostEstimate(flops=400_000_000, bytes_accessed=6_000_000, transcendentals=0),
        compiler_params=pltpu.CompilerParams(vmem_limit_bytes=VMEM_LIMIT),
        name="prepare",
    )(offsets, probe, amplitudes, order)


def rows_of(pieces, refs, first, rows):
    found, at = [], 0
    for ref, (start, count, sides) in zip(refs, pieces):
        lo, hi = max(first, at), min(first + rows, at + count)
        if lo < hi:
            found.append((ref, start + lo - at, hi - lo, sides))
        at += count
    return found


def window_kernel(i, j, side, own, carried_own, carried_side, outs, *refs):
    off_ref, tab_ref, tw_ref, probes_ref, amps_ref = refs[:5]
    refs = refs[5:]
    side_refs, refs = refs[: len(side)], refs[len(side) :]
    own_refs, refs = refs[: len(own)], refs[len(own) :]
    sum_refs, refs = refs[: len(carried_own)], refs[len(carried_own) :]
    strip_refs, refs = refs[: len(carried_side)], refs[len(carried_side) :]
    out_refs, refs = refs[: 2 * len(outs)], refs[2 * len(outs) :]
    halves = [refs[n : n + 2] for n in range(0, 16, 2)]
    g_in, h_in, m_in, g_out = halves[0:2], halves[2:4], halves[4:6], halves[6:8]
    wide, tall, tall_back, wide_back = refs[16:18], refs[18:20], refs[20:22], refs[22:24]

    number = 2 * i + j
    row_start = off_ref[i, j, 0]
    col_start = off_ref[i, j, 1] + 32 + 64 * j
    row_iota = lax.broadcasted_iota(jnp.int32, (HALF, HALF), 0)
    lane_iota = lax.broadcasted_iota(jnp.int32, (HALF, HALF), 1)
    in_row = row_iota >= row_start
    first_h, first_l, second_h, second_l = (tab_ref.at[n] for n in range(4))
    strip_at = 0 if j == 0 else 3

    def place(group):
        if group == strip_at:
            return True, slice(0, LANE)
        at = (group - (1 if j == 0 else 0)) * LANE
        return False, slice(at, at + LANE)

    def load(channel, first, group):
        is_strip, lanes = place(group)
        pieces, sources = (side, side_refs) if is_strip else (own, own_refs)
        blocks = [
            kept(ref[channel, at : at + rows, lanes], *sides)
            for ref, at, rows, sides in rows_of(pieces, sources, first, HALF)
        ]
        return blocks[0] if len(blocks) == 1 else jnp.concatenate(blocks, axis=0)

    def emit(channel, first, group, value):
        is_strip, lanes = place(group)
        extra = (carried_side, strip_refs) if is_strip else (carried_own, sum_refs)
        which = 1 if is_strip else 0
        for n, (start, count) in enumerate(outs):
            lo, hi = max(first, start), min(first + HALF, start + count)
            if lo >= hi:
                continue
            cuts = sorted({lo, hi} | {c for at, rows in extra[0] for c in (at, at + rows) if lo < c < hi})
            for a, b in zip(cuts, cuts[1:]):
                part = value[a - first : b - first]
                for (at, rows), ref in zip(*extra):
                    if at <= a and b <= at + rows:
                        part = part + ref[channel, a - at : b - at, lanes]
                out_refs[2 * n + which][channel, a - start : b - start, lanes] = part

    def store_split(pair, rows, lanes, value):
        high, low = split(value)
        pair[0][rows, lanes] = high
        pair[1][rows, lanes] = low

    lo, hi = slice(0, HALF), slice(HALF, WIN)
    tw_c, tw_s = tw_ref[0], tw_ref[1]
    for cb in range(2):
        in_col = lane_iota + cb * LANE >= col_start
        field = []
        for rb in range(2):
            value = []
            for channel in range(2):
                picked = jnp.where(in_col, load(channel, rb * HALF, cb), load(channel, rb * HALF, cb + 2))
                if rb == 0:
                    other = jnp.where(in_col, load(channel, WIN, cb), load(channel, WIN, cb + 2))
                    picked = jnp.where(in_row, picked, other)
                value.append(picked)
            box = (slice(rb * HALF, (rb + 1) * HALF), slice(cb * LANE, (cb + 1) * LANE))
            p_re = probes_ref[(number, 0) + box]
            p_im = probes_ref[(number, 1) + box]
            field.append((p_re * value[0] - p_im * value[1], p_re * value[1] + p_im * value[0]))
        (re0, im0), (re1, im1) = field
        store_split(g_in[cb], lo, lo, re0 + re1)
        store_split(g_in[cb], hi, lo, im0 + im1)
        d_re = re0 - re1
        d_im = im0 - im1
        store_split(g_in[cb], lo, hi, d_re * tw_c + d_im * tw_s)
        store_split(g_in[cb], hi, hi, d_im * tw_c - d_re * tw_s)
        high, low = g_in[cb][0][...], g_in[cb][1][...]
        wide[cb][...] = mul(first_h[...], high) + mul(first_h[...], low) + mul(first_l[...], high)

    for p in range(2):
        tl_c, tl_s = tw_ref[2], tw_ref[3]
        cols = slice(p * HALF, (p + 1) * HALF)
        re0, re1 = wide[0][lo, cols], wide[1][lo, cols]
        im0, im1 = wide[0][hi, cols], wide[1][hi, cols]
        store_split(h_in[p], lo, lo, re0 + re1)
        store_split(h_in[p], lo, hi, im0 + im1)
        d_re = re0 - re1
        d_im = im0 - im1
        store_split(h_in[p], hi, lo, d_re * tl_c + d_im * tl_s)
        store_split(h_in[p], hi, hi, d_im * tl_c - d_re * tl_s)
        high, low = h_in[p][0][...], h_in[p][1][...]
        tall[p][...] = mul(high, second_h[...]) + mul(low, second_h[...]) + mul(high, second_l[...])

    for p in range(2):
        for q, rows in enumerate((lo, hi)):
            re, im = tall[p][rows, lo], tall[p][rows, hi]
            power = jnp.maximum(re * re + im * im, amp_floor * amp_floor)
            at = q * WIN + p * HALF
            keeping = 1.0 - amps_ref[number, at : at + HALF, :] * lax.rsqrt(power)
            store_split(m_in[p], rows, lo, re * keeping)
            store_split(m_in[p], rows, hi, im * keeping)
        high, low = m_in[p][0][...], m_in[p][1][...]
        tall_back[p][...] = mul(high, first_h[...]) + mul(low, first_h[...]) + mul(high, first_l[...])

    for p in range(2):
        tl_c, tl_s = tw_ref[2], tw_ref[3]
        u_re, u_im = tall_back[p][lo, lo], tall_back[p][lo, hi]
        v_re, v_im = tall_back[p][hi, lo], tall_back[p][hi, hi]
        w_re = v_re * tl_c - v_im * tl_s
        w_im = v_im * tl_c + v_re * tl_s
        store_split(g_out[p], lo, lo, u_re + w_re)
        store_split(g_out[p], lo, hi, u_re - w_re)
        store_split(g_out[p], hi, lo, u_im + w_im)
        store_split(g_out[p], hi, hi, u_im - w_im)
        high, low = g_out[p][0][...], g_out[p][1][...]
        wide_back[p][...] = mul(second_h[...], high) + mul(second_h[...], low) + mul(second_l[...], high)

    for cb in range(2):
        in_col = lane_iota + cb * LANE >= col_start
        cols = slice(cb * LANE, (cb + 1) * LANE)
        u_re, u_im = wide_back[0][lo, cols], wide_back[0][hi, cols]
        v_re, v_im = wide_back[1][lo, cols], wide_back[1][hi, cols]
        w_re = v_re * tw_c - v_im * tw_s
        w_im = v_im * tw_c + v_re * tw_s
        for rb in range(2):
            b_re = u_re + w_re if rb == 0 else u_re - w_re
            b_im = u_im + w_im if rb == 0 else u_im - w_im
            box = (slice(rb * HALF, (rb + 1) * HALF), cols)
            p_re = probes_ref[(number, 0) + box]
            p_im = probes_ref[(number, 1) + box]
            grads = (p_re * b_re + p_im * b_im, p_re * b_im - p_im * b_re)
            for channel in range(2):
                grad = grads[channel]
                targets = [(rb * HALF, grad)]
                if rb == 0:
                    targets = [(0, jnp.where(in_row, grad, 0.0)), (WIN, jnp.where(in_row, 0.0, grad))]
                for at, piece in targets:
                    emit(channel, at, cb, jnp.where(in_col, piece, 0.0))
                    emit(channel, at, cb + 2, jnp.where(in_col, 0.0, piece))


def window(i, j, consts, side, own, carried_own, carried_side, outs):
    border = ("left",) if j == 0 else ("right",)
    own_width = 3 * LANE
    shapes = []
    for _, rows in outs:
        shapes += [jax.ShapeDtypeStruct((2, rows, width), F32) for width in (own_width, LANE)]
    operands = [piece[0] for piece in list(side) + list(own) + list(carried_own) + list(carried_side)]
    kernel = functools.partial(
        window_kernel,
        i,
        j,
        tuple((p[1], p[2], p[3:] + border) for p in side),
        tuple((p[1], p[2], p[3:]) for p in own),
        tuple((at, array.shape[1]) for array, at in carried_own),
        tuple((at, array.shape[1]) for array, at in carried_side),
        outs,
    )
    return pl.pallas_call(
        kernel,
        out_shape=tuple(shapes),
        in_specs=[pl.BlockSpec(memory_space=pltpu.SMEM)] + vmem(4 + len(operands)),
        out_specs=tuple(vmem(len(shapes))),
        scratch_shapes=[pltpu.VMEM((WIN, WIN), BF16)] * 16 + [pltpu.VMEM((WIN, WIN), F32)] * 8,
        cost_estimate=pl.CostEstimate(flops=1_600_000_000, bytes_accessed=5_000_000, transcendentals=0),
        compiler_params=pltpu.CompilerParams(vmem_limit_bytes=VMEM_LIMIT),
        name=f"window_{i}{j}",
    )(*consts, *operands)


def variation_kernel(plan, *refs):
    reg = refs[-1]
    out_ref = refs[-2]
    which = 0
    for part, (lo, hi) in zip(plan, ((0, LANE), (LANE, 4 * LANE), (4 * LANE, 5 * LANE))):
        row = 0
        for first, rows, sides in part:
            for channel in range(2):
                reg[channel, row : row + rows, lo:hi] = kept(refs[which][channel, first : first + rows, :], *sides)
            row += rows
            which += 1

    def chunk(step, _):
        base = pl.multiple_of(step * 32, 8)
        flows = []
        power = tv_smooth
        for channel in range(2):
            block = reg[channel, pl.ds(base, 48), :]
            down = pltpu.roll(block, 47, 0) - block
            right = pltpu.roll(block, 5 * LANE - 1, 1) - block
            power = power + down * down + right * right
            flows.append((down, right))
        inverse = lax.rsqrt(power)
        for channel in range(2):
            down, right = flows[channel]
            down = down * inverse
            right = right * inverse
            change = pltpu.roll(down, 1, 0) - down + pltpu.roll(right, 1, 1) - right
            out_ref[channel, pl.ds(base, 32), :] = tv_weight * change[8:40, LANE : 4 * LANE]
        return 0

    lax.fori_loop(0, 6, chunk, 0)


def variation(left, own, right):
    parts = (left, own, right)
    plan = tuple(
        tuple((p[1], p[2], p[3:] + border) for p in part) for part, border in zip(parts, (("left",), (), ("right",)))
    )
    operands = [piece[0] for part in parts for piece in part]
    return pl.pallas_call(
        functools.partial(variation_kernel, plan),
        out_shape=jax.ShapeDtypeStruct((2, 192, 3 * LANE), F32),
        in_specs=vmem(len(operands)),
        out_specs=pl.BlockSpec(memory_space=pltpu.VMEM),
        scratch_shapes=[pltpu.VMEM((2, 208, 5 * LANE), F32)],
        cost_estimate=pl.CostEstimate(flops=200_000_000, bytes_accessed=5_000_000, transcendentals=0),
        compiler_params=pltpu.CompilerParams(vmem_limit_bytes=VMEM_LIMIT),
        name="variation",
    )(*operands)


def totals_kernel(outs, extras, own_ref, left_ref, right_ref, *refs):
    added, out_refs = refs[: len(extras)], refs[len(extras) :]
    for (first, rows), out in zip(outs, out_refs):
        cuts = {first, first + rows}
        for at, count, _ in extras:
            cuts |= {c for c in (at, at + count) if first < c < first + rows}
        cuts = sorted(cuts)
        for a, b in zip(cuts, cuts[1:]):
            for channel in range(2):
                value = own_ref[channel, a:b, :]
                for (at, count, source), ref in zip(extras, added):
                    if at <= a and b <= at + count:
                        value = value + ref[channel, source + a - at : source + b - at, :]
                to = slice(a - first, b - first)
                out[channel, to, :LANE] = value[:, :LANE] + kept(left_ref[channel, a:b, :], "left")
                out[channel, to, LANE : 2 * LANE] = value[:, LANE : 2 * LANE]
                out[channel, to, 2 * LANE :] = value[:, 2 * LANE :] + kept(right_ref[channel, a:b, :], "right")


def totals(own, from_left, from_right, outs, extras):
    plan = tuple((at, rows, source) for _, source, at, rows in extras)
    return pl.pallas_call(
        functools.partial(totals_kernel, outs, plan),
        out_shape=tuple(jax.ShapeDtypeStruct((2, rows, own.shape[2]), F32) for _, rows in outs),
        in_specs=vmem(3 + len(extras)),
        out_specs=tuple(vmem(len(outs))),
        cost_estimate=pl.CostEstimate(flops=500_000, bytes_accessed=3_000_000, transcendentals=0),
        compiler_params=pltpu.CompilerParams(vmem_limit_bytes=VMEM_LIMIT),
        name="totals",
    )(own, from_left, from_right, *[extra[0] for extra in extras])


def update_kernel(pieces, side, *refs):
    new, left, right = refs[-3:]
    ins = refs[:-3]
    row = 0
    for which, first, rows, grads, masked in pieces:
        for channel in range(2):
            total = None
            for grad, at in grads:
                term = ins[grad][channel, at : at + rows, :]
                if grad == len(ins) - 1:
                    term = kept(term, side)
                total = term if total is None else total + term
            value = ins[which][channel, first : first + rows, :] - step_size * total
            if masked:
                value = kept(value, side)
            new[channel, row : row + rows, :] = value
            left[channel, row : row + rows, :] = value[:, :LANE]
            right[channel, row : row + rows, :] = value[:, 2 * LANE :]
        row += rows


def update(operands, pieces, side):
    rows = sum(piece[2] for piece in pieces)
    shape = [jax.ShapeDtypeStruct((2, rows, width), F32) for width in (3 * LANE, LANE, LANE)]
    return pl.pallas_call(
        functools.partial(update_kernel, pieces, side),
        out_shape=tuple(shape),
        in_specs=vmem(len(operands)),
        out_specs=tuple(vmem(3)),
        cost_estimate=pl.CostEstimate(flops=1_000_000, bytes_accessed=4_000_000, transcendentals=0),
        compiler_params=pltpu.CompilerParams(vmem_limit_bytes=VMEM_LIMIT),
        name="update",
    )(*operands)


def finish_kernel(top_ref, bottom_ref, mid_ref, low_ref, above_ref, below_ref, out_ref):
    for channel in range(2):
        above = mid_ref[channel, :MARGIN, :] + kept(above_ref[channel], "above")
        out_ref[channel, :MARGIN, :] = top_ref[channel, MARGIN:, :] - step_size * above
        out_ref[channel, MARGIN:288, :] = bottom_ref[channel, :192, :] - step_size * mid_ref[channel, MARGIN:, :]
        below = low_ref[channel] + kept(below_ref[channel], "below")
        out_ref[channel, 288:, :] = bottom_ref[channel, 192:288, :] - step_size * below


def finish(*operands):
    return pl.pallas_call(
        finish_kernel,
        out_shape=jax.ShapeDtypeStruct((2, 3 * LANE, 3 * LANE), F32),
        in_specs=vmem(len(operands)),
        out_specs=pl.BlockSpec(memory_space=pltpu.VMEM),
        cost_estimate=pl.CostEstimate(flops=1_000_000, bytes_accessed=4_000_000, transcendentals=0),
        compiler_params=pltpu.CompilerParams(vmem_limit_bytes=VMEM_LIMIT),
        name="finish",
    )(*operands)


def moved(block, axis, distance):
    count = lax.axis_size(axis)
    return lax.ppermute(block, axis, [(n, (n + distance) % count) for n in range(count)])


def rightward(block):
    return moved(block, "col", 1)


def leftward(block):
    return moved(block, "col", -1)


def on_device(table, twiddle, order, object_field, probe, amplitudes, offsets):
    tile = object_field.shape[1]
    last = tile - MARGIN
    band = 2 * MARGIN
    edge = tile - LANE
    obj = object_field
    after = lax.optimization_barrier

    top = moved(obj[:, last:, :], "row", 1)
    left, right = rightward(obj[:, :, edge:]), leftward(obj[:, :, :LANE])
    up_rows, top = after((obj[:, :MARGIN, :], top))
    bottom = moved(up_rows, "row", -1)
    probes, amps = prepare(offsets, probe, amplitudes, order)
    consts = (offsets, table, twiddle, probes, amps)

    top_l, top_r = rightward(top[:, :, edge:]), leftward(top[:, :, :LANE])
    own = [(top, 0, MARGIN, "above"), (obj, 0, last)]
    halves = ((0, band), (band, band))
    lo_o, lo_l, mid_o, mid_l = window(
        0, 0, consts, [(top_l, 0, MARGIN, "above"), (left, 0, last)], own, [], [], halves
    )
    in_r = leftward(lo_l)
    lo_o, lo_r, mid_o, mid_r = window(
        0, 1, consts, [(top_r, 0, MARGIN, "above"), (right, 0, last)], own, [(lo_o, 0), (mid_o, band)], [], halves
    )
    in_l = rightward(lo_r)
    bottom, lo_r = after((bottom, lo_r))
    bot_l, bot_r = rightward(bottom[:, :, edge:]), leftward(bottom[:, :, :LANE])
    tv_top = variation(
        [(top_l, 88, 8, "above"), (left, 0, 200)],
        [(top, 88, 8, "above"), (obj, 0, 200)],
        [(top_r, 88, 8, "above"), (right, 0, 200)],
    )
    (top_sum,) = totals(lo_o, in_l, in_r, ((0, band),), [(tv_top, 0, MARGIN, MARGIN)])
    from_below = moved(top_sum, "row", -1)

    mid_o, top_sum = after((mid_o, top_sum))
    own = [(obj, MARGIN, last), (bottom, 0, MARGIN, "below")]
    whole = ((0, tile),)
    hi_o, hi_l = window(
        1, 0, consts, [(left, MARGIN, last), (bot_l, 0, MARGIN, "below")], own, [(mid_o, 0)], [(mid_l, 0)], whole
    )
    in_r = leftward(hi_l)
    hi_o, hi_r = window(
        1, 1, consts, [(right, MARGIN, last), (bot_r, 0, MARGIN, "below")], own, [(hi_o, 0)], [(mid_r, 0)], whole
    )
    in_l = rightward(hi_r)
    tv_bottom = variation(
        [(left, 184, 200), (bot_l, 0, 8, "below")],
        [(obj, 184, 200), (bottom, 0, 8, "below")],
        [(right, 184, 200), (bot_r, 0, 8, "below")],
    )
    mid_sum, bot_sum = totals(
        hi_o, in_l, in_r, halves, [(tv_top, MARGIN, 0, MARGIN), (tv_bottom, 0, MARGIN, band)]
    )
    from_above = moved(bot_sum, "row", 1)

    low, low_to_left, low_to_right = update(
        (obj, bottom, mid_sum, bot_sum, from_below),
        (
            (0, MARGIN, band, ((2, 0),), False),
            (0, last, MARGIN, ((3, 0), (4, 0)), False),
            (1, 0, MARGIN, ((3, MARGIN), (4, MARGIN)), True),
        ),
        "below",
    )
    low_l, low_r = rightward(low_to_right), leftward(low_to_left)
    own = [(low, 0, tile)]
    mid_o, mid_l, hi_o, hi_l = window(1, 0, consts, [(low_l, 0, tile)], own, [], [], halves)
    in_r = leftward(hi_l)
    mid_o, mid_r, hi_o, hi_r = window(
        1, 1, consts, [(low_r, 0, tile)], own, [(mid_o, 0), (hi_o, band)], [], halves
    )
    in_l = rightward(hi_r)
    tv_bottom = variation([(low_l, 88, 208)], [(low, 88, 208)], [(low_r, 88, 208)])
    low_sum, over = totals(hi_o, in_l, in_r, ((0, MARGIN), (MARGIN, MARGIN)), [(tv_bottom, MARGIN, 0, MARGIN)])
    last_above = moved(over, "row", 1)

    up, up_to_left, up_to_right = update(
        (top, obj, top_sum, from_above),
        (
            (0, 0, MARGIN, ((2, 0), (3, 0)), True),
            (1, 0, MARGIN, ((2, MARGIN), (3, MARGIN)), False),
        ),
        "above",
    )
    up_l, up_r = rightward(up_to_right), leftward(up_to_left)
    mid_o, over = after((mid_o, over))
    own = [(up, 0, band), (low, 0, band)]
    cut = ((0, MARGIN), (MARGIN, last))
    over_o, over_l, lo_o, lo_l = window(
        0, 0, consts, [(up_l, 0, band), (low_l, 0, band)], own, [(mid_o, band)], [(mid_l, band)], cut
    )
    over_r, in_r = leftward(over_l), leftward(lo_l)
    over_o, over_rr, lo_o, lo_r = window(
        0, 1, consts, [(up_r, 0, band), (low_r, 0, band)], own, [(over_o, 0), (lo_o, MARGIN)], [(mid_r, band)], cut
    )
    over_l = rightward(over_rr)
    (over,) = totals(over_o, over_l, over_r, ((0, MARGIN),), [])
    last_below = moved(over, "row", -1)
    in_l = rightward(lo_r)
    tv_top = variation(
        [(up_l, 88, 104), (low_l, 0, 104)], [(up, 88, 104), (low, 0, 104)], [(up_r, 88, 104), (low_r, 0, 104)]
    )
    (mid_sum,) = totals(lo_o, in_l, in_r, ((0, last),), [(tv_top, 0, 0, band), (tv_bottom, 0, band, MARGIN)])
    return finish(up, low, mid_sum, low_sum, last_above, last_below)


def solution(mesh):
    table, twiddle, order = tables()
    body = jax.shard_map(
        on_device,
        mesh=mesh,
        in_specs=(P(), P(), P(), P(None, "row", "col"), P(), P("row", "col"), P("row", "col", None)),
        out_specs=P(None, "row", "col"),
        check_vma=False,
    )

    def step(object_field, probe, amplitudes, offsets):
        return body(table, twiddle, order, object_field, probe, amplitudes, offsets)

    return step
```

```python
import functools
import math

import jax
import jax.numpy as jnp
import numpy as np
from jax import lax
from jax.experimental import pallas as pl
from jax.experimental.pallas import tpu as pltpu
from jax.sharding import PartitionSpec as P

WIN = 256
HALF = 128
MARGIN = 96
LANE = 128
VMEM_LIMIT = 24 * 1024 * 1024

step_size = 0.3
tv_weight = 0.2
tv_smooth = 0.1
amp_floor = 0.5

F32 = jnp.float32
BF16 = jnp.bfloat16


def tables():
    counter = np.arange(HALF)
    angle = (counter[:, None] * counter[None, :] % HALF) * (2.0 * math.pi / HALF)
    cosine = np.cos(angle) / math.sqrt(WIN)
    sine = np.sin(angle) / math.sqrt(WIN)
    first = np.block([[cosine, sine], [-sine, cosine]])
    second = np.block([[cosine, -sine], [sine, cosine]])
    parts = []
    for table in (first, second):
        table = table.astype(np.float32)
        high = table.astype(jnp.bfloat16)
        low = (table - high.astype(np.float32)).astype(jnp.bfloat16)
        parts += [high, low]
    turn = counter * (2.0 * math.pi / WIN)
    rows = np.stack([np.cos(turn), np.sin(turn)])
    by_row = np.broadcast_to(rows[:, :, None], (2, HALF, HALF))
    by_lane = np.broadcast_to(rows[:, None, :], (2, HALF, HALF))
    twiddle = np.concatenate([by_row, by_lane]).astype(np.float32)
    order = np.zeros((WIN, WIN), np.float32)
    for parity in range(2):
        order[2 * counter + parity, parity * HALF + counter] = 1.0
    return np.stack(parts), twiddle, order.astype(jnp.bfloat16)


def split(value):
    high = value.astype(BF16)
    return high, (value - high.astype(F32)).astype(BF16)


def has(side):
    if side == "above":
        return lax.axis_index("row") > 0
    if side == "below":
        return lax.axis_index("row") < lax.axis_size("row") - 1
    return (lax.axis_index("col") > 0) & (lax.axis_index("col") < lax.axis_size("col") - 1)


def even_column():
    return lax.axis_index("col") % 2 == 0


def kept(value, *sides):
    for side in sides:
        value = jnp.where(has(side), value, 0.0)
    return value


def mul(left, right):
    return jnp.dot(left, right, preferred_element_type=F32)


def vmem(count):
    return [pl.BlockSpec(memory_space=pltpu.VMEM)] * count


def prepare_kernel(off_ref, probe_ref, amp_ref, order_ref, probes_ref, amps_ref, parts_ref):
    order = order_ref[...]
    for i in range(2):
        for j in range(2):
            row = off_ref[i, j, 0]
            col = (off_ref[i, j, 1] + (32 if j == 0 else 224)) % WIN
            for channel in range(2):
                turned = pltpu.roll(probe_ref[channel], row, 0)
                probes_ref[2 * i + j, channel] = pltpu.roll(turned, col, 1)
            amp = amp_ref[i * WIN : (i + 1) * WIN, j * WIN : (j + 1) * WIN]
            high, rest = split(amp)
            middle, low = split(amp - high.astype(F32) - rest.astype(F32))
            sorted_lanes = mul(high, order) + mul(rest, order) + mul(middle, order)
            for q in range(2):
                parts_ref[...] = sorted_lanes[:, q * HALF : (q + 1) * HALF]
                for p in range(2):
                    at = q * WIN + p * HALF
                    amps_ref[2 * i + j, at : at + HALF, :] = parts_ref[pl.ds(p, HALF, stride=2), :]


def prepare(offsets, probe, amplitudes, order):
    return pl.pallas_call(
        prepare_kernel,
        out_shape=(
            jax.ShapeDtypeStruct((4, 2, WIN, WIN), F32),
            jax.ShapeDtypeStruct((4, 2 * WIN, HALF), F32),
        ),
        in_specs=[pl.BlockSpec(memory_space=pltpu.SMEM)] + vmem(3),
        out_specs=tuple(vmem(2)),
        scratch_shapes=[pltpu.VMEM((WIN, HALF), F32)],
        cost_estimate=pl.CostEstimate(flops=400_000_000, bytes_accessed=6_000_000, transcendentals=0),
        compiler_params=pltpu.CompilerParams(vmem_limit_bytes=VMEM_LIMIT),
        name="prepare",
    )(offsets, probe, amplitudes, order)


def rows_of(pieces, refs, first, rows):
    found, at = [], 0
    for ref, (start, count, sides) in zip(refs, pieces):
        lo, hi = max(first, at), min(first + rows, at + count)
        if lo < hi:
            found.append((ref, start + lo - at, hi - lo, sides))
        at += count
    return found


def window_kernel(i, near, side, own, carried_own, carried_side, outs, *refs):
    off_ref, tab_ref, tw_ref, probes_ref, amps_ref = refs[:5]
    refs = refs[5:]
    side_refs, refs = refs[: len(side)], refs[len(side) :]
    own_refs, refs = refs[: len(own)], refs[len(own) :]
    sum_refs, refs = refs[: len(carried_own)], refs[len(carried_own) :]
    strip_refs, refs = refs[: len(carried_side)], refs[len(carried_side) :]
    out_refs, refs = refs[: 2 * len(outs)], refs[2 * len(outs) :]
    halves = [refs[n : n + 2] for n in range(0, 16, 2)]
    g_in, h_in, m_in, g_out = halves[0:2], halves[2:4], halves[4:6], halves[6:8]
    wide, tall, tall_back, wide_back = refs[16:18], refs[18:20], refs[20:22], refs[22:24]

    to_right = even_column() if near else jnp.logical_not(even_column())
    j = jnp.where(to_right, 1, 0)
    number = 2 * i + j
    row_start = off_ref[i, j, 0]
    col_start = off_ref[i, j, 1]
    row_iota = lax.broadcasted_iota(jnp.int32, (HALF, HALF), 0)
    lane_iota = lax.broadcasted_iota(jnp.int32, (HALF, HALF), 1)
    in_row = row_iota >= row_start
    sign = jnp.where(to_right, -1, 1)
    in_first = (
        sign * lane_iota >= jnp.where(to_right, 33 - col_start, 32 + col_start),
        lane_iota >= jnp.where(to_right, 96 + col_start, col_start - 96),
    )
    first_h, first_l, second_h, second_l = (tab_ref.at[n] for n in range(4))
    groups = (("strip", 1), (0, 2))

    def place(group):
        if group == "strip":
            return True, slice(0, LANE)
        return False, slice(group * LANE, (group + 1) * LANE)

    def load(channel, first, group):
        is_strip, lanes = place(group)
        pieces, sources = (side, side_refs) if is_strip else (own, own_refs)
        blocks = [
            kept(ref[channel, at : at + rows, lanes], *sides)
            for ref, at, rows, sides in rows_of(pieces, sources, first, HALF)
        ]
        return blocks[0] if len(blocks) == 1 else jnp.concatenate(blocks, axis=0)

    def emit(channel, first, group, value):
        is_strip, lanes = place(group)
        extra = (carried_side, strip_refs) if is_strip else (carried_own, sum_refs)
        which = 1 if is_strip else 0
        for n, (start, count) in enumerate(outs):
            lo, hi = max(first, start), min(first + HALF, start + count)
            if lo >= hi:
                continue
            cuts = sorted({lo, hi} | {c for at, rows in extra[0] for c in (at, at + rows) if lo < c < hi})
            for a, b in zip(cuts, cuts[1:]):
                part = value[a - first : b - first]
                for (at, rows), ref in zip(*extra):
                    if at <= a and b <= at + rows:
                        part = part + ref[channel, a - at : b - at, lanes]
                out_refs[2 * n + which][channel, a - start : b - start, lanes] = part

    def store_split(pair, rows, lanes, value):
        high, low = split(value)
        pair[0][rows, lanes] = high
        pair[1][rows, lanes] = low

    lo, hi = slice(0, HALF), slice(HALF, WIN)
    tw_c, tw_s = tw_ref[0], tw_ref[1]
    for cb in range(2):
        in_col = in_first[cb]
        first_group, second_group = groups[cb]
        field = []
        for rb in range(2):
            value = []
            for channel in range(2):
                at = rb * HALF
                picked = jnp.where(in_col, load(channel, at, first_group), load(channel, at, second_group))
                if rb == 0:
                    other = jnp.where(in_col, load(channel, WIN, first_group), load(channel, WIN, second_group))
                    picked = jnp.where(in_row, picked, other)
                value.append(picked)
            box = (slice(rb * HALF, (rb + 1) * HALF), slice(cb * LANE, (cb + 1) * LANE))
            p_re = probes_ref[(number, 0) + box]
            p_im = probes_ref[(number, 1) + box]
            field.append((p_re * value[0] - p_im * value[1], p_re * value[1] + p_im * value[0]))
        (re0, im0), (re1, im1) = field
        store_split(g_in[cb], lo, lo, re0 + re1)
        store_split(g_in[cb], hi, lo, im0 + im1)
        d_re = re0 - re1
        d_im = im0 - im1
        store_split(g_in[cb], lo, hi, d_re * tw_c + d_im * tw_s)
        store_split(g_in[cb], hi, hi, d_im * tw_c - d_re * tw_s)
        high, low = g_in[cb][0][...], g_in[cb][1][...]
        wide[cb][...] = mul(first_h[...], high) + mul(first_h[...], low) + mul(first_l[...], high)

    for p in range(2):
        tl_c, tl_s = tw_ref[2], tw_ref[3]
        cols = slice(p * HALF, (p + 1) * HALF)
        re0, re1 = wide[0][lo, cols], wide[1][lo, cols]
        im0, im1 = wide[0][hi, cols], wide[1][hi, cols]
        store_split(h_in[p], lo, lo, re0 + re1)
        store_split(h_in[p], lo, hi, im0 + im1)
        d_re = re0 - re1
        d_im = im0 - im1
        store_split(h_in[p], hi, lo, d_re * tl_c + d_im * tl_s)
        store_split(h_in[p], hi, hi, d_im * tl_c - d_re * tl_s)
        high, low = h_in[p][0][...], h_in[p][1][...]
        tall[p][...] = mul(high, second_h[...]) + mul(low, second_h[...]) + mul(high, second_l[...])

    for p in range(2):
        for q, rows in enumerate((lo, hi)):
            re, im = tall[p][rows, lo], tall[p][rows, hi]
            power = jnp.maximum(re * re + im * im, amp_floor * amp_floor)
            at = q * WIN + p * HALF
            keeping = 1.0 - amps_ref[number, at : at + HALF, :] * lax.rsqrt(power)
            store_split(m_in[p], rows, lo, re * keeping)
            store_split(m_in[p], rows, hi, im * keeping)
        high, low = m_in[p][0][...], m_in[p][1][...]
        tall_back[p][...] = mul(high, first_h[...]) + mul(low, first_h[...]) + mul(high, first_l[...])

    for p in range(2):
        tl_c, tl_s = tw_ref[2], tw_ref[3]
        u_re, u_im = tall_back[p][lo, lo], tall_back[p][lo, hi]
        v_re, v_im = tall_back[p][hi, lo], tall_back[p][hi, hi]
        w_re = v_re * tl_c - v_im * tl_s
        w_im = v_im * tl_c + v_re * tl_s
        store_split(g_out[p], lo, lo, u_re + w_re)
        store_split(g_out[p], lo, hi, u_re - w_re)
        store_split(g_out[p], hi, lo, u_im + w_im)
        store_split(g_out[p], hi, hi, u_im - w_im)
        high, low = g_out[p][0][...], g_out[p][1][...]
        wide_back[p][...] = mul(second_h[...], high) + mul(second_h[...], low) + mul(second_l[...], high)

    for cb in range(2):
        in_col = in_first[cb]
        first_group, second_group = groups[cb]
        cols = slice(cb * LANE, (cb + 1) * LANE)
        u_re, u_im = wide_back[0][lo, cols], wide_back[0][hi, cols]
        v_re, v_im = wide_back[1][lo, cols], wide_back[1][hi, cols]
        w_re = v_re * tw_c - v_im * tw_s
        w_im = v_im * tw_c + v_re * tw_s
        for rb in range(2):
            b_re = u_re + w_re if rb == 0 else u_re - w_re
            b_im = u_im + w_im if rb == 0 else u_im - w_im
            box = (slice(rb * HALF, (rb + 1) * HALF), cols)
            p_re = probes_ref[(number, 0) + box]
            p_im = probes_ref[(number, 1) + box]
            grads = (p_re * b_re + p_im * b_im, p_re * b_im - p_im * b_re)
            for channel in range(2):
                grad = grads[channel]
                targets = [(rb * HALF, grad)]
                if rb == 0:
                    targets = [(0, jnp.where(in_row, grad, 0.0)), (WIN, jnp.where(in_row, 0.0, grad))]
                for at, piece in targets:
                    emit(channel, at, first_group, jnp.where(in_col, piece, 0.0))
                    emit(channel, at, second_group, jnp.where(in_col, 0.0, piece))


def window(i, near, consts, side, own, carried_own, carried_side, outs):
    border = () if near else ("beside",)
    own_width = 3 * LANE
    shapes = []
    for _, rows in outs:
        shapes += [jax.ShapeDtypeStruct((2, rows, width), F32) for width in (own_width, LANE)]
    operands = [piece[0] for piece in list(side) + list(own) + list(carried_own) + list(carried_side)]
    kernel = functools.partial(
        window_kernel,
        i,
        near,
        tuple((p[1], p[2], p[3:] + border) for p in side),
        tuple((p[1], p[2], p[3:]) for p in own),
        tuple((at, array.shape[1]) for array, at in carried_own),
        tuple((at, array.shape[1]) for array, at in carried_side),
        outs,
    )
    return pl.pallas_call(
        kernel,
        out_shape=tuple(shapes),
        in_specs=[pl.BlockSpec(memory_space=pltpu.SMEM)] + vmem(4 + len(operands)),
        out_specs=tuple(vmem(len(shapes))),
        scratch_shapes=[pltpu.VMEM((WIN, WIN), BF16)] * 16 + [pltpu.VMEM((WIN, WIN), F32)] * 8,
        cost_estimate=pl.CostEstimate(flops=1_600_000_000, bytes_accessed=5_000_000, transcendentals=0),
        compiler_params=pltpu.CompilerParams(vmem_limit_bytes=VMEM_LIMIT),
        name=f"window_{i}" + ("a" if near else "b"),
    )(*consts, *operands)


def variation_kernel(near, own, far, *refs):
    reg = refs[-1]
    out_ref = refs[-2]
    near_refs, refs = refs[: len(near)], refs[len(near) :]
    own_refs, far_refs = refs[: len(own)], refs[len(own) : len(own) + len(far)]
    even = even_column()

    def block(pieces, sources, at, channel):
        first, rows, sides = pieces[at]
        return kept(sources[at][channel, first : first + rows, :], *sides)

    row = 0
    for n, (_, rows, _) in enumerate(own):
        for channel in range(2):
            span = slice(row, row + rows)
            one = block(near, near_refs, n, channel)
            other = block(far, far_refs, n, channel)
            reg[channel, span, LANE : 4 * LANE] = block(own, own_refs, n, channel)
            reg[channel, span, :LANE] = jnp.where(even, other, one)
            reg[channel, span, 4 * LANE :] = jnp.where(even, one, other)
        row += rows

    def chunk(step, _):
        base = pl.multiple_of(step * 32, 8)
        flows = []
        power = tv_smooth
        for channel in range(2):
            block = reg[channel, pl.ds(base, 48), :]
            down = pltpu.roll(block, 47, 0) - block
            right = pltpu.roll(block, 5 * LANE - 1, 1) - block
            power = power + down * down + right * right
            flows.append((down, right))
        inverse = lax.rsqrt(power)
        for channel in range(2):
            down, right = flows[channel]
            down = down * inverse
            right = right * inverse
            change = pltpu.roll(down, 1, 0) - down + pltpu.roll(right, 1, 1) - right
            out_ref[channel, pl.ds(base, 32), :] = tv_weight * change[8:40, LANE : 4 * LANE]
        return 0

    lax.fori_loop(0, 6, chunk, 0)


def variation(near, own, far):
    parts = (near, own, far)
    plan = [
        tuple((p[1], p[2], p[3:] + border) for p in part) for part, border in zip(parts, ((), (), ("beside",)))
    ]
    operands = [piece[0] for part in parts for piece in part]
    return pl.pallas_call(
        functools.partial(variation_kernel, *plan),
        out_shape=jax.ShapeDtypeStruct((2, 192, 3 * LANE), F32),
        in_specs=vmem(len(operands)),
        out_specs=pl.BlockSpec(memory_space=pltpu.VMEM),
        scratch_shapes=[pltpu.VMEM((2, 208, 5 * LANE), F32)],
        cost_estimate=pl.CostEstimate(flops=200_000_000, bytes_accessed=5_000_000, transcendentals=0),
        compiler_params=pltpu.CompilerParams(vmem_limit_bytes=VMEM_LIMIT),
        name="variation",
    )(*operands)


def totals_kernel(outs, extras, own_ref, near_ref, far_ref, *refs):
    added, out_refs = refs[: len(extras)], refs[len(extras) :]
    even = even_column()
    for (first, rows), out in zip(outs, out_refs):
        cuts = {first, first + rows}
        for at, count, _ in extras:
            cuts |= {c for c in (at, at + count) if first < c < first + rows}
        cuts = sorted(cuts)
        for a, b in zip(cuts, cuts[1:]):
            for channel in range(2):
                value = own_ref[channel, a:b, :]
                for (at, count, source), ref in zip(extras, added):
                    if at <= a and b <= at + count:
                        value = value + ref[channel, source + a - at : source + b - at, :]
                to = slice(a - first, b - first)
                one = near_ref[channel, a:b, :]
                other = kept(far_ref[channel, a:b, :], "beside")
                out[channel, to, :LANE] = value[:, :LANE] + jnp.where(even, other, one)
                out[channel, to, LANE : 2 * LANE] = value[:, LANE : 2 * LANE]
                out[channel, to, 2 * LANE :] = value[:, 2 * LANE :] + jnp.where(even, one, other)


def totals(own, near, far, outs, extras):
    plan = tuple((at, rows, source) for _, source, at, rows in extras)
    return pl.pallas_call(
        functools.partial(totals_kernel, outs, plan),
        out_shape=tuple(jax.ShapeDtypeStruct((2, rows, own.shape[2]), F32) for _, rows in outs),
        in_specs=vmem(3 + len(extras)),
        out_specs=tuple(vmem(len(outs))),
        cost_estimate=pl.CostEstimate(flops=500_000, bytes_accessed=3_000_000, transcendentals=0),
        compiler_params=pltpu.CompilerParams(vmem_limit_bytes=VMEM_LIMIT),
        name="totals",
    )(own, near, far, *[extra[0] for extra in extras])


def update_kernel(pieces, side, *refs):
    new, near, far = refs[-3:]
    even = even_column()
    ins = refs[:-3]
    row = 0
    for which, first, rows, grads, masked in pieces:
        for channel in range(2):
            total = None
            for grad, at in grads:
                term = ins[grad][channel, at : at + rows, :]
                if grad == len(ins) - 1:
                    term = kept(term, side)
                total = term if total is None else total + term
            value = ins[which][channel, first : first + rows, :] - step_size * total
            if masked:
                value = kept(value, side)
            new[channel, row : row + rows, :] = value
            near[channel, row : row + rows, :] = jnp.where(even, value[:, 2 * LANE :], value[:, :LANE])
            far[channel, row : row + rows, :] = jnp.where(even, value[:, :LANE], value[:, 2 * LANE :])
        row += rows


def update(operands, pieces, side):
    rows = sum(piece[2] for piece in pieces)
    shape = [jax.ShapeDtypeStruct((2, rows, width), F32) for width in (3 * LANE, LANE, LANE)]
    return pl.pallas_call(
        functools.partial(update_kernel, pieces, side),
        out_shape=tuple(shape),
        in_specs=vmem(len(operands)),
        out_specs=tuple(vmem(3)),
        cost_estimate=pl.CostEstimate(flops=1_000_000, bytes_accessed=4_000_000, transcendentals=0),
        compiler_params=pltpu.CompilerParams(vmem_limit_bytes=VMEM_LIMIT),
        name="update",
    )(*operands)


def finish_kernel(top_ref, bottom_ref, mid_ref, low_ref, above_ref, below_ref, out_ref):
    for channel in range(2):
        above = mid_ref[channel, :MARGIN, :] + kept(above_ref[channel], "above")
        out_ref[channel, :MARGIN, :] = top_ref[channel, MARGIN:, :] - step_size * above
        out_ref[channel, MARGIN:288, :] = bottom_ref[channel, :192, :] - step_size * mid_ref[channel, MARGIN:, :]
        below = low_ref[channel] + kept(below_ref[channel], "below")
        out_ref[channel, 288:, :] = bottom_ref[channel, 192:288, :] - step_size * below


def finish(*operands):
    return pl.pallas_call(
        finish_kernel,
        out_shape=jax.ShapeDtypeStruct((2, 3 * LANE, 3 * LANE), F32),
        in_specs=vmem(len(operands)),
        out_specs=pl.BlockSpec(memory_space=pltpu.VMEM),
        cost_estimate=pl.CostEstimate(flops=1_000_000, bytes_accessed=4_000_000, transcendentals=0),
        compiler_params=pltpu.CompilerParams(vmem_limit_bytes=VMEM_LIMIT),
        name="finish",
    )(*operands)


def moved(block, axis, distance):
    count = lax.axis_size(axis)
    return lax.ppermute(block, axis, [(n, (n + distance) % count) for n in range(count)])


def to_near(block):
    rows, cols = lax.axis_size("row"), lax.axis_size("col")
    return lax.ppermute(block, ("row", "col"), [(r * cols + c, r * cols + (c ^ 1)) for r in range(rows) for c in range(cols)])


def to_far(block):
    rows, cols = lax.axis_size("row"), lax.axis_size("col")
    step = 2 if rows % 4 == 0 else 1 if rows % 2 == 0 else 0
    route = []
    for r in range(rows):
        for c in range(cols):
            other = c - 1 if c % 2 == 0 else c + 1
            inside = 0 <= other < cols
            route.append((r * cols + c, r * cols + other if inside else (r ^ step) * cols + c))
    return lax.ppermute(block, ("row", "col"), route)


def edges(block):
    width = block.shape[2]
    low, high = block[:, :, :LANE], block[:, :, width - LANE :]
    even = even_column()
    return jnp.where(even, high, low), jnp.where(even, low, high)


def on_device(table, twiddle, order, object_field, probe, amplitudes, offsets):
    tile = object_field.shape[1]
    last = tile - MARGIN
    band = 2 * MARGIN
    obj = object_field
    after = lax.optimization_barrier

    top = moved(obj[:, last:, :], "row", 1)
    near_strip, far_strip = edges(obj)
    far, near = to_far(far_strip), to_near(near_strip)
    up_rows, top = after((obj[:, :MARGIN, :], top))
    bottom = moved(up_rows, "row", -1)
    probes, amps = prepare(offsets, probe, amplitudes, order)
    consts = (offsets, table, twiddle, probes, amps)

    near_strip, far_strip = edges(top)
    top_b, top_a = to_far(far_strip), to_near(near_strip)
    own = [(top, 0, MARGIN, "above"), (obj, 0, last)]
    halves = ((0, band), (band, band))
    lo_o, lo_b, mid_o, mid_b = window(
        0, False, consts, [(top_b, 0, MARGIN, "above"), (far, 0, last)], own, [], [], halves
    )
    in_b = to_far(lo_b)
    lo_o, lo_a, mid_o, mid_a = window(
        0, True, consts, [(top_a, 0, MARGIN, "above"), (near, 0, last)], own, [(lo_o, 0), (mid_o, band)], [], halves
    )
    in_a = to_near(lo_a)
    bottom, lo_a = after((bottom, lo_a))
    near_strip, far_strip = edges(bottom)
    bot_b, bot_a = to_far(far_strip), to_near(near_strip)
    tv_top = variation(
        [(top_a, 88, 8, "above"), (near, 0, 200)],
        [(top, 88, 8, "above"), (obj, 0, 200)],
        [(top_b, 88, 8, "above"), (far, 0, 200)],
    )
    (top_sum,) = totals(lo_o, in_a, in_b, ((0, band),), [(tv_top, 0, MARGIN, MARGIN)])
    from_below = moved(top_sum, "row", -1)

    mid_o, top_sum = after((mid_o, top_sum))
    own = [(obj, MARGIN, last), (bottom, 0, MARGIN, "below")]
    whole = ((0, tile),)
    hi_o, hi_b = window(
        1, False, consts, [(far, MARGIN, last), (bot_b, 0, MARGIN, "below")], own, [(mid_o, 0)], [(mid_b, 0)], whole
    )
    in_b = to_far(hi_b)
    hi_o, hi_a = window(
        1, True, consts, [(near, MARGIN, last), (bot_a, 0, MARGIN, "below")], own, [(hi_o, 0)], [(mid_a, 0)], whole
    )
    in_a = to_near(hi_a)
    tv_bottom = variation(
        [(near, 184, 200), (bot_a, 0, 8, "below")],
        [(obj, 184, 200), (bottom, 0, 8, "below")],
        [(far, 184, 200), (bot_b, 0, 8, "below")],
    )
    mid_sum, bot_sum = totals(
        hi_o, in_a, in_b, halves, [(tv_top, MARGIN, 0, MARGIN), (tv_bottom, 0, MARGIN, band)]
    )
    from_above = moved(bot_sum, "row", 1)

    low, near_strip, far_strip = update(
        (obj, bottom, mid_sum, bot_sum, from_below),
        (
            (0, MARGIN, band, ((2, 0),), False),
            (0, last, MARGIN, ((3, 0), (4, 0)), False),
            (1, 0, MARGIN, ((3, MARGIN), (4, MARGIN)), True),
        ),
        "below",
    )
    low_b, low_a = to_far(far_strip), to_near(near_strip)
    own = [(low, 0, tile)]
    mid_o, mid_a, hi_o, hi_a = window(1, True, consts, [(low_a, 0, tile)], own, [], [], halves)
    in_a = to_near(hi_a)
    mid_o, mid_b, hi_o, hi_b = window(
        1, False, consts, [(low_b, 0, tile)], own, [(mid_o, 0), (hi_o, band)], [], halves
    )
    in_b = to_far(hi_b)
    tv_bottom = variation([(low_a, 88, 208)], [(low, 88, 208)], [(low_b, 88, 208)])
    low_sum, over = totals(hi_o, in_a, in_b, ((0, MARGIN), (MARGIN, MARGIN)), [(tv_bottom, MARGIN, 0, MARGIN)])
    last_above = moved(over, "row", 1)

    up, near_strip, far_strip = update(
        (top, obj, top_sum, from_above),
        (
            (0, 0, MARGIN, ((2, 0), (3, 0)), True),
            (1, 0, MARGIN, ((2, MARGIN), (3, MARGIN)), False),
        ),
        "above",
    )
    up_b, up_a = to_far(far_strip), to_near(near_strip)
    mid_o, over = after((mid_o, over))
    own = [(up, 0, band), (low, 0, band)]
    cut = ((0, MARGIN), (MARGIN, last))
    over_o, over_a, lo_o, lo_a = window(
        0, True, consts, [(up_a, 0, band), (low_a, 0, band)], own, [(mid_o, band)], [(mid_a, band)], cut
    )
    over_a, in_a = to_near(over_a), to_near(lo_a)
    over_o, over_b, lo_o, lo_b = window(
        0, False, consts, [(up_b, 0, band), (low_b, 0, band)], own, [(over_o, 0), (lo_o, MARGIN)], [(mid_b, band)], cut
    )
    over_b = to_far(over_b)
    (over,) = totals(over_o, over_a, over_b, ((0, MARGIN),), [])
    last_below = moved(over, "row", -1)
    in_b = to_far(lo_b)
    tv_top = variation(
        [(up_a, 88, 104), (low_a, 0, 104)], [(up, 88, 104), (low, 0, 104)], [(up_b, 88, 104), (low_b, 0, 104)]
    )
    (mid_sum,) = totals(lo_o, in_a, in_b, ((0, last),), [(tv_top, 0, 0, band), (tv_bottom, 0, band, MARGIN)])
    return finish(up, low, mid_sum, low_sum, last_above, last_below)


def solution(mesh):
    table, twiddle, order = tables()
    body = jax.shard_map(
        on_device,
        mesh=mesh,
        in_specs=(P(), P(), P(), P(None, "row", "col"), P(), P("row", "col"), P("row", "col", None)),
        out_specs=P(None, "row", "col"),
        check_vma=False,
    )

    def step(object_field, probe, amplitudes, offsets):
        return body(table, twiddle, order, object_field, probe, amplitudes, offsets)

    return step
```

```python
import functools
import math

import jax
import jax.numpy as jnp
import numpy as np
from jax import lax
from jax.experimental import pallas as pl
from jax.experimental.pallas import tpu as pltpu
from jax.sharding import PartitionSpec as P


WIN = 256
HALF = 128
MARGIN = 96
LANE = 128
COST = pl.CostEstimate(flops=100_000, bytes_accessed=100_000, transcendentals=0)
VMEM_LIMIT = 24 * 1024 * 1024

step_size = 0.3
tv_weight = 0.2
tv_smooth = 0.1
amp_floor = 0.5

F32 = jnp.float32
BF16 = jnp.bfloat16


def tables():
    counter = np.arange(HALF)
    angle = (counter[:, None] * counter[None, :] % HALF) * (2.0 * math.pi / HALF)
    cosine = np.cos(angle) / math.sqrt(WIN)
    sine = np.sin(angle) / math.sqrt(WIN)
    first = np.block([[cosine, sine], [-sine, cosine]])
    second = np.block([[cosine, -sine], [sine, cosine]])
    parts = []
    for table in (first, second):
        table = table.astype(np.float32)
        high = table.astype(jnp.bfloat16)
        low = (table - high.astype(np.float32)).astype(jnp.bfloat16)
        parts += [high, low]
    turn = counter * (2.0 * math.pi / WIN)
    rows = np.stack([np.cos(turn), np.sin(turn)])
    by_row = np.broadcast_to(rows[:, :, None], (2, HALF, HALF))
    by_lane = np.broadcast_to(rows[:, None, :], (2, HALF, HALF))
    twiddle = np.concatenate([by_row, by_lane]).astype(np.float32)
    order = np.zeros((WIN, WIN), np.float32)
    for parity in range(2):
        order[2 * counter + parity, parity * HALF + counter] = 1.0
    return np.stack(parts), twiddle, order.astype(jnp.bfloat16)


def split(value):
    high = value.astype(BF16)
    return high, (value - high.astype(F32)).astype(BF16)


def has(side):
    if side == "above":
        return lax.axis_index("row") > 0
    if side == "below":
        return lax.axis_index("row") < lax.axis_size("row") - 1
    return (lax.axis_index("col") > 0) & (lax.axis_index("col") < lax.axis_size("col") - 1)


def even_column():
    return lax.axis_index("col") % 2 == 0


def kept(value, *sides):
    for side in sides:
        value = jnp.where(has(side), value, 0.0)
    return value


def mul(left, right):
    return jnp.dot(left, right, preferred_element_type=F32)


def vmem(count):
    return [pl.BlockSpec(memory_space=pltpu.VMEM)] * count


def prepare_kernel(off_ref, probe_ref, amp_ref, order_ref, probes_ref, amps_ref, parts_ref):
    order = order_ref[...]
    for i in range(2):
        for j in range(2):
            row = off_ref[i, j, 0]
            col = (off_ref[i, j, 1] + (32 if j == 0 else 224)) % WIN
            for channel in range(2):
                turned = pltpu.roll(probe_ref[channel], row, 0)
                probes_ref[2 * i + j, channel] = pltpu.roll(turned, col, 1)
            amp = amp_ref[i * WIN : (i + 1) * WIN, j * WIN : (j + 1) * WIN]
            high, rest = split(amp)
            middle, _ = split(amp - high.astype(F32) - rest.astype(F32))
            sorted_lanes = mul(high, order) + mul(rest, order) + mul(middle, order)
            for q in range(2):
                parts_ref[...] = sorted_lanes[:, q * HALF : (q + 1) * HALF]
                for p in range(2):
                    at = q * WIN + p * HALF
                    amps_ref[2 * i + j, at : at + HALF, :] = parts_ref[pl.ds(p, HALF, stride=2), :]


def prepare(offsets, probe, amplitudes, order):
    return pl.pallas_call(
        prepare_kernel,
        out_shape=(
            jax.ShapeDtypeStruct((4, 2, WIN, WIN), F32),
            jax.ShapeDtypeStruct((4, 2 * WIN, HALF), F32),
        ),
        in_specs=[pl.BlockSpec(memory_space=pltpu.SMEM)] + vmem(3),
        out_specs=tuple(vmem(2)),
        scratch_shapes=[pltpu.VMEM((WIN, HALF), F32)],
        cost_estimate=COST,
        compiler_params=pltpu.CompilerParams(vmem_limit_bytes=VMEM_LIMIT),
        name="prepare",
    )(offsets, probe, amplitudes, order)


def rows_of(pieces, refs, first, rows):
    found, at = [], 0
    for ref, (start, count, sides) in zip(refs, pieces):
        lo, hi = max(first, at), min(first + rows, at + count)
        if lo < hi:
            found.append((ref, start + lo - at, hi - lo, sides))
        at += count
    return found


def window_kernel(i, near, side, own, carried_own, carried_side, outs, *refs):
    off_ref, tab_ref, tw_ref, probes_ref, amps_ref = refs[:5]
    refs = refs[5:]
    side_refs, refs = refs[: len(side)], refs[len(side) :]
    own_refs, refs = refs[: len(own)], refs[len(own) :]
    sum_refs, refs = refs[: len(carried_own)], refs[len(carried_own) :]
    strip_refs, refs = refs[: len(carried_side)], refs[len(carried_side) :]
    out_refs, refs = refs[: 2 * len(outs)], refs[2 * len(outs) :]
    halves = [refs[n : n + 2] for n in range(0, 16, 2)]
    g_in, h_in, m_in, g_out = halves[0:2], halves[2:4], halves[4:6], halves[6:8]
    wide, tall, tall_back, wide_back = refs[16:18], refs[18:20], refs[20:22], refs[22:24]

    to_right = even_column() if near else jnp.logical_not(even_column())
    j = jnp.where(to_right, 1, 0)
    number = 2 * i + j
    row_start = off_ref[i, j, 0]
    col_start = off_ref[i, j, 1]
    row_iota = lax.broadcasted_iota(jnp.int32, (HALF, HALF), 0)
    lane_iota = lax.broadcasted_iota(jnp.int32, (HALF, HALF), 1)
    in_row = row_iota >= row_start
    sign = jnp.where(to_right, -1, 1)
    in_first = (
        sign * lane_iota >= jnp.where(to_right, 33 - col_start, 32 + col_start),
        lane_iota >= jnp.where(to_right, 96 + col_start, col_start - 96),
    )
    first_h, first_l, second_h, second_l = (tab_ref.at[n] for n in range(4))
    groups = (("strip", 1), (0, 2))

    def place(group):
        if group == "strip":
            return True, slice(0, LANE)
        return False, slice(group * LANE, (group + 1) * LANE)

    def load(channel, first, group):
        is_strip, lanes = place(group)
        pieces, sources = (side, side_refs) if is_strip else (own, own_refs)
        blocks = [
            kept(ref[channel, at : at + rows, lanes], *sides)
            for ref, at, rows, sides in rows_of(pieces, sources, first, HALF)
        ]
        return blocks[0] if len(blocks) == 1 else jnp.concatenate(blocks, axis=0)

    def emit(channel, first, group, value):
        is_strip, lanes = place(group)
        extra = (carried_side, strip_refs) if is_strip else (carried_own, sum_refs)
        which = 1 if is_strip else 0
        for n, (start, count) in enumerate(outs):
            lo, hi = max(first, start), min(first + HALF, start + count)
            if lo >= hi:
                continue
            cuts = sorted({lo, hi} | {c for at, rows in extra[0] for c in (at, at + rows) if lo < c < hi})
            for a, b in zip(cuts, cuts[1:]):
                part = value[a - first : b - first]
                for (at, rows), ref in zip(*extra):
                    if at <= a and b <= at + rows:
                        part = part + ref[channel, a - at : b - at, lanes]
                out_refs[2 * n + which][channel, a - start : b - start, lanes] = part

    def store_split(pair, rows, lanes, value):
        high, low = split(value)
        pair[0][rows, lanes] = high
        pair[1][rows, lanes] = low

    lo, hi = slice(0, HALF), slice(HALF, WIN)
    tw_c, tw_s = tw_ref[0], tw_ref[1]
    for cb in range(2):
        in_col = in_first[cb]
        first_group, second_group = groups[cb]
        field = []
        for rb in range(2):
            value = []
            for channel in range(2):
                at = rb * HALF
                picked = jnp.where(in_col, load(channel, at, first_group), load(channel, at, second_group))
                if rb == 0:
                    other = jnp.where(in_col, load(channel, WIN, first_group), load(channel, WIN, second_group))
                    picked = jnp.where(in_row, picked, other)
                value.append(picked)
            box = (slice(rb * HALF, (rb + 1) * HALF), slice(cb * LANE, (cb + 1) * LANE))
            p_re = probes_ref[(number, 0) + box]
            p_im = probes_ref[(number, 1) + box]
            field.append((p_re * value[0] - p_im * value[1], p_re * value[1] + p_im * value[0]))
        (re0, im0), (re1, im1) = field
        store_split(g_in[cb], lo, lo, re0 + re1)
        store_split(g_in[cb], hi, lo, im0 + im1)
        d_re = re0 - re1
        d_im = im0 - im1
        store_split(g_in[cb], lo, hi, d_re * tw_c + d_im * tw_s)
        store_split(g_in[cb], hi, hi, d_im * tw_c - d_re * tw_s)
        high, low = g_in[cb][0][...], g_in[cb][1][...]
        wide[cb][...] = mul(first_h[...], high) + mul(first_h[...], low) + mul(first_l[...], high)

    for p in range(2):
        tl_c, tl_s = tw_ref[2], tw_ref[3]
        cols = slice(p * HALF, (p + 1) * HALF)
        re0, re1 = wide[0][lo, cols], wide[1][lo, cols]
        im0, im1 = wide[0][hi, cols], wide[1][hi, cols]
        store_split(h_in[p], lo, lo, re0 + re1)
        store_split(h_in[p], lo, hi, im0 + im1)
        d_re = re0 - re1
        d_im = im0 - im1
        store_split(h_in[p], hi, lo, d_re * tl_c + d_im * tl_s)
        store_split(h_in[p], hi, hi, d_im * tl_c - d_re * tl_s)
        high, low = h_in[p][0][...], h_in[p][1][...]
        tall[p][...] = mul(high, second_h[...]) + mul(low, second_h[...]) + mul(high, second_l[...])

    for p in range(2):
        for q, rows in enumerate((lo, hi)):
            re, im = tall[p][rows, lo], tall[p][rows, hi]
            power = jnp.maximum(re * re + im * im, amp_floor * amp_floor)
            at = q * WIN + p * HALF
            keeping = 1.0 - amps_ref[number, at : at + HALF, :] * lax.rsqrt(power)
            store_split(m_in[p], rows, lo, re * keeping)
            store_split(m_in[p], rows, hi, im * keeping)
        high, low = m_in[p][0][...], m_in[p][1][...]
        tall_back[p][...] = mul(high, first_h[...]) + mul(low, first_h[...]) + mul(high, first_l[...])

    for p in range(2):
        tl_c, tl_s = tw_ref[2], tw_ref[3]
        u_re, u_im = tall_back[p][lo, lo], tall_back[p][lo, hi]
        v_re, v_im = tall_back[p][hi, lo], tall_back[p][hi, hi]
        w_re = v_re * tl_c - v_im * tl_s
        w_im = v_im * tl_c + v_re * tl_s
        store_split(g_out[p], lo, lo, u_re + w_re)
        store_split(g_out[p], lo, hi, u_re - w_re)
        store_split(g_out[p], hi, lo, u_im + w_im)
        store_split(g_out[p], hi, hi, u_im - w_im)
        high, low = g_out[p][0][...], g_out[p][1][...]
        wide_back[p][...] = mul(second_h[...], high) + mul(second_h[...], low) + mul(second_l[...], high)

    for cb in range(2):
        in_col = in_first[cb]
        first_group, second_group = groups[cb]
        cols = slice(cb * LANE, (cb + 1) * LANE)
        u_re, u_im = wide_back[0][lo, cols], wide_back[0][hi, cols]
        v_re, v_im = wide_back[1][lo, cols], wide_back[1][hi, cols]
        w_re = v_re * tw_c - v_im * tw_s
        w_im = v_im * tw_c + v_re * tw_s
        for rb in range(2):
            b_re = u_re + w_re if rb == 0 else u_re - w_re
            b_im = u_im + w_im if rb == 0 else u_im - w_im
            box = (slice(rb * HALF, (rb + 1) * HALF), cols)
            p_re = probes_ref[(number, 0) + box]
            p_im = probes_ref[(number, 1) + box]
            grads = (p_re * b_re + p_im * b_im, p_re * b_im - p_im * b_re)
            for channel in range(2):
                grad = grads[channel]
                targets = [(rb * HALF, grad)]
                if rb == 0:
                    targets = [(0, jnp.where(in_row, grad, 0.0)), (WIN, jnp.where(in_row, 0.0, grad))]
                for at, piece in targets:
                    emit(channel, at, first_group, jnp.where(in_col, piece, 0.0))
                    emit(channel, at, second_group, jnp.where(in_col, 0.0, piece))


def window(i, near, consts, side, own, carried_own, carried_side, outs):
    border = () if near else ("beside",)
    own_width = 3 * LANE
    shapes = []
    for _, rows in outs:
        shapes += [jax.ShapeDtypeStruct((2, rows, width), F32) for width in (own_width, LANE)]
    operands = [piece[0] for piece in list(side) + list(own) + list(carried_own) + list(carried_side)]
    kernel = functools.partial(
        window_kernel,
        i,
        near,
        tuple((p[1], p[2], p[3:] + border) for p in side),
        tuple((p[1], p[2], p[3:]) for p in own),
        tuple((at, array.shape[1]) for array, at in carried_own),
        tuple((at, array.shape[1]) for array, at in carried_side),
        outs,
    )
    return pl.pallas_call(
        kernel,
        out_shape=tuple(shapes),
        in_specs=[pl.BlockSpec(memory_space=pltpu.SMEM)] + vmem(4 + len(operands)),
        out_specs=tuple(vmem(len(shapes))),
        scratch_shapes=[pltpu.VMEM((WIN, WIN), BF16)] * 16 + [pltpu.VMEM((WIN, WIN), F32)] * 8,
        cost_estimate=COST,
        compiler_params=pltpu.CompilerParams(vmem_limit_bytes=VMEM_LIMIT),
    )(*consts, *operands)


def variation_kernel(near, own, far, *refs):
    reg = refs[-1]
    out_ref = refs[-2]
    near_refs, refs = refs[: len(near)], refs[len(near) :]
    own_refs, far_refs = refs[: len(own)], refs[len(own) : len(own) + len(far)]
    even = even_column()

    def block(pieces, sources, at, channel):
        first, rows, sides = pieces[at]
        return kept(sources[at][channel, first : first + rows, :], *sides)

    row = 0
    for n, (_, rows, _) in enumerate(own):
        for channel in range(2):
            span = slice(row, row + rows)
            one = block(near, near_refs, n, channel)
            other = block(far, far_refs, n, channel)
            reg[channel, span, LANE : 4 * LANE] = block(own, own_refs, n, channel)
            reg[channel, span, :LANE] = jnp.where(even, other, one)
            reg[channel, span, 4 * LANE :] = jnp.where(even, one, other)
        row += rows

    def chunk(step, _):
        base = pl.multiple_of(step * 32, 8)
        flows = []
        power = tv_smooth
        for channel in range(2):
            block = reg[channel, pl.ds(base, 48), :]
            down = pltpu.roll(block, 47, 0) - block
            right = pltpu.roll(block, 5 * LANE - 1, 1) - block
            power = power + down * down + right * right
            flows.append((down, right))
        inverse = lax.rsqrt(power)
        for channel in range(2):
            down, right = flows[channel]
            down = down * inverse
            right = right * inverse
            change = pltpu.roll(down, 1, 0) - down + pltpu.roll(right, 1, 1) - right
            out_ref[channel, pl.ds(base, 32), :] = tv_weight * change[8:40, LANE : 4 * LANE]
        return 0

    lax.fori_loop(0, 6, chunk, 0)


def variation(near, own, far):
    parts = (near, own, far)
    plan = [
        tuple((p[1], p[2], p[3:] + border) for p in part) for part, border in zip(parts, ((), (), ("beside",)))
    ]
    operands = [piece[0] for part in parts for piece in part]
    return pl.pallas_call(
        functools.partial(variation_kernel, *plan),
        out_shape=jax.ShapeDtypeStruct((2, 192, 3 * LANE), F32),
        in_specs=vmem(len(operands)),
        out_specs=pl.BlockSpec(memory_space=pltpu.VMEM),
        scratch_shapes=[pltpu.VMEM((2, 208, 5 * LANE), F32)],
        cost_estimate=COST,
        compiler_params=pltpu.CompilerParams(vmem_limit_bytes=VMEM_LIMIT),
        name="variation",
    )(*operands)


def totals_kernel(outs, extras, own_ref, near_ref, far_ref, *refs):
    added, out_refs = refs[: len(extras)], refs[len(extras) :]
    even = even_column()
    for (first, rows), out in zip(outs, out_refs):
        cuts = {first, first + rows}
        for at, count, _ in extras:
            cuts |= {c for c in (at, at + count) if first < c < first + rows}
        cuts = sorted(cuts)
        for a, b in zip(cuts, cuts[1:]):
            for channel in range(2):
                value = own_ref[channel, a:b, :]
                for (at, count, source), ref in zip(extras, added):
                    if at <= a and b <= at + count:
                        value = value + ref[channel, source + a - at : source + b - at, :]
                to = slice(a - first, b - first)
                one = near_ref[channel, a:b, :]
                other = kept(far_ref[channel, a:b, :], "beside")
                out[channel, to, :LANE] = value[:, :LANE] + jnp.where(even, other, one)
                out[channel, to, LANE : 2 * LANE] = value[:, LANE : 2 * LANE]
                out[channel, to, 2 * LANE :] = value[:, 2 * LANE :] + jnp.where(even, one, other)


def totals(own, near, far, outs, extras):
    plan = tuple((at, rows, source) for _, source, at, rows in extras)
    return pl.pallas_call(
        functools.partial(totals_kernel, outs, plan),
        out_shape=tuple(jax.ShapeDtypeStruct((2, rows, own.shape[2]), F32) for _, rows in outs),
        in_specs=vmem(3 + len(extras)),
        out_specs=tuple(vmem(len(outs))),
        cost_estimate=COST,
        compiler_params=pltpu.CompilerParams(vmem_limit_bytes=VMEM_LIMIT),
        name="totals",
    )(own, near, far, *[extra[0] for extra in extras])


def update_kernel(pieces, side, *refs):
    new, near, far = refs[-3:]
    even = even_column()
    ins = refs[:-3]
    row = 0
    for which, first, rows, grads, masked in pieces:
        for channel in range(2):
            total = None
            for grad, at in grads:
                term = ins[grad][channel, at : at + rows, :]
                if grad == len(ins) - 1:
                    term = kept(term, side)
                total = term if total is None else total + term
            value = ins[which][channel, first : first + rows, :] - step_size * total
            if masked:
                value = kept(value, side)
            new[channel, row : row + rows, :] = value
            near[channel, row : row + rows, :] = jnp.where(even, value[:, 2 * LANE :], value[:, :LANE])
            far[channel, row : row + rows, :] = jnp.where(even, value[:, :LANE], value[:, 2 * LANE :])
        row += rows


def update(operands, pieces, side):
    rows = sum(piece[2] for piece in pieces)
    shape = [jax.ShapeDtypeStruct((2, rows, width), F32) for width in (3 * LANE, LANE, LANE)]
    return pl.pallas_call(
        functools.partial(update_kernel, pieces, side),
        out_shape=tuple(shape),
        in_specs=vmem(len(operands)),
        out_specs=tuple(vmem(3)),
        cost_estimate=COST,
        compiler_params=pltpu.CompilerParams(vmem_limit_bytes=VMEM_LIMIT),
        name="update",
    )(*operands)


def finish_kernel(top_ref, bottom_ref, mid_ref, low_ref, above_ref, below_ref, out_ref):
    for channel in range(2):
        above = mid_ref[channel, :MARGIN, :] + kept(above_ref[channel], "above")
        out_ref[channel, :MARGIN, :] = top_ref[channel, MARGIN:, :] - step_size * above
        out_ref[channel, MARGIN:288, :] = bottom_ref[channel, :192, :] - step_size * mid_ref[channel, MARGIN:, :]
        below = low_ref[channel] + kept(below_ref[channel], "below")
        out_ref[channel, 288:, :] = bottom_ref[channel, 192:288, :] - step_size * below


def finish(*operands):
    return pl.pallas_call(
        finish_kernel,
        out_shape=jax.ShapeDtypeStruct((2, 3 * LANE, 3 * LANE), F32),
        in_specs=vmem(len(operands)),
        out_specs=pl.BlockSpec(memory_space=pltpu.VMEM),
        cost_estimate=COST,
        compiler_params=pltpu.CompilerParams(vmem_limit_bytes=VMEM_LIMIT),
        name="finish",
    )(*operands)


def moved(block, axis, distance):
    count = lax.axis_size(axis)
    return lax.ppermute(block, axis, [(n, (n + distance) % count) for n in range(count)])


def to_near(block):
    rows, cols = lax.axis_size("row"), lax.axis_size("col")
    return lax.ppermute(block, ("row", "col"), [(r * cols + c, r * cols + (c ^ 1)) for r in range(rows) for c in range(cols)])


def to_far(block):
    rows, cols = lax.axis_size("row"), lax.axis_size("col")
    route = []
    for r in range(rows):
        for c in range(cols):
            other = c - 1 if c % 2 == 0 else c + 1
            route.append((r * cols + c, r * cols + other % cols))
    return lax.ppermute(block, ("row", "col"), route)


def edges(block):
    width = block.shape[2]
    low, high = block[:, :, :LANE], block[:, :, width - LANE :]
    even = even_column()
    return jnp.where(even, high, low), jnp.where(even, low, high)


def on_device(table, twiddle, order, object_field, probe, amplitudes, offsets):
    tile = object_field.shape[1]
    last = tile - MARGIN
    band = 2 * MARGIN
    obj = object_field
    after = lax.optimization_barrier

    top = moved(obj[:, last:, :], "row", 1)
    near_strip, far_strip = edges(obj)
    far, near = to_far(far_strip), to_near(near_strip)
    up_rows, top = after((obj[:, :MARGIN, :], top))
    bottom = moved(up_rows, "row", -1)
    probes, amps = prepare(offsets, probe, amplitudes, order)
    consts = (offsets, table, twiddle, probes, amps)

    near_strip, far_strip = edges(top)
    top_b, top_a = to_far(far_strip), to_near(near_strip)
    own = [(top, 0, MARGIN, "above"), (obj, 0, last)]
    halves = ((0, band), (band, band))
    lo_o, lo_b, mid_o, mid_b = window(
        0, False, consts, [(top_b, 0, MARGIN, "above"), (far, 0, last)], own, [], [], halves
    )
    in_b = to_far(lo_b)
    lo_o, lo_a, mid_o, mid_a = window(
        0, True, consts, [(top_a, 0, MARGIN, "above"), (near, 0, last)], own, [(lo_o, 0), (mid_o, band)], [], halves
    )
    in_a = to_near(lo_a)
    bottom, lo_a = after((bottom, lo_a))
    near_strip, far_strip = edges(bottom)
    bot_b, bot_a = to_far(far_strip), to_near(near_strip)
    tv_top = variation(
        [(top_a, 88, 8, "above"), (near, 0, 200)],
        [(top, 88, 8, "above"), (obj, 0, 200)],
        [(top_b, 88, 8, "above"), (far, 0, 200)],
    )
    (top_sum,) = totals(lo_o, in_a, in_b, ((0, band),), [(tv_top, 0, MARGIN, MARGIN)])
    from_below = moved(top_sum, "row", -1)

    mid_o, top_sum = after((mid_o, top_sum))
    own = [(obj, MARGIN, last), (bottom, 0, MARGIN, "below")]
    whole = ((0, tile),)
    hi_o, hi_b = window(
        1, False, consts, [(far, MARGIN, last), (bot_b, 0, MARGIN, "below")], own, [(mid_o, 0)], [(mid_b, 0)], whole
    )
    in_b = to_far(hi_b)
    hi_o, hi_a = window(
        1, True, consts, [(near, MARGIN, last), (bot_a, 0, MARGIN, "below")], own, [(hi_o, 0)], [(mid_a, 0)], whole,
    )
    in_a = to_near(hi_a)
    tv_bottom = variation(
        [(near, 184, 200), (bot_a, 0, 8, "below")],
        [(obj, 184, 200), (bottom, 0, 8, "below")],
        [(far, 184, 200), (bot_b, 0, 8, "below")],
    )
    mid_sum, bot_sum = totals(
        hi_o, in_a, in_b, halves, [(tv_top, MARGIN, 0, MARGIN), (tv_bottom, 0, MARGIN, band)]
    )
    from_above = moved(bot_sum, "row", 1)

    low, near_strip, far_strip = update(
        (obj, bottom, mid_sum, bot_sum, from_below),
        (
            (0, MARGIN, band, ((2, 0),), False),
            (0, last, MARGIN, ((3, 0), (4, 0)), False),
            (1, 0, MARGIN, ((3, MARGIN), (4, MARGIN)), True),
        ),
        "below",
    )
    low_b, low_a = to_far(far_strip), to_near(near_strip)
    own = [(low, 0, tile)]
    mid_o, mid_a, hi_o, hi_a = window(1, True, consts, [(low_a, 0, tile)], own, [], [], halves)
    in_a = to_near(hi_a)
    mid_o, mid_b, hi_o, hi_b = window(
        1, False, consts, [(low_b, 0, tile)], own, [(mid_o, 0), (hi_o, band)], [], halves
    )
    in_b = to_far(hi_b)
    tv_bottom = variation([(low_a, 88, 208)], [(low, 88, 208)], [(low_b, 88, 208)])
    low_sum, over = totals(hi_o, in_a, in_b, ((0, MARGIN), (MARGIN, MARGIN)), [(tv_bottom, MARGIN, 0, MARGIN)])
    last_above = moved(over, "row", 1)

    up, near_strip, far_strip = update(
        (top, obj, top_sum, from_above),
        (
            (0, 0, MARGIN, ((2, 0), (3, 0)), True),
            (1, 0, MARGIN, ((2, MARGIN), (3, MARGIN)), False),
        ),
        "above",
    )
    up_b, up_a = to_far(far_strip), to_near(near_strip)
    mid_o, over = after((mid_o, over))
    own = [(up, 0, band), (low, 0, band)]
    cut = ((0, MARGIN), (MARGIN, last))
    over_o, over_a, lo_o, lo_a = window(
        0, True, consts, [(up_a, 0, band), (low_a, 0, band)], own, [(mid_o, band)], [(mid_a, band)], cut,
    )
    over_a, in_a = to_near(over_a), to_near(lo_a)
    over_o, over_b, lo_o, lo_b = window(
        0, False, consts, [(up_b, 0, band), (low_b, 0, band)], own, [(over_o, 0), (lo_o, MARGIN)], [(mid_b, band)], cut
    )
    over_b = to_far(over_b)
    (over,) = totals(over_o, over_a, over_b, ((0, MARGIN),), [])
    last_below = moved(over, "row", -1)
    in_b = to_far(lo_b)
    tv_top = variation(
        [(up_a, 88, 104), (low_a, 0, 104)], [(up, 88, 104), (low, 0, 104)], [(up_b, 88, 104), (low_b, 0, 104)]
    )
    (mid_sum,) = totals(lo_o, in_a, in_b, ((0, last),), [(tv_top, 0, 0, band), (tv_bottom, 0, band, MARGIN)])
    return finish(up, low, mid_sum, low_sum, last_above, last_below)


def solution(mesh):
    table, twiddle, order = tables()
    body = jax.shard_map(
        on_device,
        mesh=mesh,
        in_specs=(P(), P(), P(), P(None, "row", "col"), P(), P("row", "col"), P("row", "col", None)),
        out_specs=P(None, "row", "col"),
        check_vma=False,
    )

    def step(object_field, probe, amplitudes, offsets):
        return body(table, twiddle, order, object_field, probe, amplitudes, offsets)

    return step
```

```python
import functools
import math

import jax
import jax.numpy as jnp
import numpy as np
from jax import lax
from jax.experimental import pallas as pl
from jax.experimental.pallas import tpu as pltpu
from jax.sharding import PartitionSpec as P


WIN = 256
HALF = 128
MARGIN = 96
LANE = 128
COST = pl.CostEstimate(flops=100_000, bytes_accessed=100_000, transcendentals=0)
VMEM_LIMIT = 24 * 1024 * 1024

step_size = 0.3
tv_weight = 0.2
tv_smooth = 0.1
amp_floor = 0.5

F32 = jnp.float32
BF16 = jnp.bfloat16


def tables():
    counter = np.arange(HALF)
    angle = (counter[:, None] * counter[None, :] % HALF) * (2.0 * math.pi / HALF)
    cosine = np.cos(angle) / math.sqrt(WIN)
    sine = np.sin(angle) / math.sqrt(WIN)
    first = np.block([[cosine, sine], [-sine, cosine]])
    second = np.block([[cosine, -sine], [sine, cosine]])
    parts = []
    for table in (first, second):
        table = table.astype(np.float32)
        high = table.astype(jnp.bfloat16)
        low = (table - high.astype(np.float32)).astype(jnp.bfloat16)
        parts += [high, low]
    turn = counter * (2.0 * math.pi / WIN)
    rows = np.stack([np.cos(turn), np.sin(turn)])
    by_row = np.broadcast_to(rows[:, :, None], (2, HALF, HALF))
    by_lane = np.broadcast_to(rows[:, None, :], (2, HALF, HALF))
    twiddle = np.concatenate([by_row, by_lane]).astype(np.float32)
    order = np.zeros((WIN, WIN), np.float32)
    for parity in range(2):
        order[2 * counter + parity, parity * HALF + counter] = 1.0
    return np.stack(parts), twiddle, order.astype(jnp.bfloat16)


def split(value):
    high = value.astype(BF16)
    return high, (value - high.astype(F32)).astype(BF16)


def has(side):
    if side == "above":
        return lax.axis_index("row") > 0
    if side == "below":
        return lax.axis_index("row") < lax.axis_size("row") - 1
    return (lax.axis_index("col") > 0) & (lax.axis_index("col") < lax.axis_size("col") - 1)


def even_column():
    return lax.axis_index("col") % 2 == 0


def kept(value, *sides):
    for side in sides:
        value = jnp.where(has(side), value, 0.0)
    return value


def mul(left, right):
    return jnp.dot(left, right, preferred_element_type=F32)


def vmem(count):
    return [pl.BlockSpec(memory_space=pltpu.VMEM)] * count


def prepare_kernel(off_ref, probe_ref, amp_ref, order_ref, probes_ref, amps_ref, parts_ref):
    order = order_ref[...]
    for i in range(2):
        for j in range(2):
            row = off_ref[i, j, 0]
            col = (off_ref[i, j, 1] + (32 if j == 0 else 224)) % WIN
            for channel in range(2):
                turned = pltpu.roll(probe_ref[channel], row, 0)
                probes_ref[2 * i + j, channel] = pltpu.roll(turned, col, 1)
            amp = amp_ref[i * WIN : (i + 1) * WIN, j * WIN : (j + 1) * WIN]
            high, rest = split(amp)
            middle, _ = split(amp - high.astype(F32) - rest.astype(F32))
            sorted_lanes = mul(high, order) + mul(rest, order) + mul(middle, order)
            for q in range(2):
                parts_ref[...] = sorted_lanes[:, q * HALF : (q + 1) * HALF]
                for p in range(2):
                    at = q * WIN + p * HALF
                    amps_ref[2 * i + j, at : at + HALF, :] = parts_ref[pl.ds(p, HALF, stride=2), :]


def prepare(offsets, probe, amplitudes, order):
    return pl.pallas_call(
        prepare_kernel,
        out_shape=(
            jax.ShapeDtypeStruct((4, 2, WIN, WIN), F32),
            jax.ShapeDtypeStruct((4, 2 * WIN, HALF), F32),
        ),
        in_specs=[pl.BlockSpec(memory_space=pltpu.SMEM)] + vmem(3),
        out_specs=tuple(vmem(2)),
        scratch_shapes=[pltpu.VMEM((WIN, HALF), F32)],
        cost_estimate=COST,
        compiler_params=pltpu.CompilerParams(vmem_limit_bytes=VMEM_LIMIT),
        name="prepare",
    )(offsets, probe, amplitudes, order)


def rows_of(pieces, refs, first, rows):
    found, at = [], 0
    for ref, (start, count, sides) in zip(refs, pieces):
        lo, hi = max(first, at), min(first + rows, at + count)
        if lo < hi:
            found.append((ref, start + lo - at, hi - lo, sides))
        at += count
    return found


def window_kernel(i, near, side, own, carried_own, carried_side, outs, *refs):
    off_ref, tab_ref, tw_ref, probes_ref, amps_ref = refs[:5]
    refs = refs[5:]
    side_refs, refs = refs[: len(side)], refs[len(side) :]
    own_refs, refs = refs[: len(own)], refs[len(own) :]
    sum_refs, refs = refs[: len(carried_own)], refs[len(carried_own) :]
    strip_refs, refs = refs[: len(carried_side)], refs[len(carried_side) :]
    out_refs, refs = refs[: 2 * len(outs)], refs[2 * len(outs) :]
    halves = [refs[n : n + 2] for n in range(0, 16, 2)]
    g_in, h_in, m_in, g_out = halves[0:2], halves[2:4], halves[4:6], halves[6:8]
    wide, tall, tall_back, wide_back = refs[16:18], refs[18:20], refs[20:22], refs[22:24]

    to_right = even_column() if near else jnp.logical_not(even_column())
    j = jnp.where(to_right, 1, 0)
    number = 2 * i + j
    row_start = off_ref[i, j, 0]
    col_start = off_ref[i, j, 1]
    row_iota = lax.broadcasted_iota(jnp.int32, (HALF, HALF), 0)
    lane_iota = lax.broadcasted_iota(jnp.int32, (HALF, HALF), 1)
    in_row = row_iota >= row_start
    sign = jnp.where(to_right, -1, 1)
    in_first = (
        sign * lane_iota >= jnp.where(to_right, 33 - col_start, 32 + col_start),
        lane_iota >= jnp.where(to_right, 96 + col_start, col_start - 96),
    )
    first_h, first_l, second_h, second_l = (tab_ref.at[n] for n in range(4))
    groups = (("strip", 1), (0, 2))

    def place(group):
        if group == "strip":
            return True, slice(0, LANE)
        return False, slice(group * LANE, (group + 1) * LANE)

    def load(channel, first, group):
        is_strip, lanes = place(group)
        pieces, sources = (side, side_refs) if is_strip else (own, own_refs)
        blocks = [
            kept(ref[channel, at : at + rows, lanes], *sides)
            for ref, at, rows, sides in rows_of(pieces, sources, first, HALF)
        ]
        return blocks[0] if len(blocks) == 1 else jnp.concatenate(blocks, axis=0)

    def emit(channel, first, group, value):
        is_strip, lanes = place(group)
        extra = (carried_side, strip_refs) if is_strip else (carried_own, sum_refs)
        which = 1 if is_strip else 0
        for n, (start, count) in enumerate(outs):
            lo, hi = max(first, start), min(first + HALF, start + count)
            if lo >= hi:
                continue
            cuts = sorted({lo, hi} | {c for at, rows in extra[0] for c in (at, at + rows) if lo < c < hi})
            for a, b in zip(cuts, cuts[1:]):
                part = value[a - first : b - first]
                for (at, rows), ref in zip(*extra):
                    if at <= a and b <= at + rows:
                        part = part + ref[channel, a - at : b - at, lanes]
                out_refs[2 * n + which][channel, a - start : b - start, lanes] = part

    def store_split(pair, rows, lanes, value):
        high, low = split(value)
        pair[0][rows, lanes] = high
        pair[1][rows, lanes] = low

    lo, hi = slice(0, HALF), slice(HALF, WIN)
    tw_c, tw_s = tw_ref[0], tw_ref[1]
    for cb in range(2):
        in_col = in_first[cb]
        first_group, second_group = groups[cb]
        field = []
        for rb in range(2):
            value = []
            for channel in range(2):
                at = rb * HALF
                picked = jnp.where(in_col, load(channel, at, first_group), load(channel, at, second_group))
                if rb == 0:
                    other = jnp.where(in_col, load(channel, WIN, first_group), load(channel, WIN, second_group))
                    picked = jnp.where(in_row, picked, other)
                value.append(picked)
            box = (slice(rb * HALF, (rb + 1) * HALF), slice(cb * LANE, (cb + 1) * LANE))
            p_re = probes_ref[(number, 0) + box]
            p_im = probes_ref[(number, 1) + box]
            field.append((p_re * value[0] - p_im * value[1], p_re * value[1] + p_im * value[0]))
        (re0, im0), (re1, im1) = field
        store_split(g_in[cb], lo, lo, re0 + re1)
        store_split(g_in[cb], hi, lo, im0 + im1)
        d_re = re0 - re1
        d_im = im0 - im1
        store_split(g_in[cb], lo, hi, d_re * tw_c + d_im * tw_s)
        store_split(g_in[cb], hi, hi, d_im * tw_c - d_re * tw_s)
        high, low = g_in[cb][0][...], g_in[cb][1][...]
        wide[cb][...] = mul(first_h[...], high) + mul(first_h[...], low) + mul(first_l[...], high)

    for p in range(2):
        tl_c, tl_s = tw_ref[2], tw_ref[3]
        cols = slice(p * HALF, (p + 1) * HALF)
        re0, re1 = wide[0][lo, cols], wide[1][lo, cols]
        im0, im1 = wide[0][hi, cols], wide[1][hi, cols]
        store_split(h_in[p], lo, lo, re0 + re1)
        store_split(h_in[p], lo, hi, im0 + im1)
        d_re = re0 - re1
        d_im = im0 - im1
        store_split(h_in[p], hi, lo, d_re * tl_c + d_im * tl_s)
        store_split(h_in[p], hi, hi, d_im * tl_c - d_re * tl_s)
        high, low = h_in[p][0][...], h_in[p][1][...]
        tall[p][...] = mul(high, second_h[...]) + mul(low, second_h[...]) + mul(high, second_l[...])

    for p in range(2):
        for q, rows in enumerate((lo, hi)):
            re, im = tall[p][rows, lo], tall[p][rows, hi]
            power = jnp.maximum(re * re + im * im, amp_floor * amp_floor)
            at = q * WIN + p * HALF
            keeping = 1.0 - amps_ref[number, at : at + HALF, :] * lax.rsqrt(power)
            store_split(m_in[p], rows, lo, re * keeping)
            store_split(m_in[p], rows, hi, im * keeping)
        high, low = m_in[p][0][...], m_in[p][1][...]
        tall_back[p][...] = mul(high, first_h[...]) + mul(low, first_h[...]) + mul(high, first_l[...])

    for p in range(2):
        tl_c, tl_s = tw_ref[2], tw_ref[3]
        u_re, u_im = tall_back[p][lo, lo], tall_back[p][lo, hi]
        v_re, v_im = tall_back[p][hi, lo], tall_back[p][hi, hi]
        w_re = v_re * tl_c - v_im * tl_s
        w_im = v_im * tl_c + v_re * tl_s
        store_split(g_out[p], lo, lo, u_re + w_re)
        store_split(g_out[p], lo, hi, u_re - w_re)
        store_split(g_out[p], hi, lo, u_im + w_im)
        store_split(g_out[p], hi, hi, u_im - w_im)
        high, low = g_out[p][0][...], g_out[p][1][...]
        wide_back[p][...] = mul(second_h[...], high) + mul(second_h[...], low) + mul(second_l[...], high)

    for cb in range(2):
        in_col = in_first[cb]
        first_group, second_group = groups[cb]
        cols = slice(cb * LANE, (cb + 1) * LANE)
        u_re, u_im = wide_back[0][lo, cols], wide_back[0][hi, cols]
        v_re, v_im = wide_back[1][lo, cols], wide_back[1][hi, cols]
        w_re = v_re * tw_c - v_im * tw_s
        w_im = v_im * tw_c + v_re * tw_s
        for rb in range(2):
            b_re = u_re + w_re if rb == 0 else u_re - w_re
            b_im = u_im + w_im if rb == 0 else u_im - w_im
            box = (slice(rb * HALF, (rb + 1) * HALF), cols)
            p_re = probes_ref[(number, 0) + box]
            p_im = probes_ref[(number, 1) + box]
            grads = (p_re * b_re + p_im * b_im, p_re * b_im - p_im * b_re)
            for channel in range(2):
                grad = grads[channel]
                targets = [(rb * HALF, grad)]
                if rb == 0:
                    targets = [(0, jnp.where(in_row, grad, 0.0)), (WIN, jnp.where(in_row, 0.0, grad))]
                for at, piece in targets:
                    emit(channel, at, first_group, jnp.where(in_col, piece, 0.0))
                    emit(channel, at, second_group, jnp.where(in_col, 0.0, piece))


def window(i, near, consts, side, own, carried_own, carried_side, outs):
    border = () if near else ("beside",)
    own_width = 3 * LANE
    shapes = []
    for _, rows in outs:
        shapes += [jax.ShapeDtypeStruct((2, rows, width), F32) for width in (own_width, LANE)]
    operands = [piece[0] for piece in list(side) + list(own) + list(carried_own) + list(carried_side)]
    kernel = functools.partial(
        window_kernel,
        i,
        near,
        tuple((p[1], p[2], p[3:] + border) for p in side),
        tuple((p[1], p[2], p[3:]) for p in own),
        tuple((at, array.shape[1]) for array, at in carried_own),
        tuple((at, array.shape[1]) for array, at in carried_side),
        outs,
    )
    return pl.pallas_call(
        kernel,
        out_shape=tuple(shapes),
        in_specs=[pl.BlockSpec(memory_space=pltpu.SMEM)] + vmem(4 + len(operands)),
        out_specs=tuple(vmem(len(shapes))),
        scratch_shapes=[pltpu.VMEM((WIN, WIN), BF16)] * 16 + [pltpu.VMEM((WIN, WIN), F32)] * 8,
        cost_estimate=COST,
        compiler_params=pltpu.CompilerParams(vmem_limit_bytes=VMEM_LIMIT),
    )(*consts, *operands)


def variation_kernel(near, own, far, *refs):
    reg = refs[-1]
    out_ref = refs[-2]
    near_refs, refs = refs[: len(near)], refs[len(near) :]
    own_refs, far_refs = refs[: len(own)], refs[len(own) : len(own) + len(far)]
    even = even_column()

    def block(pieces, sources, at, channel):
        first, rows, sides = pieces[at]
        return kept(sources[at][channel, first : first + rows, :], *sides)

    row = 0
    for n, (_, rows, _) in enumerate(own):
        for channel in range(2):
            span = slice(row, row + rows)
            one = block(near, near_refs, n, channel)
            other = block(far, far_refs, n, channel)
            reg[channel, span, LANE : 4 * LANE] = block(own, own_refs, n, channel)
            reg[channel, span, :LANE] = jnp.where(even, other, one)
            reg[channel, span, 4 * LANE :] = jnp.where(even, one, other)
        row += rows

    def chunk(step, _):
        base = pl.multiple_of(step * 32, 8)
        flows = []
        power = tv_smooth
        for channel in range(2):
            block = reg[channel, pl.ds(base, 48), :]
            down = pltpu.roll(block, 47, 0) - block
            right = pltpu.roll(block, 5 * LANE - 1, 1) - block
            power = power + down * down + right * right
            flows.append((down, right))
        inverse = lax.rsqrt(power)
        for channel in range(2):
            down, right = flows[channel]
            down = down * inverse
            right = right * inverse
            change = pltpu.roll(down, 1, 0) - down + pltpu.roll(right, 1, 1) - right
            out_ref[channel, pl.ds(base, 32), :] = tv_weight * change[8:40, LANE : 4 * LANE]
        return 0

    lax.fori_loop(0, 6, chunk, 0)


def variation(near, own, far):
    parts = (near, own, far)
    plan = [
        tuple((p[1], p[2], p[3:] + border) for p in part) for part, border in zip(parts, ((), (), ("beside",)))
    ]
    operands = [piece[0] for part in parts for piece in part]
    return pl.pallas_call(
        functools.partial(variation_kernel, *plan),
        out_shape=jax.ShapeDtypeStruct((2, 192, 3 * LANE), F32),
        in_specs=vmem(len(operands)),
        out_specs=pl.BlockSpec(memory_space=pltpu.VMEM),
        scratch_shapes=[pltpu.VMEM((2, 208, 5 * LANE), F32)],
        cost_estimate=COST,
        compiler_params=pltpu.CompilerParams(vmem_limit_bytes=VMEM_LIMIT),
        name="variation",
    )(*operands)


def totals_kernel(outs, extras, own_ref, near_ref, far_ref, *refs):
    added, out_refs = refs[: len(extras)], refs[len(extras) :]
    even = even_column()
    for (first, rows), out in zip(outs, out_refs):
        cuts = {first, first + rows}
        for at, count, _ in extras:
            cuts |= {c for c in (at, at + count) if first < c < first + rows}
        cuts = sorted(cuts)
        for a, b in zip(cuts, cuts[1:]):
            for channel in range(2):
                value = own_ref[channel, a:b, :]
                for (at, count, source), ref in zip(extras, added):
                    if at <= a and b <= at + count:
                        value = value + ref[channel, source + a - at : source + b - at, :]
                to = slice(a - first, b - first)
                one = near_ref[channel, a:b, :]
                other = kept(far_ref[channel, a:b, :], "beside")
                out[channel, to, :LANE] = value[:, :LANE] + jnp.where(even, other, one)
                out[channel, to, LANE : 2 * LANE] = value[:, LANE : 2 * LANE]
                out[channel, to, 2 * LANE :] = value[:, 2 * LANE :] + jnp.where(even, one, other)


def totals(own, near, far, outs, extras):
    plan = tuple((at, rows, source) for _, source, at, rows in extras)
    return pl.pallas_call(
        functools.partial(totals_kernel, outs, plan),
        out_shape=tuple(jax.ShapeDtypeStruct((2, rows, own.shape[2]), F32) for _, rows in outs),
        in_specs=vmem(3 + len(extras)),
        out_specs=tuple(vmem(len(outs))),
        cost_estimate=COST,
        compiler_params=pltpu.CompilerParams(vmem_limit_bytes=VMEM_LIMIT),
        name="totals",
    )(own, near, far, *[extra[0] for extra in extras])


def update_kernel(pieces, side, *refs):
    new, near, far = refs[-3:]
    even = even_column()
    ins = refs[:-3]
    row = 0
    for which, first, rows, grads, masked in pieces:
        for channel in range(2):
            total = None
            for grad, at in grads:
                term = ins[grad][channel, at : at + rows, :]
                if grad == len(ins) - 1:
                    term = kept(term, side)
                total = term if total is None else total + term
            value = ins[which][channel, first : first + rows, :] - step_size * total
            if masked:
                value = kept(value, side)
            new[channel, row : row + rows, :] = value
            near[channel, row : row + rows, :] = jnp.where(even, value[:, 2 * LANE :], value[:, :LANE])
            far[channel, row : row + rows, :] = jnp.where(even, value[:, :LANE], value[:, 2 * LANE :])
        row += rows


def update(operands, pieces, side):
    rows = sum(piece[2] for piece in pieces)
    shape = [jax.ShapeDtypeStruct((2, rows, width), F32) for width in (3 * LANE, LANE, LANE)]
    return pl.pallas_call(
        functools.partial(update_kernel, pieces, side),
        out_shape=tuple(shape),
        in_specs=vmem(len(operands)),
        out_specs=tuple(vmem(3)),
        cost_estimate=COST,
        compiler_params=pltpu.CompilerParams(vmem_limit_bytes=VMEM_LIMIT),
        name="update",
    )(*operands)


def finish_kernel(top_ref, bottom_ref, mid_ref, low_ref, above_ref, below_ref, out_ref):
    for channel in range(2):
        above = mid_ref[channel, :MARGIN, :] + kept(above_ref[channel], "above")
        out_ref[channel, :MARGIN, :] = top_ref[channel, MARGIN:, :] - step_size * above
        out_ref[channel, MARGIN:288, :] = bottom_ref[channel, :192, :] - step_size * mid_ref[channel, MARGIN:, :]
        below = low_ref[channel] + kept(below_ref[channel], "below")
        out_ref[channel, 288:, :] = bottom_ref[channel, 192:288, :] - step_size * below


def finish(*operands):
    return pl.pallas_call(
        finish_kernel,
        out_shape=jax.ShapeDtypeStruct((2, 3 * LANE, 3 * LANE), F32),
        in_specs=vmem(len(operands)),
        out_specs=pl.BlockSpec(memory_space=pltpu.VMEM),
        cost_estimate=COST,
        compiler_params=pltpu.CompilerParams(vmem_limit_bytes=VMEM_LIMIT),
        name="finish",
    )(*operands)


def moved(block, axis, distance):
    count = lax.axis_size(axis)
    return lax.ppermute(block, axis, [(n, (n + distance) % count) for n in range(count)])


def to_near(block):
    rows, cols = lax.axis_size("row"), lax.axis_size("col")
    return lax.ppermute(block, ("row", "col"), [(r * cols + c, r * cols + (c ^ 1)) for r in range(rows) for c in range(cols)])


def to_far(block, ends=True):
    rows, cols = lax.axis_size("row"), lax.axis_size("col")
    route = []
    for r in range(rows):
        for c in range(cols):
            other = c - 1 if c % 2 == 0 else c + 1
            if ends or 0 <= other < cols:
                route.append((r * cols + c, r * cols + other % cols))
    return lax.ppermute(block, ("row", "col"), route)


def edges(block):
    width = block.shape[2]
    low, high = block[:, :, :LANE], block[:, :, width - LANE :]
    even = even_column()
    return jnp.where(even, high, low), jnp.where(even, low, high)


def on_device(table, twiddle, order, object_field, probe, amplitudes, offsets):
    tile = object_field.shape[1]
    last = tile - MARGIN
    band = 2 * MARGIN
    obj = object_field
    after = lax.optimization_barrier

    top = moved(obj[:, last:, :], "row", 1)
    near_strip, far_strip = edges(obj)
    far, near = to_far(far_strip), to_near(near_strip)
    up_rows, top = after((obj[:, :MARGIN, :], top))
    bottom = moved(up_rows, "row", -1)
    probes, amps = prepare(offsets, probe, amplitudes, order)
    consts = (offsets, table, twiddle, probes, amps)

    near_strip, far_strip = edges(top)
    top_b, top_a = to_far(far_strip), to_near(near_strip)
    own = [(top, 0, MARGIN, "above"), (obj, 0, last)]
    halves = ((0, band), (band, band))
    lo_o, lo_a, mid_o, mid_a = window(
        0, True, consts, [(top_a, 0, MARGIN, "above"), (near, 0, last)], own, [], [], halves
    )
    in_a = to_near(lo_a)
    lo_o, lo_b, mid_o, mid_b = window(
        0, False, consts, [(top_b, 0, MARGIN, "above"), (far, 0, last)], own, [(lo_o, 0), (mid_o, band)], [], halves
    )
    in_b = to_far(lo_b)
    bottom, lo_b = after((bottom, lo_b))
    near_strip, far_strip = edges(bottom)
    bot_b, bot_a = to_far(far_strip), to_near(near_strip)
    tv_top = variation(
        [(top_a, 88, 8, "above"), (near, 0, 200)],
        [(top, 88, 8, "above"), (obj, 0, 200)],
        [(top_b, 88, 8, "above"), (far, 0, 200)],
    )
    (top_sum,) = totals(lo_o, in_a, in_b, ((0, band),), [(tv_top, 0, MARGIN, MARGIN)])
    from_below = moved(top_sum, "row", -1)

    mid_o, top_sum = after((mid_o, top_sum))
    own = [(obj, MARGIN, last), (bottom, 0, MARGIN, "below")]
    whole = ((0, tile),)
    hi_o, hi_b = window(
        1, False, consts, [(far, MARGIN, last), (bot_b, 0, MARGIN, "below")], own, [(mid_o, 0)], [(mid_b, 0)], whole
    )
    in_b = to_far(hi_b, ends=False)
    hi_o, hi_a = window(
        1, True, consts, [(near, MARGIN, last), (bot_a, 0, MARGIN, "below")], own, [(hi_o, 0)], [(mid_a, 0)], whole,
    )
    in_a = to_near(hi_a)
    tv_bottom = variation(
        [(near, 184, 200), (bot_a, 0, 8, "below")],
        [(obj, 184, 200), (bottom, 0, 8, "below")],
        [(far, 184, 200), (bot_b, 0, 8, "below")],
    )
    mid_sum, bot_sum = totals(
        hi_o, in_a, in_b, halves, [(tv_top, MARGIN, 0, MARGIN), (tv_bottom, 0, MARGIN, band)]
    )
    from_above = moved(bot_sum, "row", 1)

    low, near_strip, far_strip = update(
        (obj, bottom, mid_sum, bot_sum, from_below),
        (
            (0, MARGIN, band, ((2, 0),), False),
            (0, last, MARGIN, ((3, 0), (4, 0)), False),
            (1, 0, MARGIN, ((3, MARGIN), (4, MARGIN)), True),
        ),
        "below",
    )
    low_a, low_b = to_near(near_strip), to_far(far_strip, ends=False)
    own = [(low, 0, tile)]
    mid_o, mid_a, hi_o, hi_a = window(1, True, consts, [(low_a, 0, tile)], own, [], [], halves)
    in_a = to_near(hi_a)
    mid_o, mid_b, hi_o, hi_b = window(
        1, False, consts, [(low_b, 0, tile)], own, [(mid_o, 0), (hi_o, band)], [], halves
    )
    hi_in_a, hi_in_b = in_a, to_far(hi_b)
    tv_bottom = variation([(low_a, 88, 208)], [(low, 88, 208)], [(low_b, 88, 208)])
    up, near_strip, far_strip = update(
        (top, obj, top_sum, from_above),
        (
            (0, 0, MARGIN, ((2, 0), (3, 0)), True),
            (1, 0, MARGIN, ((2, MARGIN), (3, MARGIN)), False),
        ),
        "above",
    )
    up_b, up_a = to_far(far_strip), to_near(near_strip)
    own = [(up, 0, band), (low, 0, band)]
    cut = ((0, MARGIN), (MARGIN, last))
    over_o, over_a, lo_o, lo_a = window(
        0, True, consts, [(up_a, 0, band), (low_a, 0, band)], own, [(mid_o, band)], [(mid_a, band)], cut
    )
    over_a, in_a = to_near(over_a), to_near(lo_a)
    lo_o, hi_o = after((lo_o, hi_o))
    low_sum, over = totals(
        hi_o, hi_in_a, hi_in_b, ((0, MARGIN), (MARGIN, MARGIN)), [(tv_bottom, MARGIN, 0, MARGIN)]
    )
    lo_o, over = after((lo_o, over))
    last_above = moved(over, "row", 1)
    over_o, over_b, lo_o, lo_b = window(
        0, False, consts, [(up_b, 0, band), (low_b, 0, band)], own, [(over_o, 0), (lo_o, MARGIN)], [(mid_b, band)], cut,
    )
    over_b = to_far(over_b)
    (over,) = totals(over_o, over_a, over_b, ((0, MARGIN),), [])
    last_below = moved(over, "row", -1)
    in_b = to_far(lo_b)
    tv_top = variation(
        [(up_a, 88, 104), (low_a, 0, 104)], [(up, 88, 104), (low, 0, 104)], [(up_b, 88, 104), (low_b, 0, 104)]
    )
    (mid_sum,) = totals(lo_o, in_a, in_b, ((0, last),), [(tv_top, 0, 0, band), (tv_bottom, 0, band, MARGIN)])
    return finish(up, low, mid_sum, low_sum, last_above, last_below)


def solution(mesh):
    table, twiddle, order = tables()
    body = jax.shard_map(
        on_device,
        mesh=mesh,
        in_specs=(P(), P(), P(), P(None, "row", "col"), P(), P("row", "col"), P("row", "col", None)),
        out_specs=P(None, "row", "col"),
        check_vma=False,
    )

    def step(object_field, probe, amplitudes, offsets):
        return body(table, twiddle, order, object_field, probe, amplitudes, offsets)

    return step
```

```python
import functools
import math

import jax
import jax.numpy as jnp
import numpy as np
from jax import lax
from jax.experimental import pallas as pl
from jax.experimental.pallas import tpu as pltpu
from jax.sharding import PartitionSpec as P


WIN = 256
HALF = 128
MARGIN = 96
LANE = 128
COST = pl.CostEstimate(flops=100_000, bytes_accessed=100_000, transcendentals=0)
VMEM_LIMIT = 24 * 1024 * 1024

step_size = 0.3
tv_weight = 0.2
tv_smooth = 0.1
amp_floor = 0.5

F32 = jnp.float32
BF16 = jnp.bfloat16


def tables():
    counter = np.arange(HALF)
    angle = (counter[:, None] * counter[None, :] % HALF) * (2.0 * math.pi / HALF)
    cosine = np.cos(angle) / math.sqrt(WIN)
    sine = np.sin(angle) / math.sqrt(WIN)
    first = np.block([[cosine, sine], [-sine, cosine]])
    second = np.block([[cosine, -sine], [sine, cosine]])
    parts = []
    for table in (first, second):
        table = table.astype(np.float32)
        high = table.astype(jnp.bfloat16)
        low = (table - high.astype(np.float32)).astype(jnp.bfloat16)
        parts += [high, low]
    turn = counter * (2.0 * math.pi / WIN)
    rows = np.stack([np.cos(turn), np.sin(turn)])
    by_row = np.broadcast_to(rows[:, :, None], (2, HALF, HALF))
    by_lane = np.broadcast_to(rows[:, None, :], (2, HALF, HALF))
    twiddle = np.concatenate([by_row, by_lane]).astype(np.float32)
    order = np.zeros((WIN, WIN), np.float32)
    for parity in range(2):
        order[2 * counter + parity, parity * HALF + counter] = 1.0
    return np.stack(parts), twiddle, order.astype(jnp.bfloat16)


def split(value):
    high = value.astype(BF16)
    return high, (value - high.astype(F32)).astype(BF16)


def has(side):
    if side == "above":
        return lax.axis_index("row") > 0
    if side == "below":
        return lax.axis_index("row") < lax.axis_size("row") - 1
    return (lax.axis_index("col") > 0) & (lax.axis_index("col") < lax.axis_size("col") - 1)


def even_column():
    return lax.axis_index("col") % 2 == 0


def kept(value, *sides):
    for side in sides:
        value = jnp.where(has(side), value, 0.0)
    return value


def mul(left, right):
    return jnp.dot(left, right, preferred_element_type=F32)


def vmem(count):
    return [pl.BlockSpec(memory_space=pltpu.VMEM)] * count


def prepare_kernel(off_ref, probe_ref, amp_ref, order_ref, probes_ref, amps_ref, parts_ref):
    order = order_ref[...]
    for i in range(2):
        for j in range(2):
            row = off_ref[i, j, 0]
            col = (off_ref[i, j, 1] + (32 if j == 0 else 224)) % WIN
            for channel in range(2):
                turned = pltpu.roll(probe_ref[channel], row, 0)
                probes_ref[2 * i + j, channel] = pltpu.roll(turned, col, 1)
            amp = amp_ref[i * WIN : (i + 1) * WIN, j * WIN : (j + 1) * WIN]
            high, rest = split(amp)
            middle, _ = split(amp - high.astype(F32) - rest.astype(F32))
            sorted_lanes = mul(high, order) + mul(rest, order) + mul(middle, order)
            for q in range(2):
                parts_ref[...] = sorted_lanes[:, q * HALF : (q + 1) * HALF]
                for p in range(2):
                    at = q * WIN + p * HALF
                    amps_ref[2 * i + j, at : at + HALF, :] = parts_ref[pl.ds(p, HALF, stride=2), :]


def prepare(offsets, probe, amplitudes, order):
    return pl.pallas_call(
        prepare_kernel,
        out_shape=(
            jax.ShapeDtypeStruct((4, 2, WIN, WIN), F32),
            jax.ShapeDtypeStruct((4, 2 * WIN, HALF), F32),
        ),
        in_specs=[pl.BlockSpec(memory_space=pltpu.SMEM)] + vmem(3),
        out_specs=tuple(vmem(2)),
        scratch_shapes=[pltpu.VMEM((WIN, HALF), F32)],
        cost_estimate=COST,
        compiler_params=pltpu.CompilerParams(vmem_limit_bytes=VMEM_LIMIT),
        name="prepare",
    )(offsets, probe, amplitudes, order)


def rows_of(pieces, refs, first, rows):
    found, at = [], 0
    for ref, (start, count, sides) in zip(refs, pieces):
        lo, hi = max(first, at), min(first + rows, at + count)
        if lo < hi:
            found.append((ref, start + lo - at, hi - lo, sides))
        at += count
    return found


def window_kernel(i, near, side, own, carried_own, carried_side, outs, *refs):
    off_ref, tab_ref, tw_ref, probes_ref, amps_ref = refs[:5]
    refs = refs[5:]
    side_refs, refs = refs[: len(side)], refs[len(side) :]
    own_refs, refs = refs[: len(own)], refs[len(own) :]
    sum_refs, refs = refs[: len(carried_own)], refs[len(carried_own) :]
    strip_refs, refs = refs[: len(carried_side)], refs[len(carried_side) :]
    out_refs, refs = refs[: 2 * len(outs)], refs[2 * len(outs) :]
    halves = [refs[n : n + 2] for n in range(0, 16, 2)]
    g_in, h_in, m_in, g_out = halves[0:2], halves[2:4], halves[4:6], halves[6:8]
    wide, tall, tall_back, wide_back = refs[16:18], refs[18:20], refs[20:22], refs[22:24]

    to_right = even_column() if near else jnp.logical_not(even_column())
    j = jnp.where(to_right, 1, 0)
    number = 2 * i + j
    row_start = off_ref[i, j, 0]
    col_start = off_ref[i, j, 1]
    row_iota = lax.broadcasted_iota(jnp.int32, (HALF, HALF), 0)
    lane_iota = lax.broadcasted_iota(jnp.int32, (HALF, HALF), 1)
    in_row = row_iota >= row_start
    sign = jnp.where(to_right, -1, 1)
    in_first = (
        sign * lane_iota >= jnp.where(to_right, 33 - col_start, 32 + col_start),
        lane_iota >= jnp.where(to_right, 96 + col_start, col_start - 96),
    )
    first_h, first_l, second_h, second_l = (tab_ref.at[n] for n in range(4))
    groups = (("strip", 1), (0, 2))

    def place(group):
        if group == "strip":
            return True, slice(0, LANE)
        return False, slice(group * LANE, (group + 1) * LANE)

    def load(channel, first, group):
        is_strip, lanes = place(group)
        pieces, sources = (side, side_refs) if is_strip else (own, own_refs)
        blocks = [
            kept(ref[channel, at : at + rows, lanes], *sides)
            for ref, at, rows, sides in rows_of(pieces, sources, first, HALF)
        ]
        return blocks[0] if len(blocks) == 1 else jnp.concatenate(blocks, axis=0)

    def emit(channel, first, group, value):
        is_strip, lanes = place(group)
        extra = (carried_side, strip_refs) if is_strip else (carried_own, sum_refs)
        which = 1 if is_strip else 0
        for n, (start, count) in enumerate(outs):
            lo, hi = max(first, start), min(first + HALF, start + count)
            if lo >= hi:
                continue
            cuts = sorted({lo, hi} | {c for at, rows in extra[0] for c in (at, at + rows) if lo < c < hi})
            for a, b in zip(cuts, cuts[1:]):
                part = value[a - first : b - first]
                for (at, rows), ref in zip(*extra):
                    if at <= a and b <= at + rows:
                        part = part + ref[channel, a - at : b - at, lanes]
                out_refs[2 * n + which][channel, a - start : b - start, lanes] = part

    def store_split(pair, rows, lanes, value):
        high, low = split(value)
        pair[0][rows, lanes] = high
        pair[1][rows, lanes] = low

    lo, hi = slice(0, HALF), slice(HALF, WIN)
    tw_c, tw_s = tw_ref[0], tw_ref[1]
    for cb in range(2):
        in_col = in_first[cb]
        first_group, second_group = groups[cb]
        field = []
        for rb in range(2):
            value = []
            for channel in range(2):
                at = rb * HALF
                picked = jnp.where(in_col, load(channel, at, first_group), load(channel, at, second_group))
                if rb == 0:
                    other = jnp.where(in_col, load(channel, WIN, first_group), load(channel, WIN, second_group))
                    picked = jnp.where(in_row, picked, other)
                value.append(picked)
            box = (slice(rb * HALF, (rb + 1) * HALF), slice(cb * LANE, (cb + 1) * LANE))
            p_re = probes_ref[(number, 0) + box]
            p_im = probes_ref[(number, 1) + box]
            field.append((p_re * value[0] - p_im * value[1], p_re * value[1] + p_im * value[0]))
        (re0, im0), (re1, im1) = field
        store_split(g_in[cb], lo, lo, re0 + re1)
        store_split(g_in[cb], hi, lo, im0 + im1)
        d_re = re0 - re1
        d_im = im0 - im1
        store_split(g_in[cb], lo, hi, d_re * tw_c + d_im * tw_s)
        store_split(g_in[cb], hi, hi, d_im * tw_c - d_re * tw_s)
        high, low = g_in[cb][0][...], g_in[cb][1][...]
        wide[cb][...] = mul(first_h[...], high) + mul(first_h[...], low) + mul(first_l[...], high)

    for p in range(2):
        tl_c, tl_s = tw_ref[2], tw_ref[3]
        cols = slice(p * HALF, (p + 1) * HALF)
        re0, re1 = wide[0][lo, cols], wide[1][lo, cols]
        im0, im1 = wide[0][hi, cols], wide[1][hi, cols]
        store_split(h_in[p], lo, lo, re0 + re1)
        store_split(h_in[p], lo, hi, im0 + im1)
        d_re = re0 - re1
        d_im = im0 - im1
        store_split(h_in[p], hi, lo, d_re * tl_c + d_im * tl_s)
        store_split(h_in[p], hi, hi, d_im * tl_c - d_re * tl_s)
        high, low = h_in[p][0][...], h_in[p][1][...]
        tall[p][...] = mul(high, second_h[...]) + mul(low, second_h[...]) + mul(high, second_l[...])

    for p in range(2):
        for q, rows in enumerate((lo, hi)):
            re, im = tall[p][rows, lo], tall[p][rows, hi]
            power = jnp.maximum(re * re + im * im, amp_floor * amp_floor)
            at = q * WIN + p * HALF
            keeping = 1.0 - amps_ref[number, at : at + HALF, :] * lax.rsqrt(power)
            store_split(m_in[p], rows, lo, re * keeping)
            store_split(m_in[p], rows, hi, im * keeping)
        high, low = m_in[p][0][...], m_in[p][1][...]
        tall_back[p][...] = mul(high, first_h[...]) + mul(low, first_h[...]) + mul(high, first_l[...])

    for p in range(2):
        tl_c, tl_s = tw_ref[2], tw_ref[3]
        u_re, u_im = tall_back[p][lo, lo], tall_back[p][lo, hi]
        v_re, v_im = tall_back[p][hi, lo], tall_back[p][hi, hi]
        w_re = v_re * tl_c - v_im * tl_s
        w_im = v_im * tl_c + v_re * tl_s
        store_split(g_out[p], lo, lo, u_re + w_re)
        store_split(g_out[p], lo, hi, u_re - w_re)
        store_split(g_out[p], hi, lo, u_im + w_im)
        store_split(g_out[p], hi, hi, u_im - w_im)
        high, low = g_out[p][0][...], g_out[p][1][...]
        wide_back[p][...] = mul(second_h[...], high) + mul(second_h[...], low) + mul(second_l[...], high)

    for cb in range(2):
        in_col = in_first[cb]
        first_group, second_group = groups[cb]
        cols = slice(cb * LANE, (cb + 1) * LANE)
        u_re, u_im = wide_back[0][lo, cols], wide_back[0][hi, cols]
        v_re, v_im = wide_back[1][lo, cols], wide_back[1][hi, cols]
        w_re = v_re * tw_c - v_im * tw_s
        w_im = v_im * tw_c + v_re * tw_s
        for rb in range(2):
            b_re = u_re + w_re if rb == 0 else u_re - w_re
            b_im = u_im + w_im if rb == 0 else u_im - w_im
            box = (slice(rb * HALF, (rb + 1) * HALF), cols)
            p_re = probes_ref[(number, 0) + box]
            p_im = probes_ref[(number, 1) + box]
            grads = (p_re * b_re + p_im * b_im, p_re * b_im - p_im * b_re)
            for channel in range(2):
                grad = grads[channel]
                targets = [(rb * HALF, grad)]
                if rb == 0:
                    targets = [(0, jnp.where(in_row, grad, 0.0)), (WIN, jnp.where(in_row, 0.0, grad))]
                for at, piece in targets:
                    emit(channel, at, first_group, jnp.where(in_col, piece, 0.0))
                    emit(channel, at, second_group, jnp.where(in_col, 0.0, piece))


def window(i, near, consts, side, own, carried_own, carried_side, outs):
    border = () if near else ("beside",)
    own_width = 3 * LANE
    shapes = []
    for _, rows in outs:
        shapes += [jax.ShapeDtypeStruct((2, rows, width), F32) for width in (own_width, LANE)]
    operands = [piece[0] for piece in list(side) + list(own) + list(carried_own) + list(carried_side)]
    kernel = functools.partial(
        window_kernel,
        i,
        near,
        tuple((p[1], p[2], p[3:] + border) for p in side),
        tuple((p[1], p[2], p[3:]) for p in own),
        tuple((at, array.shape[1]) for array, at in carried_own),
        tuple((at, array.shape[1]) for array, at in carried_side),
        outs,
    )
    return pl.pallas_call(
        kernel,
        out_shape=tuple(shapes),
        in_specs=[pl.BlockSpec(memory_space=pltpu.SMEM)] + vmem(4 + len(operands)),
        out_specs=tuple(vmem(len(shapes))),
        scratch_shapes=[pltpu.VMEM((WIN, WIN), BF16)] * 16 + [pltpu.VMEM((WIN, WIN), F32)] * 8,
        cost_estimate=COST,
        compiler_params=pltpu.CompilerParams(vmem_limit_bytes=VMEM_LIMIT),
    )(*consts, *operands)


def variation_kernel(near, own, far, *refs):
    reg = refs[-1]
    out_ref = refs[-2]
    near_refs, refs = refs[: len(near)], refs[len(near) :]
    own_refs, far_refs = refs[: len(own)], refs[len(own) : len(own) + len(far)]
    even = even_column()

    def block(pieces, sources, at, channel):
        first, rows, sides = pieces[at]
        return kept(sources[at][channel, first : first + rows, :], *sides)

    row = 0
    for n, (_, rows, _) in enumerate(own):
        for channel in range(2):
            span = slice(row, row + rows)
            one = block(near, near_refs, n, channel)
            other = block(far, far_refs, n, channel)
            reg[channel, span, LANE : 4 * LANE] = block(own, own_refs, n, channel)
            reg[channel, span, :LANE] = jnp.where(even, other, one)
            reg[channel, span, 4 * LANE :] = jnp.where(even, one, other)
        row += rows

    def chunk(step, _):
        base = pl.multiple_of(step * 32, 8)
        flows = []
        power = tv_smooth
        for channel in range(2):
            block = reg[channel, pl.ds(base, 48), :]
            down = pltpu.roll(block, 47, 0) - block
            right = pltpu.roll(block, 5 * LANE - 1, 1) - block
            power = power + down * down + right * right
            flows.append((down, right))
        inverse = lax.rsqrt(power)
        for channel in range(2):
            down, right = flows[channel]
            down = down * inverse
            right = right * inverse
            change = pltpu.roll(down, 1, 0) - down + pltpu.roll(right, 1, 1) - right
            out_ref[channel, pl.ds(base, 32), :] = tv_weight * change[8:40, LANE : 4 * LANE]
        return 0

    lax.fori_loop(0, 6, chunk, 0)


def variation(near, own, far):
    parts = (near, own, far)
    plan = [
        tuple((p[1], p[2], p[3:] + border) for p in part) for part, border in zip(parts, ((), (), ("beside",)))
    ]
    operands = [piece[0] for part in parts for piece in part]
    return pl.pallas_call(
        functools.partial(variation_kernel, *plan),
        out_shape=jax.ShapeDtypeStruct((2, 192, 3 * LANE), F32),
        in_specs=vmem(len(operands)),
        out_specs=pl.BlockSpec(memory_space=pltpu.VMEM),
        scratch_shapes=[pltpu.VMEM((2, 208, 5 * LANE), F32)],
        cost_estimate=COST,
        compiler_params=pltpu.CompilerParams(vmem_limit_bytes=VMEM_LIMIT),
        name="variation",
    )(*operands)


def totals_kernel(outs, extras, own_ref, near_ref, far_ref, *refs):
    added, out_refs = refs[: len(extras)], refs[len(extras) :]
    even = even_column()
    for (first, rows), out in zip(outs, out_refs):
        cuts = {first, first + rows}
        for at, count, _ in extras:
            cuts |= {c for c in (at, at + count) if first < c < first + rows}
        cuts = sorted(cuts)
        for a, b in zip(cuts, cuts[1:]):
            for channel in range(2):
                value = own_ref[channel, a:b, :]
                for (at, count, source), ref in zip(extras, added):
                    if at <= a and b <= at + count:
                        value = value + ref[channel, source + a - at : source + b - at, :]
                to = slice(a - first, b - first)
                one = near_ref[channel, a:b, :]
                other = kept(far_ref[channel, a:b, :], "beside")
                out[channel, to, :LANE] = value[:, :LANE] + jnp.where(even, other, one)
                out[channel, to, LANE : 2 * LANE] = value[:, LANE : 2 * LANE]
                out[channel, to, 2 * LANE :] = value[:, 2 * LANE :] + jnp.where(even, one, other)


def totals(own, near, far, outs, extras):
    plan = tuple((at, rows, source) for _, source, at, rows in extras)
    return pl.pallas_call(
        functools.partial(totals_kernel, outs, plan),
        out_shape=tuple(jax.ShapeDtypeStruct((2, rows, own.shape[2]), F32) for _, rows in outs),
        in_specs=vmem(3 + len(extras)),
        out_specs=tuple(vmem(len(outs))),
        cost_estimate=COST,
        compiler_params=pltpu.CompilerParams(vmem_limit_bytes=VMEM_LIMIT),
        name="totals",
    )(own, near, far, *[extra[0] for extra in extras])


def update_kernel(pieces, side, *refs):
    new, near, far = refs[-3:]
    even = even_column()
    ins = refs[:-3]
    row = 0
    for which, first, rows, grads, masked in pieces:
        for channel in range(2):
            total = None
            for grad, at in grads:
                term = ins[grad][channel, at : at + rows, :]
                if grad == len(ins) - 1:
                    term = kept(term, side)
                total = term if total is None else total + term
            value = ins[which][channel, first : first + rows, :] - step_size * total
            if masked:
                value = kept(value, side)
            new[channel, row : row + rows, :] = value
            near[channel, row : row + rows, :] = jnp.where(even, value[:, 2 * LANE :], value[:, :LANE])
            far[channel, row : row + rows, :] = jnp.where(even, value[:, :LANE], value[:, 2 * LANE :])
        row += rows


def update(operands, pieces, side):
    rows = sum(piece[2] for piece in pieces)
    shape = [jax.ShapeDtypeStruct((2, rows, width), F32) for width in (3 * LANE, LANE, LANE)]
    return pl.pallas_call(
        functools.partial(update_kernel, pieces, side),
        out_shape=tuple(shape),
        in_specs=vmem(len(operands)),
        out_specs=tuple(vmem(3)),
        cost_estimate=COST,
        compiler_params=pltpu.CompilerParams(vmem_limit_bytes=VMEM_LIMIT),
        name="update",
    )(*operands)


def finish_kernel(top_ref, bottom_ref, mid_ref, low_ref, above_ref, below_ref, out_ref):
    for channel in range(2):
        above = mid_ref[channel, :MARGIN, :] + kept(above_ref[channel], "above")
        out_ref[channel, :MARGIN, :] = top_ref[channel, MARGIN:, :] - step_size * above
        out_ref[channel, MARGIN:288, :] = bottom_ref[channel, :192, :] - step_size * mid_ref[channel, MARGIN:, :]
        below = low_ref[channel] + kept(below_ref[channel], "below")
        out_ref[channel, 288:, :] = bottom_ref[channel, 192:288, :] - step_size * below


def finish(*operands):
    return pl.pallas_call(
        finish_kernel,
        out_shape=jax.ShapeDtypeStruct((2, 3 * LANE, 3 * LANE), F32),
        in_specs=vmem(len(operands)),
        out_specs=pl.BlockSpec(memory_space=pltpu.VMEM),
        cost_estimate=COST,
        compiler_params=pltpu.CompilerParams(vmem_limit_bytes=VMEM_LIMIT),
        name="finish",
    )(*operands)


def moved(block, axis, distance):
    count = lax.axis_size(axis)
    return lax.ppermute(block, axis, [(n, (n + distance) % count) for n in range(count)])


def to_near(block):
    rows, cols = lax.axis_size("row"), lax.axis_size("col")
    return lax.ppermute(block, ("row", "col"), [(r * cols + c, r * cols + (c ^ 1)) for r in range(rows) for c in range(cols)])


def to_far(block, ends=True):
    rows, cols = lax.axis_size("row"), lax.axis_size("col")
    route = []
    for r in range(rows):
        for c in range(cols):
            other = c - 1 if c % 2 == 0 else c + 1
            if ends or 0 <= other < cols:
                route.append((r * cols + c, r * cols + other % cols))
    return lax.ppermute(block, ("row", "col"), route)


def edges(block):
    width = block.shape[2]
    low, high = block[:, :, :LANE], block[:, :, width - LANE :]
    even = even_column()
    return jnp.where(even, high, low), jnp.where(even, low, high)


def on_device(table, twiddle, order, object_field, probe, amplitudes, offsets):
    tile = object_field.shape[1]
    last = tile - MARGIN
    band = 2 * MARGIN
    obj = object_field
    after = lax.optimization_barrier

    top = moved(obj[:, last:, :], "row", 1)
    near_strip, far_strip = edges(obj)
    far, near = to_far(far_strip), to_near(near_strip)
    up_rows, top = after((obj[:, :MARGIN, :], top))
    bottom = moved(up_rows, "row", -1)
    probes, amps = prepare(offsets, probe, amplitudes, order)
    consts = (offsets, table, twiddle, probes, amps)

    near_strip, far_strip = edges(top)
    top_b, top_a = to_far(far_strip), to_near(near_strip)
    own = [(top, 0, MARGIN, "above"), (obj, 0, last)]
    halves = ((0, band), (band, band))
    lo_o, lo_a, mid_o, mid_a = window(
        0, True, consts, [(top_a, 0, MARGIN, "above"), (near, 0, last)], own, [], [], halves
    )
    in_a = to_near(lo_a)
    lo_o, lo_b, mid_o, mid_b = window(
        0, False, consts, [(top_b, 0, MARGIN, "above"), (far, 0, last)], own, [(lo_o, 0), (mid_o, band)], [], halves
    )
    in_b = to_far(lo_b)
    bottom, lo_b = after((bottom, lo_b))
    near_strip, far_strip = edges(bottom)
    bot_b, bot_a = to_far(far_strip), to_near(near_strip)
    tv_top = variation(
        [(top_a, 88, 8, "above"), (near, 0, 200)],
        [(top, 88, 8, "above"), (obj, 0, 200)],
        [(top_b, 88, 8, "above"), (far, 0, 200)],
    )
    (top_sum,) = totals(lo_o, in_a, in_b, ((0, band),), [(tv_top, 0, MARGIN, MARGIN)])
    from_below = moved(top_sum, "row", -1)

    mid_o, top_sum = after((mid_o, top_sum))
    own = [(obj, MARGIN, last), (bottom, 0, MARGIN, "below")]
    whole = ((0, tile),)
    hi_o, hi_b = window(
        1, False, consts, [(far, MARGIN, last), (bot_b, 0, MARGIN, "below")], own, [(mid_o, 0)], [(mid_b, 0)], whole,
    )
    in_b = to_far(hi_b, ends=False)
    hi_o, hi_a = window(
        1, True, consts, [(near, MARGIN, last), (bot_a, 0, MARGIN, "below")], own, [(hi_o, 0)], [(mid_a, 0)], whole,
    )
    in_a = to_near(hi_a)
    tv_bottom = variation(
        [(near, 184, 200), (bot_a, 0, 8, "below")],
        [(obj, 184, 200), (bottom, 0, 8, "below")],
        [(far, 184, 200), (bot_b, 0, 8, "below")],
    )
    mid_sum, bot_sum = totals(
        hi_o, in_a, in_b, halves, [(tv_top, MARGIN, 0, MARGIN), (tv_bottom, 0, MARGIN, band)]
    )
    from_above = moved(bot_sum, "row", 1)

    low, near_strip, far_strip = update(
        (obj, bottom, mid_sum, bot_sum, from_below),
        (
            (0, MARGIN, band, ((2, 0),), False),
            (0, last, MARGIN, ((3, 0), (4, 0)), False),
            (1, 0, MARGIN, ((3, MARGIN), (4, MARGIN)), True),
        ),
        "below",
    )
    low_a, low_b = to_near(near_strip), to_far(far_strip, ends=False)
    own = [(low, 0, tile)]
    mid_o, mid_a, hi_o, hi_a = window(1, True, consts, [(low_a, 0, tile)], own, [], [], halves)
    in_a = to_near(hi_a)
    mid_o, mid_b, hi_o, hi_b = window(
        1, False, consts, [(low_b, 0, tile)], own, [(mid_o, 0), (hi_o, band)], [], halves
    )
    hi_in_b = to_far(hi_b)
    hi_in_a = in_a
    tv_bottom = variation([(low_a, 88, 208)], [(low, 88, 208)], [(low_b, 88, 208)])
    top, hi_b = after((top, hi_b))
    up, near_strip, far_strip = update(
        (top, obj, top_sum, from_above),
        (
            (0, 0, MARGIN, ((2, 0), (3, 0)), True),
            (1, 0, MARGIN, ((2, MARGIN), (3, MARGIN)), False),
        ),
        "above",
    )
    up_b, up_a = to_far(far_strip), to_near(near_strip)
    own = [(up, 0, band), (low, 0, band)]
    cut = ((0, MARGIN), (MARGIN, last))
    over_o, over_a, lo_o, lo_a = window(
        0, True, consts, [(up_a, 0, band), (low_a, 0, band)], own, [(mid_o, band)], [(mid_a, band)], cut
    )
    over_a, in_a = to_near(over_a), to_near(lo_a)
    lo_o, hi_o = after((lo_o, hi_o))
    low_sum, over = totals(
        hi_o, hi_in_a, hi_in_b, ((0, MARGIN), (MARGIN, MARGIN)), [(tv_bottom, MARGIN, 0, MARGIN)]
    )
    lo_o, over = after((lo_o, over))
    last_above = moved(over, "row", 1)
    over_o, over_b, lo_o, lo_b = window(
        0, False, consts, [(up_b, 0, band), (low_b, 0, band)], own, [(over_o, 0), (lo_o, MARGIN)], [(mid_b, band)], cut,
    )
    over_b = to_far(over_b)
    (over,) = totals(over_o, over_a, over_b, ((0, MARGIN),), [])
    last_below = moved(over, "row", -1)
    in_b = to_far(lo_b)
    tv_top = variation(
        [(up_a, 88, 104), (low_a, 0, 104)], [(up, 88, 104), (low, 0, 104)], [(up_b, 88, 104), (low_b, 0, 104)]
    )
    (mid_sum,) = totals(lo_o, in_a, in_b, ((0, last),), [(tv_top, 0, 0, band), (tv_bottom, 0, band, MARGIN)])
    return finish(up, low, mid_sum, low_sum, last_above, last_below)


def solution(mesh):
    table, twiddle, order = tables()
    body = jax.shard_map(
        on_device,
        mesh=mesh,
        in_specs=(P(), P(), P(), P(None, "row", "col"), P(), P("row", "col"), P("row", "col", None)),
        out_specs=P(None, "row", "col"),
        check_vma=False,
    )

    def step(object_field, probe, amplitudes, offsets):
        return body(table, twiddle, order, object_field, probe, amplitudes, offsets)

    return step
```

```python
import functools
import math

import jax
import jax.numpy as jnp
import numpy as np
from jax import lax
from jax.experimental import pallas as pl
from jax.experimental.pallas import tpu as pltpu
from jax.sharding import PartitionSpec as P


WIN = 256
HALF = 128
MARGIN = 96
LANE = 128
COST = pl.CostEstimate(flops=100_000, bytes_accessed=100_000, transcendentals=0)
VMEM_LIMIT = 24 * 1024 * 1024

step_size = 0.3
tv_weight = 0.2
tv_smooth = 0.1
amp_floor = 0.5

F32 = jnp.float32
BF16 = jnp.bfloat16


def tables():
    counter = np.arange(HALF)
    angle = (counter[:, None] * counter[None, :] % HALF) * (2.0 * math.pi / HALF)
    cosine = np.cos(angle) / math.sqrt(WIN)
    sine = np.sin(angle) / math.sqrt(WIN)
    first = np.block([[cosine, sine], [-sine, cosine]])
    second = np.block([[cosine, -sine], [sine, cosine]])
    parts = []
    for table in (first, second):
        table = table.astype(np.float32)
        high = table.astype(jnp.bfloat16)
        low = (table - high.astype(np.float32)).astype(jnp.bfloat16)
        parts += [high, low]
    turn = counter * (2.0 * math.pi / WIN)
    rows = np.stack([np.cos(turn), np.sin(turn)])
    by_row = np.broadcast_to(rows[:, :, None], (2, HALF, HALF))
    by_lane = np.broadcast_to(rows[:, None, :], (2, HALF, HALF))
    twiddle = np.concatenate([by_row, by_lane]).astype(np.float32)
    order = np.zeros((WIN, WIN), np.float32)
    for parity in range(2):
        order[2 * counter + parity, parity * HALF + counter] = 1.0
    return np.stack(parts), twiddle, order.astype(jnp.bfloat16)


def split(value):
    high = value.astype(BF16)
    return high, (value - high.astype(F32)).astype(BF16)


def has(side):
    if side == "above":
        return lax.axis_index("row") > 0
    if side == "below":
        return lax.axis_index("row") < lax.axis_size("row") - 1
    return (lax.axis_index("col") > 0) & (lax.axis_index("col") < lax.axis_size("col") - 1)


def even_column():
    return lax.axis_index("col") % 2 == 0


def kept(value, *sides):
    for side in sides:
        value = jnp.where(has(side), value, 0.0)
    return value


def mul(left, right):
    return jnp.dot(left, right, preferred_element_type=F32)


def vmem(count):
    return [pl.BlockSpec(memory_space=pltpu.VMEM)] * count


def prepare_kernel(off_ref, probe_ref, amp_ref, order_ref, probes_ref, amps_ref, parts_ref):
    order = order_ref[...]
    for i in range(2):
        for j in range(2):
            row = off_ref[i, j, 0]
            col = (off_ref[i, j, 1] + (32 if j == 0 else 224)) % WIN
            for channel in range(2):
                turned = pltpu.roll(probe_ref[channel], row, 0)
                probes_ref[2 * i + j, channel] = pltpu.roll(turned, col, 1)
            amp = amp_ref[i * WIN : (i + 1) * WIN, j * WIN : (j + 1) * WIN]
            high, rest = split(amp)
            middle, _ = split(amp - high.astype(F32) - rest.astype(F32))
            sorted_lanes = mul(high, order) + mul(rest, order) + mul(middle, order)
            for q in range(2):
                parts_ref[...] = sorted_lanes[:, q * HALF : (q + 1) * HALF]
                for p in range(2):
                    at = q * WIN + p * HALF
                    amps_ref[2 * i + j, at : at + HALF, :] = parts_ref[pl.ds(p, HALF, stride=2), :]


def prepare(offsets, probe, amplitudes, order):
    return pl.pallas_call(
        prepare_kernel,
        out_shape=(
            jax.ShapeDtypeStruct((4, 2, WIN, WIN), F32),
            jax.ShapeDtypeStruct((4, 2 * WIN, HALF), F32),
        ),
        in_specs=[pl.BlockSpec(memory_space=pltpu.SMEM)] + vmem(3),
        out_specs=tuple(vmem(2)),
        scratch_shapes=[pltpu.VMEM((WIN, HALF), F32)],
        cost_estimate=COST,
        compiler_params=pltpu.CompilerParams(vmem_limit_bytes=VMEM_LIMIT),
        name="prepare",
    )(offsets, probe, amplitudes, order)


def rows_of(pieces, refs, first, rows):
    found, at = [], 0
    for ref, (start, count, sides) in zip(refs, pieces):
        lo, hi = max(first, at), min(first + rows, at + count)
        if lo < hi:
            found.append((ref, start + lo - at, hi - lo, sides))
        at += count
    return found


def window_kernel(i, near, side, own, carried_own, carried_side, outs, *refs):
    off_ref, tab_ref, tw_ref, probes_ref, amps_ref = refs[:5]
    refs = refs[5:]
    side_refs, refs = refs[: len(side)], refs[len(side) :]
    own_refs, refs = refs[: len(own)], refs[len(own) :]
    sum_refs, refs = refs[: len(carried_own)], refs[len(carried_own) :]
    strip_refs, refs = refs[: len(carried_side)], refs[len(carried_side) :]
    out_refs, refs = refs[: 2 * len(outs)], refs[2 * len(outs) :]
    halves = [refs[n : n + 2] for n in range(0, 16, 2)]
    g_in, h_in, m_in, g_out = halves[0:2], halves[2:4], halves[4:6], halves[6:8]
    wide, tall, tall_back, wide_back = refs[16:18], refs[18:20], refs[20:22], refs[22:24]

    to_right = even_column() if near else jnp.logical_not(even_column())
    j = jnp.where(to_right, 1, 0)
    number = 2 * i + j
    row_start = off_ref[i, j, 0]
    col_start = off_ref[i, j, 1]
    row_iota = lax.broadcasted_iota(jnp.int32, (HALF, HALF), 0)
    lane_iota = lax.broadcasted_iota(jnp.int32, (HALF, HALF), 1)
    in_row = row_iota >= row_start
    sign = jnp.where(to_right, -1, 1)
    in_first = (
        sign * lane_iota >= jnp.where(to_right, 33 - col_start, 32 + col_start),
        lane_iota >= jnp.where(to_right, 96 + col_start, col_start - 96),
    )
    first_h, first_l, second_h, second_l = (tab_ref.at[n] for n in range(4))
    groups = (("strip", 1), (0, 2))

    def place(group):
        if group == "strip":
            return True, slice(0, LANE)
        return False, slice(group * LANE, (group + 1) * LANE)

    def load(channel, first, group):
        is_strip, lanes = place(group)
        pieces, sources = (side, side_refs) if is_strip else (own, own_refs)
        blocks = [
            kept(ref[channel, at : at + rows, lanes], *sides)
            for ref, at, rows, sides in rows_of(pieces, sources, first, HALF)
        ]
        return blocks[0] if len(blocks) == 1 else jnp.concatenate(blocks, axis=0)

    def emit(channel, first, group, value):
        is_strip, lanes = place(group)
        extra = (carried_side, strip_refs) if is_strip else (carried_own, sum_refs)
        which = 1 if is_strip else 0
        for n, (start, count) in enumerate(outs):
            lo, hi = max(first, start), min(first + HALF, start + count)
            if lo >= hi:
                continue
            cuts = sorted({lo, hi} | {c for at, rows in extra[0] for c in (at, at + rows) if lo < c < hi})
            for a, b in zip(cuts, cuts[1:]):
                part = value[a - first : b - first]
                for (at, rows), ref in zip(*extra):
                    if at <= a and b <= at + rows:
                        part = part + ref[channel, a - at : b - at, lanes]
                out_refs[2 * n + which][channel, a - start : b - start, lanes] = part

    def store_split(pair, rows, lanes, value):
        high, low = split(value)
        pair[0][rows, lanes] = high
        pair[1][rows, lanes] = low

    lo, hi = slice(0, HALF), slice(HALF, WIN)
    tw_c, tw_s = tw_ref[0], tw_ref[1]
    for cb in range(2):
        in_col = in_first[cb]
        first_group, second_group = groups[cb]
        field = []
        for rb in range(2):
            value = []
            for channel in range(2):
                at = rb * HALF
                picked = jnp.where(in_col, load(channel, at, first_group), load(channel, at, second_group))
                if rb == 0:
                    other = jnp.where(in_col, load(channel, WIN, first_group), load(channel, WIN, second_group))
                    picked = jnp.where(in_row, picked, other)
                value.append(picked)
            box = (slice(rb * HALF, (rb + 1) * HALF), slice(cb * LANE, (cb + 1) * LANE))
            p_re = probes_ref[(number, 0) + box]
            p_im = probes_ref[(number, 1) + box]
            field.append((p_re * value[0] - p_im * value[1], p_re * value[1] + p_im * value[0]))
        (re0, im0), (re1, im1) = field
        store_split(g_in[cb], lo, lo, re0 + re1)
        store_split(g_in[cb], hi, lo, im0 + im1)
        d_re = re0 - re1
        d_im = im0 - im1
        store_split(g_in[cb], lo, hi, d_re * tw_c + d_im * tw_s)
        store_split(g_in[cb], hi, hi, d_im * tw_c - d_re * tw_s)
        high, low = g_in[cb][0][...], g_in[cb][1][...]
        wide[cb][...] = mul(first_h[...], high) + mul(first_h[...], low) + mul(first_l[...], high)

    for p in range(2):
        tl_c, tl_s = tw_ref[2], tw_ref[3]
        cols = slice(p * HALF, (p + 1) * HALF)
        re0, re1 = wide[0][lo, cols], wide[1][lo, cols]
        im0, im1 = wide[0][hi, cols], wide[1][hi, cols]
        store_split(h_in[p], lo, lo, re0 + re1)
        store_split(h_in[p], lo, hi, im0 + im1)
        d_re = re0 - re1
        d_im = im0 - im1
        store_split(h_in[p], hi, lo, d_re * tl_c + d_im * tl_s)
        store_split(h_in[p], hi, hi, d_im * tl_c - d_re * tl_s)
        high, low = h_in[p][0][...], h_in[p][1][...]
        tall[p][...] = mul(high, second_h[...]) + mul(low, second_h[...]) + mul(high, second_l[...])

    for p in range(2):
        for q, rows in enumerate((lo, hi)):
            re, im = tall[p][rows, lo], tall[p][rows, hi]
            power = jnp.maximum(re * re + im * im, amp_floor * amp_floor)
            at = q * WIN + p * HALF
            keeping = 1.0 - amps_ref[number, at : at + HALF, :] * lax.rsqrt(power)
            store_split(m_in[p], rows, lo, re * keeping)
            store_split(m_in[p], rows, hi, im * keeping)
        high, low = m_in[p][0][...], m_in[p][1][...]
        tall_back[p][...] = mul(high, first_h[...]) + mul(low, first_h[...]) + mul(high, first_l[...])

    for p in range(2):
        tl_c, tl_s = tw_ref[2], tw_ref[3]
        u_re, u_im = tall_back[p][lo, lo], tall_back[p][lo, hi]
        v_re, v_im = tall_back[p][hi, lo], tall_back[p][hi, hi]
        w_re = v_re * tl_c - v_im * tl_s
        w_im = v_im * tl_c + v_re * tl_s
        store_split(g_out[p], lo, lo, u_re + w_re)
        store_split(g_out[p], lo, hi, u_re - w_re)
        store_split(g_out[p], hi, lo, u_im + w_im)
        store_split(g_out[p], hi, hi, u_im - w_im)
        high, low = g_out[p][0][...], g_out[p][1][...]
        wide_back[p][...] = mul(second_h[...], high) + mul(second_h[...], low) + mul(second_l[...], high)

    for cb in range(2):
        in_col = in_first[cb]
        first_group, second_group = groups[cb]
        cols = slice(cb * LANE, (cb + 1) * LANE)
        u_re, u_im = wide_back[0][lo, cols], wide_back[0][hi, cols]
        v_re, v_im = wide_back[1][lo, cols], wide_back[1][hi, cols]
        w_re = v_re * tw_c - v_im * tw_s
        w_im = v_im * tw_c + v_re * tw_s
        for rb in range(2):
            b_re = u_re + w_re if rb == 0 else u_re - w_re
            b_im = u_im + w_im if rb == 0 else u_im - w_im
            box = (slice(rb * HALF, (rb + 1) * HALF), cols)
            p_re = probes_ref[(number, 0) + box]
            p_im = probes_ref[(number, 1) + box]
            grads = (p_re * b_re + p_im * b_im, p_re * b_im - p_im * b_re)
            for channel in range(2):
                grad = grads[channel]
                targets = [(rb * HALF, grad)]
                if rb == 0:
                    targets = [(0, jnp.where(in_row, grad, 0.0)), (WIN, jnp.where(in_row, 0.0, grad))]
                for at, piece in targets:
                    emit(channel, at, first_group, jnp.where(in_col, piece, 0.0))
                    emit(channel, at, second_group, jnp.where(in_col, 0.0, piece))


def window(i, near, consts, side, own, carried_own, carried_side, outs):
    border = () if near else ("beside",)
    own_width = 3 * LANE
    shapes = []
    for _, rows in outs:
        shapes += [jax.ShapeDtypeStruct((2, rows, width), F32) for width in (own_width, LANE)]
    operands = [piece[0] for piece in list(side) + list(own) + list(carried_own) + list(carried_side)]
    kernel = functools.partial(
        window_kernel,
        i,
        near,
        tuple((p[1], p[2], p[3:] + border) for p in side),
        tuple((p[1], p[2], p[3:]) for p in own),
        tuple((at, array.shape[1]) for array, at in carried_own),
        tuple((at, array.shape[1]) for array, at in carried_side),
        outs,
    )
    return pl.pallas_call(
        kernel,
        out_shape=tuple(shapes),
        in_specs=[pl.BlockSpec(memory_space=pltpu.SMEM)] + vmem(4 + len(operands)),
        out_specs=tuple(vmem(len(shapes))),
        scratch_shapes=[pltpu.VMEM((WIN, WIN), BF16)] * 16 + [pltpu.VMEM((WIN, WIN), F32)] * 8,
        cost_estimate=COST,
        compiler_params=pltpu.CompilerParams(vmem_limit_bytes=VMEM_LIMIT),
    )(*consts, *operands)


def variation_kernel(near, own, far, *refs):
    reg = refs[-1]
    out_ref = refs[-2]
    near_refs, refs = refs[: len(near)], refs[len(near) :]
    own_refs, far_refs = refs[: len(own)], refs[len(own) : len(own) + len(far)]
    even = even_column()

    def block(pieces, sources, at, channel):
        first, rows, sides = pieces[at]
        return kept(sources[at][channel, first : first + rows, :], *sides)

    row = 0
    for n, (_, rows, _) in enumerate(own):
        for channel in range(2):
            span = slice(row, row + rows)
            one = block(near, near_refs, n, channel)
            other = block(far, far_refs, n, channel)
            reg[channel, span, LANE : 4 * LANE] = block(own, own_refs, n, channel)
            reg[channel, span, :LANE] = jnp.where(even, other, one)
            reg[channel, span, 4 * LANE :] = jnp.where(even, one, other)
        row += rows

    def chunk(step, _):
        base = pl.multiple_of(step * 32, 8)
        flows = []
        power = tv_smooth
        for channel in range(2):
            block = reg[channel, pl.ds(base, 48), :]
            down = pltpu.roll(block, 47, 0) - block
            right = pltpu.roll(block, 5 * LANE - 1, 1) - block
            power = power + down * down + right * right
            flows.append((down, right))
        inverse = lax.rsqrt(power)
        for channel in range(2):
            down, right = flows[channel]
            down = down * inverse
            right = right * inverse
            change = pltpu.roll(down, 1, 0) - down + pltpu.roll(right, 1, 1) - right
            out_ref[channel, pl.ds(base, 32), :] = tv_weight * change[8:40, LANE : 4 * LANE]
        return 0

    lax.fori_loop(0, 6, chunk, 0)


def variation(near, own, far):
    parts = (near, own, far)
    plan = [
        tuple((p[1], p[2], p[3:] + border) for p in part) for part, border in zip(parts, ((), (), ("beside",)))
    ]
    operands = [piece[0] for part in parts for piece in part]
    return pl.pallas_call(
        functools.partial(variation_kernel, *plan),
        out_shape=jax.ShapeDtypeStruct((2, 192, 3 * LANE), F32),
        in_specs=vmem(len(operands)),
        out_specs=pl.BlockSpec(memory_space=pltpu.VMEM),
        scratch_shapes=[pltpu.VMEM((2, 208, 5 * LANE), F32)],
        cost_estimate=COST,
        compiler_params=pltpu.CompilerParams(vmem_limit_bytes=VMEM_LIMIT),
        name="variation",
    )(*operands)


def totals_kernel(outs, extras, own_ref, near_ref, far_ref, *refs):
    added, out_refs = refs[: len(extras)], refs[len(extras) :]
    even = even_column()
    for (first, rows), out in zip(outs, out_refs):
        cuts = {first, first + rows}
        for at, count, _ in extras:
            cuts |= {c for c in (at, at + count) if first < c < first + rows}
        cuts = sorted(cuts)
        for a, b in zip(cuts, cuts[1:]):
            for channel in range(2):
                value = own_ref[channel, a:b, :]
                for (at, count, source), ref in zip(extras, added):
                    if at <= a and b <= at + count:
                        value = value + ref[channel, source + a - at : source + b - at, :]
                to = slice(a - first, b - first)
                one = near_ref[channel, a:b, :]
                other = kept(far_ref[channel, a:b, :], "beside")
                out[channel, to, :LANE] = value[:, :LANE] + jnp.where(even, other, one)
                out[channel, to, LANE : 2 * LANE] = value[:, LANE : 2 * LANE]
                out[channel, to, 2 * LANE :] = value[:, 2 * LANE :] + jnp.where(even, one, other)


def totals(own, near, far, outs, extras):
    plan = tuple((at, rows, source) for _, source, at, rows in extras)
    return pl.pallas_call(
        functools.partial(totals_kernel, outs, plan),
        out_shape=tuple(jax.ShapeDtypeStruct((2, rows, own.shape[2]), F32) for _, rows in outs),
        in_specs=vmem(3 + len(extras)),
        out_specs=tuple(vmem(len(outs))),
        cost_estimate=COST,
        compiler_params=pltpu.CompilerParams(vmem_limit_bytes=VMEM_LIMIT),
        name="totals",
    )(own, near, far, *[extra[0] for extra in extras])


def update_kernel(pieces, side, *refs):
    new, near, far = refs[-3:]
    even = even_column()
    ins = refs[:-3]
    row = 0
    for which, first, rows, grads, masked in pieces:
        for channel in range(2):
            total = None
            for grad, at in grads:
                term = ins[grad][channel, at : at + rows, :]
                if grad == len(ins) - 1:
                    term = kept(term, side)
                total = term if total is None else total + term
            value = ins[which][channel, first : first + rows, :] - step_size * total
            if masked:
                value = kept(value, side)
            new[channel, row : row + rows, :] = value
            near[channel, row : row + rows, :] = jnp.where(even, value[:, 2 * LANE :], value[:, :LANE])
            far[channel, row : row + rows, :] = jnp.where(even, value[:, :LANE], value[:, 2 * LANE :])
        row += rows


def update(operands, pieces, side):
    rows = sum(piece[2] for piece in pieces)
    shape = [jax.ShapeDtypeStruct((2, rows, width), F32) for width in (3 * LANE, LANE, LANE)]
    return pl.pallas_call(
        functools.partial(update_kernel, pieces, side),
        out_shape=tuple(shape),
        in_specs=vmem(len(operands)),
        out_specs=tuple(vmem(3)),
        cost_estimate=COST,
        compiler_params=pltpu.CompilerParams(vmem_limit_bytes=VMEM_LIMIT),
        name="update",
    )(*operands)


def near_kernel(own_ref, near_ref, out_ref):
    even = even_column()
    for channel in range(2):
        strip = near_ref[channel]
        out_ref[channel, :, :LANE] = own_ref[channel, :, :LANE] + jnp.where(even, 0.0, strip)
        out_ref[channel, :, LANE : 2 * LANE] = own_ref[channel, :, LANE : 2 * LANE]
        out_ref[channel, :, 2 * LANE :] = own_ref[channel, :, 2 * LANE :] + jnp.where(even, strip, 0.0)


def sums_near(own, near):
    return (
        pl.pallas_call(
            near_kernel,
            out_shape=jax.ShapeDtypeStruct(own.shape, F32),
            in_specs=vmem(2),
            out_specs=pl.BlockSpec(memory_space=pltpu.VMEM),
            cost_estimate=COST,
            compiler_params=pltpu.CompilerParams(vmem_limit_bytes=VMEM_LIMIT),
            name="sums_near",
        )(own, near),
    )


def finish_kernel(top_ref, bottom_ref, mid_ref, low_ref, above_ref, below_ref, corner_ref, out_ref):
    for channel in range(2):
        above = mid_ref[channel, :MARGIN, :] + kept(above_ref[channel], "above")
        out_ref[channel, :MARGIN, :] = top_ref[channel, MARGIN:, :] - step_size * above
        out_ref[channel, MARGIN:288, :] = bottom_ref[channel, :192, :] - step_size * mid_ref[channel, MARGIN:, :]
        base = bottom_ref[channel, 192:288, :] - step_size * (low_ref[channel] + kept(below_ref[channel], "below"))
        corner = step_size * kept(corner_ref[channel], "below", "beside")
        even = even_column()
        out_ref[channel, 288:, :LANE] = base[:, :LANE] - jnp.where(even, corner, 0.0)
        out_ref[channel, 288:, LANE : 2 * LANE] = base[:, LANE : 2 * LANE]
        out_ref[channel, 288:, 2 * LANE :] = base[:, 2 * LANE :] - jnp.where(even, 0.0, corner)


def finish(*operands):
    return pl.pallas_call(
        finish_kernel,
        out_shape=jax.ShapeDtypeStruct((2, 3 * LANE, 3 * LANE), F32),
        in_specs=vmem(len(operands)),
        out_specs=pl.BlockSpec(memory_space=pltpu.VMEM),
        cost_estimate=COST,
        compiler_params=pltpu.CompilerParams(vmem_limit_bytes=VMEM_LIMIT),
        name="finish",
    )(*operands)


def moved(block, axis, distance):
    count = lax.axis_size(axis)
    return lax.ppermute(block, axis, [(n, (n + distance) % count) for n in range(count)])


def to_near(block):
    rows, cols = lax.axis_size("row"), lax.axis_size("col")
    return lax.ppermute(block, ("row", "col"), [(r * cols + c, r * cols + (c ^ 1)) for r in range(rows) for c in range(cols)])


def to_far(block, ends=True):
    rows, cols = lax.axis_size("row"), lax.axis_size("col")
    route = []
    for r in range(rows):
        for c in range(cols):
            other = c - 1 if c % 2 == 0 else c + 1
            if ends or 0 <= other < cols:
                route.append((r * cols + c, r * cols + other % cols))
    return lax.ppermute(block, ("row", "col"), route)


def to_far_above(block):
    rows, cols = lax.axis_size("row"), lax.axis_size("col")
    route = []
    for r in range(rows):
        for c in range(cols):
            other = c - 1 if c % 2 == 0 else c + 1
            route.append((r * cols + c, (r - 1) % rows * cols + other % cols))
    return lax.ppermute(block, ("row", "col"), route)


def edges(block):
    width = block.shape[2]
    low, high = block[:, :, :LANE], block[:, :, width - LANE :]
    even = even_column()
    return jnp.where(even, high, low), jnp.where(even, low, high)


def on_device(table, twiddle, order, object_field, probe, amplitudes, offsets):
    tile = object_field.shape[1]
    last = tile - MARGIN
    band = 2 * MARGIN
    obj = object_field
    after = lax.optimization_barrier

    top = moved(obj[:, last:, :], "row", 1)
    near_strip, far_strip = edges(obj)
    far, near = to_far(far_strip), to_near(near_strip)
    up_rows, top = after((obj[:, :MARGIN, :], top))
    bottom = moved(up_rows, "row", -1)
    probes, amps = prepare(offsets, probe, amplitudes, order)
    consts = (offsets, table, twiddle, probes, amps)

    near_strip, far_strip = edges(top)
    top_b, top_a = to_far(far_strip), to_near(near_strip)
    own = [(top, 0, MARGIN, "above"), (obj, 0, last)]
    halves = ((0, band), (band, band))
    lo_o, lo_a, mid_o, mid_a = window(
        0, True, consts, [(top_a, 0, MARGIN, "above"), (near, 0, last)], own, [], [], halves
    )
    in_a = to_near(lo_a)
    lo_o, lo_b, mid_o, mid_b = window(
        0, False, consts, [(top_b, 0, MARGIN, "above"), (far, 0, last)], own, [(lo_o, 0), (mid_o, band)], [], halves
    )
    in_b = to_far(lo_b)
    bottom, lo_b = after((bottom, lo_b))
    near_strip, far_strip = edges(bottom)
    bot_b, bot_a = to_far(far_strip), to_near(near_strip)
    tv_top = variation(
        [(top_a, 88, 8, "above"), (near, 0, 200)],
        [(top, 88, 8, "above"), (obj, 0, 200)],
        [(top_b, 88, 8, "above"), (far, 0, 200)],
    )
    own = [(obj, MARGIN, last), (bottom, 0, MARGIN, "below")]
    whole = ((0, tile),)
    hi_o, hi_a = window(
        1, True, consts, [(near, MARGIN, last), (bot_a, 0, MARGIN, "below")], own, [(mid_o, 0)], [(mid_a, 0)], whole
    )
    lo_o, hi_o = after((lo_o, hi_o))
    (top_sum,) = totals(lo_o, in_a, in_b, ((0, band),), [(tv_top, 0, MARGIN, MARGIN)])
    from_below = moved(top_sum, "row", -1)
    in_a = to_near(hi_a)
    hi_o, hi_b = window(
        1, False, consts, [(far, MARGIN, last), (bot_b, 0, MARGIN, "below")], own, [(hi_o, 0)], [(mid_b, 0)], whole,
    )
    in_b = to_far(hi_b, ends=False)
    tv_bottom = variation(
        [(near, 184, 200), (bot_a, 0, 8, "below")],
        [(obj, 184, 200), (bottom, 0, 8, "below")],
        [(far, 184, 200), (bot_b, 0, 8, "below")],
    )
    mid_sum, bot_sum = totals(
        hi_o, in_a, in_b, halves, [(tv_top, MARGIN, 0, MARGIN), (tv_bottom, 0, MARGIN, band)]
    )

    bot_sum, from_below = after((bot_sum, from_below))
    low, near_strip, far_strip = update(
        (obj, bottom, mid_sum, bot_sum, from_below),
        (
            (0, MARGIN, band, ((2, 0),), False),
            (0, last, MARGIN, ((3, 0), (4, 0)), False),
            (1, 0, MARGIN, ((3, MARGIN), (4, MARGIN)), True),
        ),
        "below",
    )
    low_a = to_near(near_strip)
    low_b = to_far(far_strip, ends=False)
    from_above = moved(bot_sum, "row", 1)
    own = [(low, 0, tile)]
    mid_o, mid_a, hi_o, hi_a = window(1, True, consts, [(low_a, 0, tile)], own, [], [], halves)
    in_a = to_near(hi_a)
    mid_o, mid_b, hi_o, hi_b = window(
        1, False, consts, [(low_b, 0, tile)], own, [(mid_o, 0), (hi_o, band)], [], halves
    )
    hi_in_b = to_far(hi_b)
    hi_in_a = in_a
    tv_bottom = variation([(low_a, 88, 208)], [(low, 88, 208)], [(low_b, 88, 208)])
    top, hi_b = after((top, hi_b))
    up, near_strip, far_strip = update(
        (top, obj, top_sum, from_above),
        (
            (0, 0, MARGIN, ((2, 0), (3, 0)), True),
            (1, 0, MARGIN, ((2, MARGIN), (3, MARGIN)), False),
        ),
        "above",
    )
    up_b, up_a = to_far(far_strip), to_near(near_strip)
    own = [(up, 0, band), (low, 0, band)]
    cut = ((0, MARGIN), (MARGIN, last))
    over_o, over_a, lo_o, lo_a = window(
        0, True, consts, [(up_a, 0, band), (low_a, 0, band)], own, [(mid_o, band)], [(mid_a, band)], cut
    )
    over_a, in_a = to_near(over_a), to_near(lo_a)
    lo_o, hi_o = after((lo_o, hi_o))
    low_sum, over = totals(
        hi_o, hi_in_a, hi_in_b, ((0, MARGIN), (MARGIN, MARGIN)), [(tv_bottom, MARGIN, 0, MARGIN)]
    )
    lo_o, over = after((lo_o, over))
    last_above = moved(over, "row", 1)
    over_o, over_b, lo_o, lo_b = window(
        0, False, consts, [(up_b, 0, band), (low_b, 0, band)], own, [(over_o, 0), (lo_o, MARGIN)], [(mid_b, band)], cut,
    )
    (over,) = sums_near(over_o, over_a)
    last_below = moved(over, "row", -1)
    corner = to_far_above(over_b)
    in_b = to_far(lo_b)
    tv_top = variation(
        [(up_a, 88, 104), (low_a, 0, 104)], [(up, 88, 104), (low, 0, 104)], [(up_b, 88, 104), (low_b, 0, 104)]
    )
    (mid_sum,) = totals(lo_o, in_a, in_b, ((0, last),), [(tv_top, 0, 0, band), (tv_bottom, 0, band, MARGIN)])
    return finish(up, low, mid_sum, low_sum, last_above, last_below, corner)


def solution(mesh):
    table, twiddle, order = tables()
    body = jax.shard_map(
        on_device,
        mesh=mesh,
        in_specs=(P(), P(), P(), P(None, "row", "col"), P(), P("row", "col"), P("row", "col", None)),
        out_specs=P(None, "row", "col"),
        check_vma=False,
    )

    def step(object_field, probe, amplitudes, offsets):
        return body(table, twiddle, order, object_field, probe, amplitudes, offsets)

    return step
```

```python
import functools
import math

import jax
import jax.numpy as jnp
import numpy as np
from jax import lax
from jax.experimental import pallas as pl
from jax.experimental.pallas import tpu as pltpu
from jax.sharding import PartitionSpec as P


WIN = 256
HALF = 128
MARGIN = 96
LANE = 128
COST = pl.CostEstimate(flops=100_000, bytes_accessed=100_000, transcendentals=0)
VMEM_LIMIT = 24 * 1024 * 1024

step_size = 0.3
tv_weight = 0.2
tv_smooth = 0.1
amp_floor = 0.5

F32 = jnp.float32
BF16 = jnp.bfloat16


def tables():
    counter = np.arange(HALF)
    angle = (counter[:, None] * counter[None, :] % HALF) * (2.0 * math.pi / HALF)
    cosine = np.cos(angle) / math.sqrt(WIN)
    sine = np.sin(angle) / math.sqrt(WIN)
    first = np.block([[cosine, sine], [-sine, cosine]])
    second = np.block([[cosine, -sine], [sine, cosine]])
    parts = []
    for table in (first, second):
        table = table.astype(np.float32)
        high = table.astype(jnp.bfloat16)
        low = (table - high.astype(np.float32)).astype(jnp.bfloat16)
        parts += [high, low]
    turn = counter * (2.0 * math.pi / WIN)
    rows = np.stack([np.cos(turn), np.sin(turn)])
    by_row = np.broadcast_to(rows[:, :, None], (2, HALF, HALF))
    by_lane = np.broadcast_to(rows[:, None, :], (2, HALF, HALF))
    twiddle = np.concatenate([by_row, by_lane]).astype(np.float32)
    order = np.zeros((WIN, WIN), np.float32)
    for parity in range(2):
        order[2 * counter + parity, parity * HALF + counter] = 1.0
    return np.stack(parts), twiddle, order.astype(jnp.bfloat16)


def split(value):
    high = value.astype(BF16)
    return high, (value - high.astype(F32)).astype(BF16)


def has(side):
    if side == "above":
        return lax.axis_index("row") > 0
    if side == "below":
        return lax.axis_index("row") < lax.axis_size("row") - 1
    return (lax.axis_index("col") > 0) & (lax.axis_index("col") < lax.axis_size("col") - 1)


def even_column():
    return lax.axis_index("col") % 2 == 0


def kept(value, *sides):
    for side in sides:
        value = jnp.where(has(side), value, 0.0)
    return value


def mul(left, right):
    return jnp.dot(left, right, preferred_element_type=F32)


def vmem(count):
    return [pl.BlockSpec(memory_space=pltpu.VMEM)] * count


def prepare_kernel(off_ref, probe_ref, amp_ref, order_ref, probes_ref, amps_ref, parts_ref):
    order = order_ref[...]
    for i in range(2):
        for j in range(2):
            row = off_ref[i, j, 0]
            col = (off_ref[i, j, 1] + (32 if j == 0 else 224)) % WIN
            for channel in range(2):
                turned = pltpu.roll(probe_ref[channel], row, 0)
                probes_ref[2 * i + j, channel] = pltpu.roll(turned, col, 1)
            amp = amp_ref[i * WIN : (i + 1) * WIN, j * WIN : (j + 1) * WIN]
            high, rest = split(amp)
            middle, _ = split(amp - high.astype(F32) - rest.astype(F32))
            sorted_lanes = mul(high, order) + mul(rest, order) + mul(middle, order)
            for q in range(2):
                parts_ref[...] = sorted_lanes[:, q * HALF : (q + 1) * HALF]
                for p in range(2):
                    at = q * WIN + p * HALF
                    amps_ref[2 * i + j, at : at + HALF, :] = parts_ref[pl.ds(p, HALF, stride=2), :]


def prepare(offsets, probe, amplitudes, order):
    return pl.pallas_call(
        prepare_kernel,
        out_shape=(
            jax.ShapeDtypeStruct((4, 2, WIN, WIN), F32),
            jax.ShapeDtypeStruct((4, 2 * WIN, HALF), F32),
        ),
        in_specs=[pl.BlockSpec(memory_space=pltpu.SMEM)] + vmem(3),
        out_specs=tuple(vmem(2)),
        scratch_shapes=[pltpu.VMEM((WIN, HALF), F32)],
        cost_estimate=COST,
        compiler_params=pltpu.CompilerParams(vmem_limit_bytes=VMEM_LIMIT),
        name="prepare",
    )(offsets, probe, amplitudes, order)


def rows_of(pieces, refs, first, rows):
    found, at = [], 0
    for ref, (start, count, sides) in zip(refs, pieces):
        lo, hi = max(first, at), min(first + rows, at + count)
        if lo < hi:
            found.append((ref, start + lo - at, hi - lo, sides))
        at += count
    return found


def window_kernel(i, near, side, own, carried_own, carried_side, outs, *refs):
    off_ref, tab_ref, tw_ref, probes_ref, amps_ref = refs[:5]
    refs = refs[5:]
    side_refs, refs = refs[: len(side)], refs[len(side) :]
    own_refs, refs = refs[: len(own)], refs[len(own) :]
    sum_refs, refs = refs[: len(carried_own)], refs[len(carried_own) :]
    strip_refs, refs = refs[: len(carried_side)], refs[len(carried_side) :]
    out_refs, refs = refs[: 2 * len(outs)], refs[2 * len(outs) :]
    halves = [refs[n : n + 2] for n in range(0, 16, 2)]
    g_in, h_in, m_in, g_out = halves[0:2], halves[2:4], halves[4:6], halves[6:8]
    wide, tall, tall_back, wide_back = refs[16:18], refs[18:20], refs[20:22], refs[22:24]

    to_right = even_column() if near else jnp.logical_not(even_column())
    j = jnp.where(to_right, 1, 0)
    number = 2 * i + j
    row_start = off_ref[i, j, 0]
    col_start = off_ref[i, j, 1]
    row_iota = lax.broadcasted_iota(jnp.int32, (HALF, HALF), 0)
    lane_iota = lax.broadcasted_iota(jnp.int32, (HALF, HALF), 1)
    in_row = row_iota >= row_start
    sign = jnp.where(to_right, -1, 1)
    in_first = (
        sign * lane_iota >= jnp.where(to_right, 33 - col_start, 32 + col_start),
        lane_iota >= jnp.where(to_right, 96 + col_start, col_start - 96),
    )
    first_h, first_l, second_h, second_l = (tab_ref.at[n] for n in range(4))
    groups = (("strip", 1), (0, 2))

    def place(group):
        if group == "strip":
            return True, slice(0, LANE)
        return False, slice(group * LANE, (group + 1) * LANE)

    def load(channel, first, group):
        is_strip, lanes = place(group)
        pieces, sources = (side, side_refs) if is_strip else (own, own_refs)
        blocks = [
            kept(ref[channel, at : at + rows, lanes], *sides)
            for ref, at, rows, sides in rows_of(pieces, sources, first, HALF)
        ]
        return blocks[0] if len(blocks) == 1 else jnp.concatenate(blocks, axis=0)

    def emit(channel, first, group, value):
        is_strip, lanes = place(group)
        extra = (carried_side, strip_refs) if is_strip else (carried_own, sum_refs)
        which = 1 if is_strip else 0
        for n, (start, count) in enumerate(outs):
            lo, hi = max(first, start), min(first + HALF, start + count)
            if lo >= hi:
                continue
            cuts = sorted({lo, hi} | {c for at, rows in extra[0] for c in (at, at + rows) if lo < c < hi})
            for a, b in zip(cuts, cuts[1:]):
                part = value[a - first : b - first]
                for (at, rows), ref in zip(*extra):
                    if at <= a and b <= at + rows:
                        part = part + ref[channel, a - at : b - at, lanes]
                out_refs[2 * n + which][channel, a - start : b - start, lanes] = part

    def store_split(pair, rows, lanes, value):
        high, low = split(value)
        pair[0][rows, lanes] = high
        pair[1][rows, lanes] = low

    lo, hi = slice(0, HALF), slice(HALF, WIN)
    tw_c, tw_s = tw_ref[0], tw_ref[1]
    for cb in range(2):
        in_col = in_first[cb]
        first_group, second_group = groups[cb]
        field = []
        for rb in range(2):
            value = []
            for channel in range(2):
                at = rb * HALF
                picked = jnp.where(in_col, load(channel, at, first_group), load(channel, at, second_group))
                if rb == 0:
                    other = jnp.where(in_col, load(channel, WIN, first_group), load(channel, WIN, second_group))
                    picked = jnp.where(in_row, picked, other)
                value.append(picked)
            box = (slice(rb * HALF, (rb + 1) * HALF), slice(cb * LANE, (cb + 1) * LANE))
            p_re = probes_ref[(number, 0) + box]
            p_im = probes_ref[(number, 1) + box]
            field.append((p_re * value[0] - p_im * value[1], p_re * value[1] + p_im * value[0]))
        (re0, im0), (re1, im1) = field
        store_split(g_in[cb], lo, lo, re0 + re1)
        store_split(g_in[cb], hi, lo, im0 + im1)
        d_re = re0 - re1
        d_im = im0 - im1
        store_split(g_in[cb], lo, hi, d_re * tw_c + d_im * tw_s)
        store_split(g_in[cb], hi, hi, d_im * tw_c - d_re * tw_s)
        high, low = g_in[cb][0][...], g_in[cb][1][...]
        wide[cb][...] = mul(first_h[...], high) + mul(first_h[...], low) + mul(first_l[...], high)

    for p in range(2):
        tl_c, tl_s = tw_ref[2], tw_ref[3]
        cols = slice(p * HALF, (p + 1) * HALF)
        re0, re1 = wide[0][lo, cols], wide[1][lo, cols]
        im0, im1 = wide[0][hi, cols], wide[1][hi, cols]
        store_split(h_in[p], lo, lo, re0 + re1)
        store_split(h_in[p], lo, hi, im0 + im1)
        d_re = re0 - re1
        d_im = im0 - im1
        store_split(h_in[p], hi, lo, d_re * tl_c + d_im * tl_s)
        store_split(h_in[p], hi, hi, d_im * tl_c - d_re * tl_s)
        high, low = h_in[p][0][...], h_in[p][1][...]
        tall[p][...] = mul(high, second_h[...]) + mul(low, second_h[...]) + mul(high, second_l[...])

    for p in range(2):
        for q, rows in enumerate((lo, hi)):
            re, im = tall[p][rows, lo], tall[p][rows, hi]
            power = jnp.maximum(re * re + im * im, amp_floor * amp_floor)
            at = q * WIN + p * HALF
            keeping = 1.0 - amps_ref[number, at : at + HALF, :] * lax.rsqrt(power)
            store_split(m_in[p], rows, lo, re * keeping)
            store_split(m_in[p], rows, hi, im * keeping)
        high, low = m_in[p][0][...], m_in[p][1][...]
        tall_back[p][...] = mul(high, first_h[...]) + mul(low, first_h[...]) + mul(high, first_l[...])

    for p in range(2):
        tl_c, tl_s = tw_ref[2], tw_ref[3]
        u_re, u_im = tall_back[p][lo, lo], tall_back[p][lo, hi]
        v_re, v_im = tall_back[p][hi, lo], tall_back[p][hi, hi]
        w_re = v_re * tl_c - v_im * tl_s
        w_im = v_im * tl_c + v_re * tl_s
        store_split(g_out[p], lo, lo, u_re + w_re)
        store_split(g_out[p], lo, hi, u_re - w_re)
        store_split(g_out[p], hi, lo, u_im + w_im)
        store_split(g_out[p], hi, hi, u_im - w_im)
        high, low = g_out[p][0][...], g_out[p][1][...]
        wide_back[p][...] = mul(second_h[...], high) + mul(second_h[...], low) + mul(second_l[...], high)

    for cb in range(2):
        in_col = in_first[cb]
        first_group, second_group = groups[cb]
        cols = slice(cb * LANE, (cb + 1) * LANE)
        u_re, u_im = wide_back[0][lo, cols], wide_back[0][hi, cols]
        v_re, v_im = wide_back[1][lo, cols], wide_back[1][hi, cols]
        w_re = v_re * tw_c - v_im * tw_s
        w_im = v_im * tw_c + v_re * tw_s
        for rb in range(2):
            b_re = u_re + w_re if rb == 0 else u_re - w_re
            b_im = u_im + w_im if rb == 0 else u_im - w_im
            box = (slice(rb * HALF, (rb + 1) * HALF), cols)
            p_re = probes_ref[(number, 0) + box]
            p_im = probes_ref[(number, 1) + box]
            grads = (p_re * b_re + p_im * b_im, p_re * b_im - p_im * b_re)
            for channel in range(2):
                grad = grads[channel]
                targets = [(rb * HALF, grad)]
                if rb == 0:
                    targets = [(0, jnp.where(in_row, grad, 0.0)), (WIN, jnp.where(in_row, 0.0, grad))]
                for at, piece in targets:
                    emit(channel, at, first_group, jnp.where(in_col, piece, 0.0))
                    emit(channel, at, second_group, jnp.where(in_col, 0.0, piece))


def window(i, near, consts, side, own, carried_own, carried_side, outs):
    border = () if near else ("beside",)
    own_width = 3 * LANE
    shapes = []
    for _, rows in outs:
        shapes += [jax.ShapeDtypeStruct((2, rows, width), F32) for width in (own_width, LANE)]
    operands = [piece[0] for piece in list(side) + list(own) + list(carried_own) + list(carried_side)]
    kernel = functools.partial(
        window_kernel,
        i,
        near,
        tuple((p[1], p[2], p[3:] + border) for p in side),
        tuple((p[1], p[2], p[3:]) for p in own),
        tuple((at, array.shape[1]) for array, at in carried_own),
        tuple((at, array.shape[1]) for array, at in carried_side),
        outs,
    )
    return pl.pallas_call(
        kernel,
        out_shape=tuple(shapes),
        in_specs=[pl.BlockSpec(memory_space=pltpu.SMEM)] + vmem(4 + len(operands)),
        out_specs=tuple(vmem(len(shapes))),
        scratch_shapes=[pltpu.VMEM((WIN, WIN), BF16)] * 16 + [pltpu.VMEM((WIN, WIN), F32)] * 8,
        cost_estimate=COST,
        compiler_params=pltpu.CompilerParams(vmem_limit_bytes=VMEM_LIMIT),
    )(*consts, *operands)


def variation_kernel(near, own, far, *refs):
    reg = refs[-1]
    out_ref = refs[-2]
    near_refs, refs = refs[: len(near)], refs[len(near) :]
    own_refs, far_refs = refs[: len(own)], refs[len(own) : len(own) + len(far)]
    even = even_column()

    def block(pieces, sources, at, channel):
        first, rows, sides = pieces[at]
        return kept(sources[at][channel, first : first + rows, :], *sides)

    row = 0
    for n, (_, rows, _) in enumerate(own):
        for channel in range(2):
            span = slice(row, row + rows)
            one = block(near, near_refs, n, channel)
            other = block(far, far_refs, n, channel)
            reg[channel, span, LANE : 4 * LANE] = block(own, own_refs, n, channel)
            reg[channel, span, :LANE] = jnp.where(even, other, one)
            reg[channel, span, 4 * LANE :] = jnp.where(even, one, other)
        row += rows

    def chunk(step, _):
        base = pl.multiple_of(step * 32, 8)
        flows = []
        power = tv_smooth
        for channel in range(2):
            block = reg[channel, pl.ds(base, 48), :]
            down = pltpu.roll(block, 47, 0) - block
            right = pltpu.roll(block, 5 * LANE - 1, 1) - block
            power = power + down * down + right * right
            flows.append((down, right))
        inverse = lax.rsqrt(power)
        for channel in range(2):
            down, right = flows[channel]
            down = down * inverse
            right = right * inverse
            change = pltpu.roll(down, 1, 0) - down + pltpu.roll(right, 1, 1) - right
            out_ref[channel, pl.ds(base, 32), :] = tv_weight * change[8:40, LANE : 4 * LANE]
        return 0

    lax.fori_loop(0, 6, chunk, 0)


def variation(near, own, far):
    parts = (near, own, far)
    plan = [
        tuple((p[1], p[2], p[3:] + border) for p in part) for part, border in zip(parts, ((), (), ("beside",)))
    ]
    operands = [piece[0] for part in parts for piece in part]
    return pl.pallas_call(
        functools.partial(variation_kernel, *plan),
        out_shape=jax.ShapeDtypeStruct((2, 192, 3 * LANE), F32),
        in_specs=vmem(len(operands)),
        out_specs=pl.BlockSpec(memory_space=pltpu.VMEM),
        scratch_shapes=[pltpu.VMEM((2, 208, 5 * LANE), F32)],
        cost_estimate=COST,
        compiler_params=pltpu.CompilerParams(vmem_limit_bytes=VMEM_LIMIT),
        name="variation",
    )(*operands)


def totals_kernel(outs, extras, own_ref, near_ref, far_ref, *refs):
    added, out_refs = refs[: len(extras)], refs[len(extras) :]
    even = even_column()
    for (first, rows), out in zip(outs, out_refs):
        cuts = {first, first + rows}
        for at, count, _ in extras:
            cuts |= {c for c in (at, at + count) if first < c < first + rows}
        cuts = sorted(cuts)
        for a, b in zip(cuts, cuts[1:]):
            for channel in range(2):
                value = own_ref[channel, a:b, :]
                for (at, count, source), ref in zip(extras, added):
                    if at <= a and b <= at + count:
                        value = value + ref[channel, source + a - at : source + b - at, :]
                to = slice(a - first, b - first)
                one = near_ref[channel, a:b, :]
                other = kept(far_ref[channel, a:b, :], "beside")
                out[channel, to, :LANE] = value[:, :LANE] + jnp.where(even, other, one)
                out[channel, to, LANE : 2 * LANE] = value[:, LANE : 2 * LANE]
                out[channel, to, 2 * LANE :] = value[:, 2 * LANE :] + jnp.where(even, one, other)


def totals(own, near, far, outs, extras):
    plan = tuple((at, rows, source) for _, source, at, rows in extras)
    return pl.pallas_call(
        functools.partial(totals_kernel, outs, plan),
        out_shape=tuple(jax.ShapeDtypeStruct((2, rows, own.shape[2]), F32) for _, rows in outs),
        in_specs=vmem(3 + len(extras)),
        out_specs=tuple(vmem(len(outs))),
        cost_estimate=COST,
        compiler_params=pltpu.CompilerParams(vmem_limit_bytes=VMEM_LIMIT),
        name="totals",
    )(own, near, far, *[extra[0] for extra in extras])


def update_kernel(pieces, side, *refs):
    new, near, far = refs[-3:]
    even = even_column()
    ins = refs[:-3]
    row = 0
    for which, first, rows, grads, masked in pieces:
        for channel in range(2):
            total = None
            for grad, at in grads:
                term = ins[grad][channel, at : at + rows, :]
                if grad == len(ins) - 1:
                    term = kept(term, side)
                total = term if total is None else total + term
            value = ins[which][channel, first : first + rows, :] - step_size * total
            if masked:
                value = kept(value, side)
            new[channel, row : row + rows, :] = value
            near[channel, row : row + rows, :] = jnp.where(even, value[:, 2 * LANE :], value[:, :LANE])
            far[channel, row : row + rows, :] = jnp.where(even, value[:, :LANE], value[:, 2 * LANE :])
        row += rows


def update(operands, pieces, side):
    rows = sum(piece[2] for piece in pieces)
    shape = [jax.ShapeDtypeStruct((2, rows, width), F32) for width in (3 * LANE, LANE, LANE)]
    return pl.pallas_call(
        functools.partial(update_kernel, pieces, side),
        out_shape=tuple(shape),
        in_specs=vmem(len(operands)),
        out_specs=tuple(vmem(3)),
        cost_estimate=COST,
        compiler_params=pltpu.CompilerParams(vmem_limit_bytes=VMEM_LIMIT),
        name="update",
    )(*operands)


def near_kernel(own_ref, near_ref, out_ref):
    even = even_column()
    for channel in range(2):
        strip = near_ref[channel]
        out_ref[channel, :, :LANE] = own_ref[channel, :, :LANE] + jnp.where(even, 0.0, strip)
        out_ref[channel, :, LANE : 2 * LANE] = own_ref[channel, :, LANE : 2 * LANE]
        out_ref[channel, :, 2 * LANE :] = own_ref[channel, :, 2 * LANE :] + jnp.where(even, strip, 0.0)


def sums_near(own, near):
    return (
        pl.pallas_call(
            near_kernel,
            out_shape=jax.ShapeDtypeStruct(own.shape, F32),
            in_specs=vmem(2),
            out_specs=pl.BlockSpec(memory_space=pltpu.VMEM),
            cost_estimate=COST,
            compiler_params=pltpu.CompilerParams(vmem_limit_bytes=VMEM_LIMIT),
            name="sums_near",
        )(own, near),
    )


def finish_kernel(top_ref, bottom_ref, mid_ref, low_ref, above_ref, below_ref, corner_ref, out_ref):
    for channel in range(2):
        above = mid_ref[channel, :MARGIN, :] + kept(above_ref[channel], "above")
        out_ref[channel, :MARGIN, :] = top_ref[channel, MARGIN:, :] - step_size * above
        out_ref[channel, MARGIN:288, :] = bottom_ref[channel, :192, :] - step_size * mid_ref[channel, MARGIN:, :]
        base = bottom_ref[channel, 192:288, :] - step_size * (low_ref[channel] + kept(below_ref[channel], "below"))
        corner = step_size * kept(corner_ref[channel], "below", "beside")
        even = even_column()
        out_ref[channel, 288:, :LANE] = base[:, :LANE] - jnp.where(even, corner, 0.0)
        out_ref[channel, 288:, LANE : 2 * LANE] = base[:, LANE : 2 * LANE]
        out_ref[channel, 288:, 2 * LANE :] = base[:, 2 * LANE :] - jnp.where(even, 0.0, corner)


def finish(*operands):
    return pl.pallas_call(
        finish_kernel,
        out_shape=jax.ShapeDtypeStruct((2, 3 * LANE, 3 * LANE), F32),
        in_specs=vmem(len(operands)),
        out_specs=pl.BlockSpec(memory_space=pltpu.VMEM),
        cost_estimate=COST,
        compiler_params=pltpu.CompilerParams(vmem_limit_bytes=VMEM_LIMIT),
        name="finish",
    )(*operands)


def moved(block, axis, distance):
    count = lax.axis_size(axis)
    return lax.ppermute(block, axis, [(n, (n + distance) % count) for n in range(count)])


def to_near(block):
    rows, cols = lax.axis_size("row"), lax.axis_size("col")
    return lax.ppermute(block, ("row", "col"), [(r * cols + c, r * cols + (c ^ 1)) for r in range(rows) for c in range(cols)])


def to_far(block, ends=True):
    rows, cols = lax.axis_size("row"), lax.axis_size("col")
    route = []
    for r in range(rows):
        for c in range(cols):
            other = c - 1 if c % 2 == 0 else c + 1
            if ends or 0 <= other < cols:
                route.append((r * cols + c, r * cols + other % cols))
    return lax.ppermute(block, ("row", "col"), route)


def to_far_above(block):
    rows, cols = lax.axis_size("row"), lax.axis_size("col")
    route = []
    for r in range(rows):
        for c in range(cols):
            other = c - 1 if c % 2 == 0 else c + 1
            route.append((r * cols + c, (r - 1) % rows * cols + other % cols))
    return lax.ppermute(block, ("row", "col"), route)


def edges(block):
    width = block.shape[2]
    low, high = block[:, :, :LANE], block[:, :, width - LANE :]
    even = even_column()
    return jnp.where(even, high, low), jnp.where(even, low, high)


def on_device(table, twiddle, order, object_field, probe, amplitudes, offsets):
    tile = object_field.shape[1]
    last = tile - MARGIN
    band = 2 * MARGIN
    obj = object_field
    after = lax.optimization_barrier

    top = moved(obj[:, last:, :], "row", 1)
    near_strip, far_strip = edges(obj)
    far, near = to_far(far_strip), to_near(near_strip)
    up_rows, top = after((obj[:, :MARGIN, :], top))
    bottom = moved(up_rows, "row", -1)
    probes, amps = prepare(offsets, probe, amplitudes, order)
    consts = (offsets, table, twiddle, probes, amps)

    near_strip, far_strip = edges(top)
    top_b, top_a = to_far(far_strip), to_near(near_strip)
    own = [(top, 0, MARGIN, "above"), (obj, 0, last)]
    halves = ((0, band), (band, band))
    lo_o, lo_a, mid_o, mid_a = window(
        0, True, consts, [(top_a, 0, MARGIN, "above"), (near, 0, last)], own, [], [], halves
    )
    in_a = to_near(lo_a)
    lo_o, lo_b, mid_o, mid_b = window(
        0, False, consts, [(top_b, 0, MARGIN, "above"), (far, 0, last)], own, [(lo_o, 0), (mid_o, band)], [], halves
    )
    in_b = to_far(lo_b)
    bottom, lo_b = after((bottom, lo_b))
    near_strip, far_strip = edges(bottom)
    bot_b = to_far(far_strip)
    bot_a = to_near(near_strip)
    tv_top = variation(
        [(top_a, 88, 8, "above"), (near, 0, 200)],
        [(top, 88, 8, "above"), (obj, 0, 200)],
        [(top_b, 88, 8, "above"), (far, 0, 200)],
    )
    own = [(obj, MARGIN, last), (bottom, 0, MARGIN, "below")]
    whole = ((0, tile),)
    hi_o, hi_a = window(
        1, True, consts, [(near, MARGIN, last), (bot_a, 0, MARGIN, "below")], own, [(mid_o, 0)], [(mid_a, 0)], whole,
    )
    lo_o, hi_o = after((lo_o, hi_o))
    (top_sum,) = totals(lo_o, in_a, in_b, ((0, band),), [(tv_top, 0, MARGIN, MARGIN)])
    from_below = moved(top_sum, "row", -1)
    in_a = to_near(hi_a)
    hi_o, hi_b = window(
        1, False, consts, [(far, MARGIN, last), (bot_b, 0, MARGIN, "below")], own, [(hi_o, 0)], [(mid_b, 0)], whole,
    )
    in_b = to_far(hi_b, ends=False)
    tv_bottom = variation(
        [(near, 184, 200), (bot_a, 0, 8, "below")],
        [(obj, 184, 200), (bottom, 0, 8, "below")],
        [(far, 184, 200), (bot_b, 0, 8, "below")],
    )
    mid_sum, bot_sum = totals(
        hi_o, in_a, in_b, halves, [(tv_top, MARGIN, 0, MARGIN), (tv_bottom, 0, MARGIN, band)]
    )

    bot_sum, from_below = after((bot_sum, from_below))
    low, near_strip, far_strip = update(
        (obj, bottom, mid_sum, bot_sum, from_below),
        (
            (0, MARGIN, band, ((2, 0),), False),
            (0, last, MARGIN, ((3, 0), (4, 0)), False),
            (1, 0, MARGIN, ((3, MARGIN), (4, MARGIN)), True),
        ),
        "below",
    )
    low_a = to_near(near_strip)
    low_b = to_far(far_strip, ends=False)
    from_above = moved(bot_sum, "row", 1)
    own = [(low, 0, tile)]
    mid_o, mid_a, hi_o, hi_a = window(1, True, consts, [(low_a, 0, tile)], own, [], [], halves)
    in_a = to_near(hi_a)
    mid_o, mid_b, hi_o, hi_b = window(
        1, False, consts, [(low_b, 0, tile)], own, [(mid_o, 0), (hi_o, band)], [], halves
    )
    hi_in_b = to_far(hi_b)
    hi_in_a = in_a
    tv_bottom = variation([(low_a, 88, 208)], [(low, 88, 208)], [(low_b, 88, 208)])
    top, hi_b = after((top, hi_b))
    up, near_strip, far_strip = update(
        (top, obj, top_sum, from_above),
        (
            (0, 0, MARGIN, ((2, 0), (3, 0)), True),
            (1, 0, MARGIN, ((2, MARGIN), (3, MARGIN)), False),
        ),
        "above",
    )
    up_b, up_a = to_far(far_strip), to_near(near_strip)
    own = [(up, 0, band), (low, 0, band)]
    cut = ((0, MARGIN), (MARGIN, last))
    over_o, over_a, lo_o, lo_a = window(
        0, True, consts, [(up_a, 0, band), (low_a, 0, band)], own, [(mid_o, band)], [(mid_a, band)], cut
    )
    over_a, in_a = to_near(over_a), to_near(lo_a)
    lo_o, hi_o = after((lo_o, hi_o))
    low_sum, over = totals(
        hi_o, hi_in_a, hi_in_b, ((0, MARGIN), (MARGIN, MARGIN)), [(tv_bottom, MARGIN, 0, MARGIN)]
    )
    lo_o, over = after((lo_o, over))
    last_above = moved(over, "row", 1)
    over_o, over_b, lo_o, lo_b = window(
        0, False, consts, [(up_b, 0, band), (low_b, 0, band)], own, [(over_o, 0), (lo_o, MARGIN)], [(mid_b, band)], cut,
    )
    (over,) = sums_near(over_o, over_a)
    last_below = moved(over, "row", -1)
    corner = to_far_above(over_b)
    in_b = to_far(lo_b)
    tv_top = variation(
        [(up_a, 88, 104), (low_a, 0, 104)], [(up, 88, 104), (low, 0, 104)], [(up_b, 88, 104), (low_b, 0, 104)]
    )
    (mid_sum,) = totals(lo_o, in_a, in_b, ((0, last),), [(tv_top, 0, 0, band), (tv_bottom, 0, band, MARGIN)])
    return finish(up, low, mid_sum, low_sum, last_above, last_below, corner)


def solution(mesh):
    table, twiddle, order = tables()
    body = jax.shard_map(
        on_device,
        mesh=mesh,
        in_specs=(P(), P(), P(), P(None, "row", "col"), P(), P("row", "col"), P("row", "col", None)),
        out_specs=P(None, "row", "col"),
        check_vma=False,
    )

    def step(object_field, probe, amplitudes, offsets):
        return body(table, twiddle, order, object_field, probe, amplitudes, offsets)

    return step
```

```python
import functools
import math

import jax
import jax.numpy as jnp
import numpy as np
from jax import lax
from jax.experimental import pallas as pl
from jax.experimental.pallas import tpu as pltpu
from jax.sharding import PartitionSpec as P


WIN = 256
HALF = 128
MARGIN = 96
LANE = 128
COST = pl.CostEstimate(flops=100_000, bytes_accessed=100_000, transcendentals=0)
VMEM_LIMIT = 24 * 1024 * 1024

step_size = 0.3
tv_weight = 0.2
tv_smooth = 0.1
amp_floor = 0.5

F32 = jnp.float32
BF16 = jnp.bfloat16


def tables():
    counter = np.arange(HALF)
    angle = (counter[:, None] * counter[None, :] % HALF) * (2.0 * math.pi / HALF)
    cosine = np.cos(angle) / math.sqrt(WIN)
    sine = np.sin(angle) / math.sqrt(WIN)
    first = np.block([[cosine, sine], [-sine, cosine]])
    second = np.block([[cosine, -sine], [sine, cosine]])
    parts = []
    for table in (first, second):
        table = table.astype(np.float32)
        high = table.astype(jnp.bfloat16)
        low = (table - high.astype(np.float32)).astype(jnp.bfloat16)
        parts += [high, low]
    turn = counter * (2.0 * math.pi / WIN)
    rows = np.stack([np.cos(turn), np.sin(turn)])
    by_row = np.broadcast_to(rows[:, :, None], (2, HALF, HALF))
    by_lane = np.broadcast_to(rows[:, None, :], (2, HALF, HALF))
    twiddle = np.concatenate([by_row, by_lane]).astype(np.float32)
    order = np.zeros((WIN, WIN), np.float32)
    for parity in range(2):
        order[2 * counter + parity, parity * HALF + counter] = 1.0
    return np.stack(parts), twiddle, order.astype(jnp.bfloat16)


def split(value):
    high = value.astype(BF16)
    return high, (value - high.astype(F32)).astype(BF16)


def has(side):
    if side == "above":
        return lax.axis_index("row") > 0
    if side == "below":
        return lax.axis_index("row") < lax.axis_size("row") - 1
    return (lax.axis_index("col") > 0) & (lax.axis_index("col") < lax.axis_size("col") - 1)


def even_column():
    return lax.axis_index("col") % 2 == 0


def kept(value, *sides):
    for side in sides:
        value = jnp.where(has(side), value, 0.0)
    return value


def mul(left, right):
    return jnp.dot(left, right, preferred_element_type=F32)


def vmem(count):
    return [pl.BlockSpec(memory_space=pltpu.VMEM)] * count


def prepare_kernel(off_ref, probe_ref, amp_ref, order_ref, probes_ref, amps_ref, parts_ref):
    order = order_ref[...]
    for i in range(2):
        for j in range(2):
            row = off_ref[i, j, 0]
            col = (off_ref[i, j, 1] + (32 if j == 0 else 224)) % WIN
            for channel in range(2):
                turned = pltpu.roll(probe_ref[channel], row, 0)
                probes_ref[2 * i + j, channel] = pltpu.roll(turned, col, 1)
            amp = amp_ref[i * WIN : (i + 1) * WIN, j * WIN : (j + 1) * WIN]
            high, rest = split(amp)
            middle, _ = split(amp - high.astype(F32) - rest.astype(F32))
            sorted_lanes = mul(high, order) + mul(rest, order) + mul(middle, order)
            for q in range(2):
                parts_ref[...] = sorted_lanes[:, q * HALF : (q + 1) * HALF]
                for p in range(2):
                    at = q * WIN + p * HALF
                    amps_ref[2 * i + j, at : at + HALF, :] = parts_ref[pl.ds(p, HALF, stride=2), :]


def prepare(offsets, probe, amplitudes, order):
    return pl.pallas_call(
        prepare_kernel,
        out_shape=(
            jax.ShapeDtypeStruct((4, 2, WIN, WIN), F32),
            jax.ShapeDtypeStruct((4, 2 * WIN, HALF), F32),
        ),
        in_specs=[pl.BlockSpec(memory_space=pltpu.SMEM)] + vmem(3),
        out_specs=tuple(vmem(2)),
        scratch_shapes=[pltpu.VMEM((WIN, HALF), F32)],
        cost_estimate=COST,
        compiler_params=pltpu.CompilerParams(vmem_limit_bytes=VMEM_LIMIT),
        name="prepare",
    )(offsets, probe, amplitudes, order)


def rows_of(pieces, refs, first, rows):
    found, at = [], 0
    for ref, (start, count, sides) in zip(refs, pieces):
        lo, hi = max(first, at), min(first + rows, at + count)
        if lo < hi:
            found.append((ref, start + lo - at, hi - lo, sides))
        at += count
    return found


def window_kernel(i, near, side, own, carried_own, carried_side, outs, *refs):
    off_ref, tab_ref, tw_ref, probes_ref, amps_ref = refs[:5]
    refs = refs[5:]
    side_refs, refs = refs[: len(side)], refs[len(side) :]
    own_refs, refs = refs[: len(own)], refs[len(own) :]
    sum_refs, refs = refs[: len(carried_own)], refs[len(carried_own) :]
    strip_refs, refs = refs[: len(carried_side)], refs[len(carried_side) :]
    out_refs, refs = refs[: 2 * len(outs)], refs[2 * len(outs) :]
    halves = [refs[n : n + 2] for n in range(0, 16, 2)]
    g_in, h_in, m_in, g_out = halves[0:2], halves[2:4], halves[4:6], halves[6:8]
    wide, tall, tall_back, wide_back = refs[16:18], refs[18:20], refs[20:22], refs[22:24]

    to_right = even_column() if near else jnp.logical_not(even_column())
    j = jnp.where(to_right, 1, 0)
    number = 2 * i + j
    row_start = off_ref[i, j, 0]
    col_start = off_ref[i, j, 1]
    row_iota = lax.broadcasted_iota(jnp.int32, (HALF, HALF), 0)
    lane_iota = lax.broadcasted_iota(jnp.int32, (HALF, HALF), 1)
    in_row = row_iota >= row_start
    sign = jnp.where(to_right, -1, 1)
    in_first = (
        sign * lane_iota >= jnp.where(to_right, 33 - col_start, 32 + col_start),
        lane_iota >= jnp.where(to_right, 96 + col_start, col_start - 96),
    )
    first_h, first_l, second_h, second_l = (tab_ref.at[n] for n in range(4))
    groups = (("strip", 1), (0, 2))

    def place(group):
        if group == "strip":
            return True, slice(0, LANE)
        return False, slice(group * LANE, (group + 1) * LANE)

    def load(channel, first, group):
        is_strip, lanes = place(group)
        pieces, sources = (side, side_refs) if is_strip else (own, own_refs)
        blocks = [
            kept(ref[channel, at : at + rows, lanes], *sides)
            for ref, at, rows, sides in rows_of(pieces, sources, first, HALF)
        ]
        return blocks[0] if len(blocks) == 1 else jnp.concatenate(blocks, axis=0)

    def emit(channel, first, group, value):
        is_strip, lanes = place(group)
        extra = (carried_side, strip_refs) if is_strip else (carried_own, sum_refs)
        which = 1 if is_strip else 0
        for n, (start, count) in enumerate(outs):
            lo, hi = max(first, start), min(first + HALF, start + count)
            if lo >= hi:
                continue
            cuts = sorted({lo, hi} | {c for at, rows in extra[0] for c in (at, at + rows) if lo < c < hi})
            for a, b in zip(cuts, cuts[1:]):
                part = value[a - first : b - first]
                for (at, rows), ref in zip(*extra):
                    if at <= a and b <= at + rows:
                        part = part + ref[channel, a - at : b - at, lanes]
                out_refs[2 * n + which][channel, a - start : b - start, lanes] = part

    def store_split(pair, rows, lanes, value):
        high, low = split(value)
        pair[0][rows, lanes] = high
        pair[1][rows, lanes] = low

    lo, hi = slice(0, HALF), slice(HALF, WIN)
    tw_c, tw_s = tw_ref[0], tw_ref[1]
    for cb in range(2):
        in_col = in_first[cb]
        first_group, second_group = groups[cb]
        field = []
        for rb in range(2):
            value = []
            for channel in range(2):
                at = rb * HALF
                picked = jnp.where(in_col, load(channel, at, first_group), load(channel, at, second_group))
                if rb == 0:
                    other = jnp.where(in_col, load(channel, WIN, first_group), load(channel, WIN, second_group))
                    picked = jnp.where(in_row, picked, other)
                value.append(picked)
            box = (slice(rb * HALF, (rb + 1) * HALF), slice(cb * LANE, (cb + 1) * LANE))
            p_re = probes_ref[(number, 0) + box]
            p_im = probes_ref[(number, 1) + box]
            field.append((p_re * value[0] - p_im * value[1], p_re * value[1] + p_im * value[0]))
        (re0, im0), (re1, im1) = field
        store_split(g_in[cb], lo, lo, re0 + re1)
        store_split(g_in[cb], hi, lo, im0 + im1)
        d_re = re0 - re1
        d_im = im0 - im1
        store_split(g_in[cb], lo, hi, d_re * tw_c + d_im * tw_s)
        store_split(g_in[cb], hi, hi, d_im * tw_c - d_re * tw_s)
        high, low = g_in[cb][0][...], g_in[cb][1][...]
        wide[cb][...] = mul(first_h[...], high) + mul(first_h[...], low) + mul(first_l[...], high)

    for p in range(2):
        tl_c, tl_s = tw_ref[2], tw_ref[3]
        cols = slice(p * HALF, (p + 1) * HALF)
        re0, re1 = wide[0][lo, cols], wide[1][lo, cols]
        im0, im1 = wide[0][hi, cols], wide[1][hi, cols]
        store_split(h_in[p], lo, lo, re0 + re1)
        store_split(h_in[p], lo, hi, im0 + im1)
        d_re = re0 - re1
        d_im = im0 - im1
        store_split(h_in[p], hi, lo, d_re * tl_c + d_im * tl_s)
        store_split(h_in[p], hi, hi, d_im * tl_c - d_re * tl_s)
        high, low = h_in[p][0][...], h_in[p][1][...]
        tall[p][...] = mul(high, second_h[...]) + mul(low, second_h[...]) + mul(high, second_l[...])

    for p in range(2):
        for q, rows in enumerate((lo, hi)):
            re, im = tall[p][rows, lo], tall[p][rows, hi]
            power = jnp.maximum(re * re + im * im, amp_floor * amp_floor)
            at = q * WIN + p * HALF
            keeping = 1.0 - amps_ref[number, at : at + HALF, :] * lax.rsqrt(power)
            store_split(m_in[p], rows, lo, re * keeping)
            store_split(m_in[p], rows, hi, im * keeping)
        high, low = m_in[p][0][...], m_in[p][1][...]
        tall_back[p][...] = mul(high, first_h[...]) + mul(low, first_h[...]) + mul(high, first_l[...])

    for p in range(2):
        tl_c, tl_s = tw_ref[2], tw_ref[3]
        u_re, u_im = tall_back[p][lo, lo], tall_back[p][lo, hi]
        v_re, v_im = tall_back[p][hi, lo], tall_back[p][hi, hi]
        w_re = v_re * tl_c - v_im * tl_s
        w_im = v_im * tl_c + v_re * tl_s
        store_split(g_out[p], lo, lo, u_re + w_re)
        store_split(g_out[p], lo, hi, u_re - w_re)
        store_split(g_out[p], hi, lo, u_im + w_im)
        store_split(g_out[p], hi, hi, u_im - w_im)
        high, low = g_out[p][0][...], g_out[p][1][...]
        wide_back[p][...] = mul(second_h[...], high) + mul(second_h[...], low) + mul(second_l[...], high)

    for cb in range(2):
        in_col = in_first[cb]
        first_group, second_group = groups[cb]
        cols = slice(cb * LANE, (cb + 1) * LANE)
        u_re, u_im = wide_back[0][lo, cols], wide_back[0][hi, cols]
        v_re, v_im = wide_back[1][lo, cols], wide_back[1][hi, cols]
        w_re = v_re * tw_c - v_im * tw_s
        w_im = v_im * tw_c + v_re * tw_s
        for rb in range(2):
            b_re = u_re + w_re if rb == 0 else u_re - w_re
            b_im = u_im + w_im if rb == 0 else u_im - w_im
            box = (slice(rb * HALF, (rb + 1) * HALF), cols)
            p_re = probes_ref[(number, 0) + box]
            p_im = probes_ref[(number, 1) + box]
            grads = (p_re * b_re + p_im * b_im, p_re * b_im - p_im * b_re)
            for channel in range(2):
                grad = grads[channel]
                targets = [(rb * HALF, grad)]
                if rb == 0:
                    targets = [(0, jnp.where(in_row, grad, 0.0)), (WIN, jnp.where(in_row, 0.0, grad))]
                for at, piece in targets:
                    emit(channel, at, first_group, jnp.where(in_col, piece, 0.0))
                    emit(channel, at, second_group, jnp.where(in_col, 0.0, piece))


def window(i, near, consts, side, own, carried_own, carried_side, outs):
    border = () if near else ("beside",)
    own_width = 3 * LANE
    shapes = []
    for _, rows in outs:
        shapes += [jax.ShapeDtypeStruct((2, rows, width), F32) for width in (own_width, LANE)]
    operands = [piece[0] for piece in list(side) + list(own) + list(carried_own) + list(carried_side)]
    kernel = functools.partial(
        window_kernel,
        i,
        near,
        tuple((p[1], p[2], p[3:] + border) for p in side),
        tuple((p[1], p[2], p[3:]) for p in own),
        tuple((at, array.shape[1]) for array, at in carried_own),
        tuple((at, array.shape[1]) for array, at in carried_side),
        outs,
    )
    return pl.pallas_call(
        kernel,
        out_shape=tuple(shapes),
        in_specs=[pl.BlockSpec(memory_space=pltpu.SMEM)] + vmem(4 + len(operands)),
        out_specs=tuple(vmem(len(shapes))),
        scratch_shapes=[pltpu.VMEM((WIN, WIN), BF16)] * 16 + [pltpu.VMEM((WIN, WIN), F32)] * 8,
        cost_estimate=COST,
        compiler_params=pltpu.CompilerParams(vmem_limit_bytes=VMEM_LIMIT),
    )(*consts, *operands)


def variation_kernel(near, own, far, *refs):
    reg = refs[-1]
    out_ref = refs[-2]
    near_refs, refs = refs[: len(near)], refs[len(near) :]
    own_refs, far_refs = refs[: len(own)], refs[len(own) : len(own) + len(far)]
    even = even_column()

    def block(pieces, sources, at, channel):
        first, rows, sides = pieces[at]
        return kept(sources[at][channel, first : first + rows, :], *sides)

    row = 0
    for n, (_, rows, _) in enumerate(own):
        for channel in range(2):
            span = slice(row, row + rows)
            one = block(near, near_refs, n, channel)
            other = block(far, far_refs, n, channel)
            reg[channel, span, LANE : 4 * LANE] = block(own, own_refs, n, channel)
            reg[channel, span, :LANE] = jnp.where(even, other, one)
            reg[channel, span, 4 * LANE :] = jnp.where(even, one, other)
        row += rows

    def chunk(step, _):
        base = pl.multiple_of(step * 32, 8)
        flows = []
        power = tv_smooth
        for channel in range(2):
            block = reg[channel, pl.ds(base, 48), :]
            down = pltpu.roll(block, 47, 0) - block
            right = pltpu.roll(block, 5 * LANE - 1, 1) - block
            power = power + down * down + right * right
            flows.append((down, right))
        inverse = lax.rsqrt(power)
        for channel in range(2):
            down, right = flows[channel]
            down = down * inverse
            right = right * inverse
            change = pltpu.roll(down, 1, 0) - down + pltpu.roll(right, 1, 1) - right
            out_ref[channel, pl.ds(base, 32), :] = tv_weight * change[8:40, LANE : 4 * LANE]
        return 0

    lax.fori_loop(0, 6, chunk, 0)


def variation(near, own, far):
    parts = (near, own, far)
    plan = [
        tuple((p[1], p[2], p[3:] + border) for p in part) for part, border in zip(parts, ((), (), ("beside",)))
    ]
    operands = [piece[0] for part in parts for piece in part]
    return pl.pallas_call(
        functools.partial(variation_kernel, *plan),
        out_shape=jax.ShapeDtypeStruct((2, 192, 3 * LANE), F32),
        in_specs=vmem(len(operands)),
        out_specs=pl.BlockSpec(memory_space=pltpu.VMEM),
        scratch_shapes=[pltpu.VMEM((2, 208, 5 * LANE), F32)],
        cost_estimate=COST,
        compiler_params=pltpu.CompilerParams(vmem_limit_bytes=VMEM_LIMIT),
        name="variation",
    )(*operands)


def totals_kernel(outs, extras, own_ref, near_ref, far_ref, *refs):
    added, out_refs = refs[: len(extras)], refs[len(extras) :]
    even = even_column()
    for (first, rows), out in zip(outs, out_refs):
        cuts = {first, first + rows}
        for at, count, _ in extras:
            cuts |= {c for c in (at, at + count) if first < c < first + rows}
        cuts = sorted(cuts)
        for a, b in zip(cuts, cuts[1:]):
            for channel in range(2):
                value = own_ref[channel, a:b, :]
                for (at, count, source), ref in zip(extras, added):
                    if at <= a and b <= at + count:
                        value = value + ref[channel, source + a - at : source + b - at, :]
                to = slice(a - first, b - first)
                one = near_ref[channel, a:b, :]
                other = kept(far_ref[channel, a:b, :], "beside")
                out[channel, to, :LANE] = value[:, :LANE] + jnp.where(even, other, one)
                out[channel, to, LANE : 2 * LANE] = value[:, LANE : 2 * LANE]
                out[channel, to, 2 * LANE :] = value[:, 2 * LANE :] + jnp.where(even, one, other)


def totals(own, near, far, outs, extras):
    plan = tuple((at, rows, source) for _, source, at, rows in extras)
    return pl.pallas_call(
        functools.partial(totals_kernel, outs, plan),
        out_shape=tuple(jax.ShapeDtypeStruct((2, rows, own.shape[2]), F32) for _, rows in outs),
        in_specs=vmem(3 + len(extras)),
        out_specs=tuple(vmem(len(outs))),
        cost_estimate=COST,
        compiler_params=pltpu.CompilerParams(vmem_limit_bytes=VMEM_LIMIT),
        name="totals",
    )(own, near, far, *[extra[0] for extra in extras])


def update_kernel(pieces, side, *refs):
    new, near, far = refs[-3:]
    even = even_column()
    ins = refs[:-3]
    row = 0
    for which, first, rows, grads, masked in pieces:
        for channel in range(2):
            total = None
            for grad, at in grads:
                term = ins[grad][channel, at : at + rows, :]
                if grad == len(ins) - 1:
                    term = kept(term, side)
                total = term if total is None else total + term
            value = ins[which][channel, first : first + rows, :] - step_size * total
            if masked:
                value = kept(value, side)
            new[channel, row : row + rows, :] = value
            near[channel, row : row + rows, :] = jnp.where(even, value[:, 2 * LANE :], value[:, :LANE])
            far[channel, row : row + rows, :] = jnp.where(even, value[:, :LANE], value[:, 2 * LANE :])
        row += rows


def update(operands, pieces, side):
    rows = sum(piece[2] for piece in pieces)
    shape = [jax.ShapeDtypeStruct((2, rows, width), F32) for width in (3 * LANE, LANE, LANE)]
    return pl.pallas_call(
        functools.partial(update_kernel, pieces, side),
        out_shape=tuple(shape),
        in_specs=vmem(len(operands)),
        out_specs=tuple(vmem(3)),
        cost_estimate=COST,
        compiler_params=pltpu.CompilerParams(vmem_limit_bytes=VMEM_LIMIT),
        name="update",
    )(*operands)


def finish_kernel(top_ref, bottom_ref, mid_ref, low_ref, above_ref, below_ref, out_ref):
    for channel in range(2):
        above = mid_ref[channel, :MARGIN, :] + kept(above_ref[channel], "above")
        out_ref[channel, :MARGIN, :] = top_ref[channel, MARGIN:, :] - step_size * above
        out_ref[channel, MARGIN:288, :] = bottom_ref[channel, :192, :] - step_size * mid_ref[channel, MARGIN:, :]
        below = low_ref[channel] + kept(below_ref[channel], "below")
        out_ref[channel, 288:, :] = bottom_ref[channel, 192:288, :] - step_size * below


def finish(*operands):
    return pl.pallas_call(
        finish_kernel,
        out_shape=jax.ShapeDtypeStruct((2, 3 * LANE, 3 * LANE), F32),
        in_specs=vmem(len(operands)),
        out_specs=pl.BlockSpec(memory_space=pltpu.VMEM),
        cost_estimate=COST,
        compiler_params=pltpu.CompilerParams(vmem_limit_bytes=VMEM_LIMIT),
        name="finish",
    )(*operands)


def moved(block, axis, distance, ring=True):
    count = lax.axis_size(axis)
    route = [(n, (n + distance) % count) for n in range(count) if ring or 0 <= n + distance < count]
    return lax.ppermute(block, axis, route)


def to_near(block):
    rows, cols = lax.axis_size("row"), lax.axis_size("col")
    return lax.ppermute(block, ("row", "col"), [(r * cols + c, r * cols + (c ^ 1)) for r in range(rows) for c in range(cols)])


def to_far(block, ends=True):
    rows, cols = lax.axis_size("row"), lax.axis_size("col")
    route = []
    for r in range(rows):
        for c in range(cols):
            other = c - 1 if c % 2 == 0 else c + 1
            if ends or 0 <= other < cols:
                route.append((r * cols + c, r * cols + other % cols))
    return lax.ppermute(block, ("row", "col"), route)


def edges(block):
    width = block.shape[2]
    low, high = block[:, :, :LANE], block[:, :, width - LANE :]
    even = even_column()
    return jnp.where(even, high, low), jnp.where(even, low, high)


def on_device(table, twiddle, order, object_field, probe, amplitudes, offsets):
    tile = object_field.shape[1]
    last = tile - MARGIN
    band = 2 * MARGIN
    obj = object_field
    after = lax.optimization_barrier

    top = moved(obj[:, last:, :], "row", 1, ring=False)
    near_strip, far_strip = edges(obj)
    far, near = to_far(far_strip), to_near(near_strip)
    up_rows, top = after((obj[:, :MARGIN, :], top))
    bottom = moved(up_rows, "row", -1)
    probes, amps = prepare(offsets, probe, amplitudes, order)
    consts = (offsets, table, twiddle, probes, amps)

    near_strip, far_strip = edges(top)
    top_b, top_a = to_far(far_strip), to_near(near_strip)
    own = [(top, 0, MARGIN, "above"), (obj, 0, last)]
    halves = ((0, band), (band, band))
    lo_o, lo_a, mid_o, mid_a = window(
        0, True, consts, [(top_a, 0, MARGIN, "above"), (near, 0, last)], own, [], [], halves
    )
    in_a = to_near(lo_a)
    lo_o, lo_b, mid_o, mid_b = window(
        0, False, consts, [(top_b, 0, MARGIN, "above"), (far, 0, last)], own, [(lo_o, 0), (mid_o, band)], [], halves
    )
    in_b = to_far(lo_b)
    bottom, lo_b = after((bottom, lo_b))
    near_strip, far_strip = edges(bottom)
    bot_b, bot_a = to_far(far_strip), to_near(near_strip)
    tv_top = variation(
        [(top_a, 88, 8, "above"), (near, 0, 200)],
        [(top, 88, 8, "above"), (obj, 0, 200)],
        [(top_b, 88, 8, "above"), (far, 0, 200)],
    )
    (top_sum,) = totals(lo_o, in_a, in_b, ((0, band),), [(tv_top, 0, MARGIN, MARGIN)])
    from_below = moved(top_sum, "row", -1)

    mid_o, top_sum = after((mid_o, top_sum))
    own = [(obj, MARGIN, last), (bottom, 0, MARGIN, "below")]
    whole = ((0, tile),)
    hi_o, hi_b = window(
        1, False, consts, [(far, MARGIN, last), (bot_b, 0, MARGIN, "below")], own, [(mid_o, 0)], [(mid_b, 0)], whole,
    )
    in_b = to_far(hi_b, ends=False)
    hi_o, hi_a = window(
        1, True, consts, [(near, MARGIN, last), (bot_a, 0, MARGIN, "below")], own, [(hi_o, 0)], [(mid_a, 0)], whole,
    )
    in_a = to_near(hi_a)
    tv_bottom = variation(
        [(near, 184, 200), (bot_a, 0, 8, "below")],
        [(obj, 184, 200), (bottom, 0, 8, "below")],
        [(far, 184, 200), (bot_b, 0, 8, "below")],
    )
    mid_sum, bot_sum = totals(
        hi_o, in_a, in_b, halves, [(tv_top, MARGIN, 0, MARGIN), (tv_bottom, 0, MARGIN, band)]
    )
    from_above = moved(bot_sum, "row", 1)

    low, near_strip, far_strip = update(
        (obj, bottom, mid_sum, bot_sum, from_below),
        (
            (0, MARGIN, band, ((2, 0),), False),
            (0, last, MARGIN, ((3, 0), (4, 0)), False),
            (1, 0, MARGIN, ((3, MARGIN), (4, MARGIN)), True),
        ),
        "below",
    )
    low_a, low_b = to_near(near_strip), to_far(far_strip, ends=False)
    own = [(low, 0, tile)]
    mid_o, mid_a, hi_o, hi_a = window(1, True, consts, [(low_a, 0, tile)], own, [], [], halves)
    in_a = to_near(hi_a)
    mid_o, mid_b, hi_o, hi_b = window(
        1, False, consts, [(low_b, 0, tile)], own, [(mid_o, 0), (hi_o, band)], [], halves
    )
    hi_in_b = to_far(hi_b)
    hi_in_a = in_a
    tv_bottom = variation([(low_a, 88, 208)], [(low, 88, 208)], [(low_b, 88, 208)])
    top, hi_b = after((top, hi_b))
    up, near_strip, far_strip = update(
        (top, obj, top_sum, from_above),
        (
            (0, 0, MARGIN, ((2, 0), (3, 0)), True),
            (1, 0, MARGIN, ((2, MARGIN), (3, MARGIN)), False),
        ),
        "above",
    )
    up_b, up_a = to_far(far_strip), to_near(near_strip)
    own = [(up, 0, band), (low, 0, band)]
    cut = ((0, MARGIN), (MARGIN, last))
    over_o, over_a, lo_o, lo_a = window(
        0, True, consts, [(up_a, 0, band), (low_a, 0, band)], own, [(mid_o, band)], [(mid_a, band)], cut
    )
    over_a, in_a = to_near(over_a), to_near(lo_a)
    lo_o, hi_o = after((lo_o, hi_o))
    low_sum, over = totals(
        hi_o, hi_in_a, hi_in_b, ((0, MARGIN), (MARGIN, MARGIN)), [(tv_bottom, MARGIN, 0, MARGIN)]
    )
    lo_o, over = after((lo_o, over))
    last_above = moved(over, "row", 1)
    over_o, over_b, lo_o, lo_b = window(
        0, False, consts, [(up_b, 0, band), (low_b, 0, band)], own, [(over_o, 0), (lo_o, MARGIN)], [(mid_b, band)], cut,
    )
    over_b = to_far(over_b)
    (over,) = totals(over_o, over_a, over_b, ((0, MARGIN),), [])
    last_below = moved(over, "row", -1)
    in_b = to_far(lo_b)
    tv_top = variation(
        [(up_a, 88, 104), (low_a, 0, 104)], [(up, 88, 104), (low, 0, 104)], [(up_b, 88, 104), (low_b, 0, 104)]
    )
    (mid_sum,) = totals(lo_o, in_a, in_b, ((0, last),), [(tv_top, 0, 0, band), (tv_bottom, 0, band, MARGIN)])
    return finish(up, low, mid_sum, low_sum, last_above, last_below)


def solution(mesh):
    table, twiddle, order = tables()
    body = jax.shard_map(
        on_device,
        mesh=mesh,
        in_specs=(P(), P(), P(), P(None, "row", "col"), P(), P("row", "col"), P("row", "col", None)),
        out_specs=P(None, "row", "col"),
        check_vma=False,
    )

    def step(object_field, probe, amplitudes, offsets):
        return body(table, twiddle, order, object_field, probe, amplitudes, offsets)

    return step
```

```python
import functools
import math

import jax
import jax.numpy as jnp
import numpy as np
from jax import lax
from jax.experimental import pallas as pl
from jax.experimental.pallas import tpu as pltpu
from jax.sharding import PartitionSpec as P


WIN = 256
HALF = 128
MARGIN = 96
LANE = 128
COST = pl.CostEstimate(flops=100_000, bytes_accessed=100_000, transcendentals=0)
VMEM_LIMIT = 24 * 1024 * 1024

step_size = 0.3
tv_weight = 0.2
tv_smooth = 0.1
amp_floor = 0.5

F32 = jnp.float32
BF16 = jnp.bfloat16


def tables():
    counter = np.arange(HALF)
    angle = (counter[:, None] * counter[None, :] % HALF) * (2.0 * math.pi / HALF)
    cosine = np.cos(angle) / math.sqrt(WIN)
    sine = np.sin(angle) / math.sqrt(WIN)
    first = np.block([[cosine, sine], [-sine, cosine]])
    second = np.block([[cosine, -sine], [sine, cosine]])
    parts = []
    for table in (first, second):
        table = table.astype(np.float32)
        high = table.astype(jnp.bfloat16)
        low = (table - high.astype(np.float32)).astype(jnp.bfloat16)
        parts += [high, low]
    turn = counter * (2.0 * math.pi / WIN)
    rows = np.stack([np.cos(turn), np.sin(turn)])
    by_row = np.broadcast_to(rows[:, :, None], (2, HALF, HALF))
    by_lane = np.broadcast_to(rows[:, None, :], (2, HALF, HALF))
    twiddle = np.concatenate([by_row, by_lane]).astype(np.float32)
    order = np.zeros((WIN, WIN), np.float32)
    for parity in range(2):
        order[2 * counter + parity, parity * HALF + counter] = 1.0
    return np.stack(parts), twiddle, order.astype(jnp.bfloat16)


def split(value):
    high = value.astype(BF16)
    return high, (value - high.astype(F32)).astype(BF16)


def has(side):
    if side == "above":
        return lax.axis_index("row") > 0
    if side == "below":
        return lax.axis_index("row") < lax.axis_size("row") - 1
    return (lax.axis_index("col") > 0) & (lax.axis_index("col") < lax.axis_size("col") - 1)


def even_column():
    return lax.axis_index("col") % 2 == 0


def kept(value, *sides):
    for side in sides:
        value = jnp.where(has(side), value, 0.0)
    return value


def mul(left, right):
    return jnp.dot(left, right, preferred_element_type=F32)


def vmem(count):
    return [pl.BlockSpec(memory_space=pltpu.VMEM)] * count


def prepare_kernel(off_ref, probe_ref, amp_ref, order_ref, probes_ref, amps_ref, parts_ref):
    order = order_ref[...]
    for i in range(2):
        for j in range(2):
            row = off_ref[i, j, 0]
            col = (off_ref[i, j, 1] + (32 if j == 0 else 224)) % WIN
            for channel in range(2):
                turned = pltpu.roll(probe_ref[channel], row, 0)
                probes_ref[2 * i + j, channel] = pltpu.roll(turned, col, 1)
            amp = amp_ref[i * WIN : (i + 1) * WIN, j * WIN : (j + 1) * WIN]
            high, rest = split(amp)
            middle, _ = split(amp - high.astype(F32) - rest.astype(F32))
            sorted_lanes = mul(high, order) + mul(rest, order) + mul(middle, order)
            for q in range(2):
                parts_ref[...] = sorted_lanes[:, q * HALF : (q + 1) * HALF]
                for p in range(2):
                    at = q * WIN + p * HALF
                    amps_ref[2 * i + j, at : at + HALF, :] = parts_ref[pl.ds(p, HALF, stride=2), :]


def prepare(offsets, probe, amplitudes, order):
    return pl.pallas_call(
        prepare_kernel,
        out_shape=(
            jax.ShapeDtypeStruct((4, 2, WIN, WIN), F32),
            jax.ShapeDtypeStruct((4, 2 * WIN, HALF), F32),
        ),
        in_specs=[pl.BlockSpec(memory_space=pltpu.SMEM)] + vmem(3),
        out_specs=tuple(vmem(2)),
        scratch_shapes=[pltpu.VMEM((WIN, HALF), F32)],
        cost_estimate=COST,
        compiler_params=pltpu.CompilerParams(vmem_limit_bytes=VMEM_LIMIT),
        name="prepare",
    )(offsets, probe, amplitudes, order)


def rows_of(pieces, refs, first, rows):
    found, at = [], 0
    for ref, (start, count, sides) in zip(refs, pieces):
        lo, hi = max(first, at), min(first + rows, at + count)
        if lo < hi:
            found.append((ref, start + lo - at, hi - lo, sides))
        at += count
    return found


def window_kernel(i, near, side, own, carried_own, carried_side, outs, *refs):
    off_ref, tab_ref, tw_ref, probes_ref, amps_ref = refs[:5]
    refs = refs[5:]
    side_refs, refs = refs[: len(side)], refs[len(side) :]
    own_refs, refs = refs[: len(own)], refs[len(own) :]
    sum_refs, refs = refs[: len(carried_own)], refs[len(carried_own) :]
    strip_refs, refs = refs[: len(carried_side)], refs[len(carried_side) :]
    out_refs, refs = refs[: 2 * len(outs)], refs[2 * len(outs) :]
    halves = [refs[n : n + 2] for n in range(0, 16, 2)]
    g_in, h_in, m_in, g_out = halves[0:2], halves[2:4], halves[4:6], halves[6:8]
    wide, tall, tall_back, wide_back = refs[16:18], refs[18:20], refs[20:22], refs[22:24]

    to_right = even_column() if near else jnp.logical_not(even_column())
    j = jnp.where(to_right, 1, 0)
    number = 2 * i + j
    row_start = off_ref[i, j, 0]
    col_start = off_ref[i, j, 1]
    row_iota = lax.broadcasted_iota(jnp.int32, (HALF, HALF), 0)
    lane_iota = lax.broadcasted_iota(jnp.int32, (HALF, HALF), 1)
    in_row = row_iota >= row_start
    sign = jnp.where(to_right, -1, 1)
    in_first = (
        sign * lane_iota >= jnp.where(to_right, 33 - col_start, 32 + col_start),
        lane_iota >= jnp.where(to_right, 96 + col_start, col_start - 96),
    )
    first_h, first_l, second_h, second_l = (tab_ref.at[n] for n in range(4))
    groups = (("strip", 1), (0, 2))

    def place(group):
        if group == "strip":
            return True, slice(0, LANE)
        return False, slice(group * LANE, (group + 1) * LANE)

    def load(channel, first, group):
        is_strip, lanes = place(group)
        pieces, sources = (side, side_refs) if is_strip else (own, own_refs)
        blocks = [
            kept(ref[channel, at : at + rows, lanes], *sides)
            for ref, at, rows, sides in rows_of(pieces, sources, first, HALF)
        ]
        return blocks[0] if len(blocks) == 1 else jnp.concatenate(blocks, axis=0)

    def emit(channel, first, group, value):
        is_strip, lanes = place(group)
        extra = (carried_side, strip_refs) if is_strip else (carried_own, sum_refs)
        which = 1 if is_strip else 0
        for n, (start, count) in enumerate(outs):
            lo, hi = max(first, start), min(first + HALF, start + count)
            if lo >= hi:
                continue
            cuts = sorted({lo, hi} | {c for at, rows in extra[0] for c in (at, at + rows) if lo < c < hi})
            for a, b in zip(cuts, cuts[1:]):
                part = value[a - first : b - first]
                for (at, rows), ref in zip(*extra):
                    if at <= a and b <= at + rows:
                        part = part + ref[channel, a - at : b - at, lanes]
                out_refs[2 * n + which][channel, a - start : b - start, lanes] = part

    def store_split(pair, rows, lanes, value):
        high, low = split(value)
        pair[0][rows, lanes] = high
        pair[1][rows, lanes] = low

    lo, hi = slice(0, HALF), slice(HALF, WIN)
    tw_c, tw_s = tw_ref[0], tw_ref[1]
    for cb in range(2):
        in_col = in_first[cb]
        first_group, second_group = groups[cb]
        field = []
        for rb in range(2):
            value = []
            for channel in range(2):
                at = rb * HALF
                picked = jnp.where(in_col, load(channel, at, first_group), load(channel, at, second_group))
                if rb == 0:
                    other = jnp.where(in_col, load(channel, WIN, first_group), load(channel, WIN, second_group))
                    picked = jnp.where(in_row, picked, other)
                value.append(picked)
            box = (slice(rb * HALF, (rb + 1) * HALF), slice(cb * LANE, (cb + 1) * LANE))
            p_re = probes_ref[(number, 0) + box]
            p_im = probes_ref[(number, 1) + box]
            field.append((p_re * value[0] - p_im * value[1], p_re * value[1] + p_im * value[0]))
        (re0, im0), (re1, im1) = field
        store_split(g_in[cb], lo, lo, re0 + re1)
        store_split(g_in[cb], hi, lo, im0 + im1)
        d_re = re0 - re1
        d_im = im0 - im1
        store_split(g_in[cb], lo, hi, d_re * tw_c + d_im * tw_s)
        store_split(g_in[cb], hi, hi, d_im * tw_c - d_re * tw_s)
        high, low = g_in[cb][0][...], g_in[cb][1][...]
        wide[cb][...] = mul(first_h[...], high) + mul(first_h[...], low) + mul(first_l[...], high)

    for p in range(2):
        tl_c, tl_s = tw_ref[2], tw_ref[3]
        cols = slice(p * HALF, (p + 1) * HALF)
        re0, re1 = wide[0][lo, cols], wide[1][lo, cols]
        im0, im1 = wide[0][hi, cols], wide[1][hi, cols]
        store_split(h_in[p], lo, lo, re0 + re1)
        store_split(h_in[p], lo, hi, im0 + im1)
        d_re = re0 - re1
        d_im = im0 - im1
        store_split(h_in[p], hi, lo, d_re * tl_c + d_im * tl_s)
        store_split(h_in[p], hi, hi, d_im * tl_c - d_re * tl_s)
        high, low = h_in[p][0][...], h_in[p][1][...]
        tall[p][...] = mul(high, second_h[...]) + mul(low, second_h[...]) + mul(high, second_l[...])

    for p in range(2):
        for q, rows in enumerate((lo, hi)):
            re, im = tall[p][rows, lo], tall[p][rows, hi]
            power = jnp.maximum(re * re + im * im, amp_floor * amp_floor)
            at = q * WIN + p * HALF
            keeping = 1.0 - amps_ref[number, at : at + HALF, :] * lax.rsqrt(power)
            store_split(m_in[p], rows, lo, re * keeping)
            store_split(m_in[p], rows, hi, im * keeping)
        high, low = m_in[p][0][...], m_in[p][1][...]
        tall_back[p][...] = mul(high, first_h[...]) + mul(low, first_h[...]) + mul(high, first_l[...])

    for p in range(2):
        tl_c, tl_s = tw_ref[2], tw_ref[3]
        u_re, u_im = tall_back[p][lo, lo], tall_back[p][lo, hi]
        v_re, v_im = tall_back[p][hi, lo], tall_back[p][hi, hi]
        w_re = v_re * tl_c - v_im * tl_s
        w_im = v_im * tl_c + v_re * tl_s
        store_split(g_out[p], lo, lo, u_re + w_re)
        store_split(g_out[p], lo, hi, u_re - w_re)
        store_split(g_out[p], hi, lo, u_im + w_im)
        store_split(g_out[p], hi, hi, u_im - w_im)
        high, low = g_out[p][0][...], g_out[p][1][...]
        wide_back[p][...] = mul(second_h[...], high) + mul(second_h[...], low) + mul(second_l[...], high)

    for cb in range(2):
        in_col = in_first[cb]
        first_group, second_group = groups[cb]
        cols = slice(cb * LANE, (cb + 1) * LANE)
        u_re, u_im = wide_back[0][lo, cols], wide_back[0][hi, cols]
        v_re, v_im = wide_back[1][lo, cols], wide_back[1][hi, cols]
        w_re = v_re * tw_c - v_im * tw_s
        w_im = v_im * tw_c + v_re * tw_s
        for rb in range(2):
            b_re = u_re + w_re if rb == 0 else u_re - w_re
            b_im = u_im + w_im if rb == 0 else u_im - w_im
            box = (slice(rb * HALF, (rb + 1) * HALF), cols)
            p_re = probes_ref[(number, 0) + box]
            p_im = probes_ref[(number, 1) + box]
            grads = (p_re * b_re + p_im * b_im, p_re * b_im - p_im * b_re)
            for channel in range(2):
                grad = grads[channel]
                targets = [(rb * HALF, grad)]
                if rb == 0:
                    targets = [(0, jnp.where(in_row, grad, 0.0)), (WIN, jnp.where(in_row, 0.0, grad))]
                for at, piece in targets:
                    emit(channel, at, first_group, jnp.where(in_col, piece, 0.0))
                    emit(channel, at, second_group, jnp.where(in_col, 0.0, piece))


def window(i, near, consts, side, own, carried_own, carried_side, outs):
    border = () if near else ("beside",)
    own_width = 3 * LANE
    shapes = []
    for _, rows in outs:
        shapes += [jax.ShapeDtypeStruct((2, rows, width), F32) for width in (own_width, LANE)]
    operands = [piece[0] for piece in list(side) + list(own) + list(carried_own) + list(carried_side)]
    kernel = functools.partial(
        window_kernel,
        i,
        near,
        tuple((p[1], p[2], p[3:] + border) for p in side),
        tuple((p[1], p[2], p[3:]) for p in own),
        tuple((at, array.shape[1]) for array, at in carried_own),
        tuple((at, array.shape[1]) for array, at in carried_side),
        outs,
    )
    return pl.pallas_call(
        kernel,
        out_shape=tuple(shapes),
        in_specs=[pl.BlockSpec(memory_space=pltpu.SMEM)] + vmem(4 + len(operands)),
        out_specs=tuple(vmem(len(shapes))),
        scratch_shapes=[pltpu.VMEM((WIN, WIN), BF16)] * 16 + [pltpu.VMEM((WIN, WIN), F32)] * 8,
        cost_estimate=COST,
        compiler_params=pltpu.CompilerParams(vmem_limit_bytes=VMEM_LIMIT),
    )(*consts, *operands)


def variation_kernel(near, own, far, *refs):
    reg = refs[-1]
    out_ref = refs[-2]
    near_refs, refs = refs[: len(near)], refs[len(near) :]
    own_refs, far_refs = refs[: len(own)], refs[len(own) : len(own) + len(far)]
    even = even_column()

    def block(pieces, sources, at, channel):
        first, rows, sides = pieces[at]
        return kept(sources[at][channel, first : first + rows, :], *sides)

    row = 0
    for n, (_, rows, _) in enumerate(own):
        for channel in range(2):
            span = slice(row, row + rows)
            one = block(near, near_refs, n, channel)
            other = block(far, far_refs, n, channel)
            reg[channel, span, LANE : 4 * LANE] = block(own, own_refs, n, channel)
            reg[channel, span, :LANE] = jnp.where(even, other, one)
            reg[channel, span, 4 * LANE :] = jnp.where(even, one, other)
        row += rows

    def chunk(step, _):
        base = pl.multiple_of(step * 32, 8)
        flows = []
        power = tv_smooth
        for channel in range(2):
            block = reg[channel, pl.ds(base, 48), :]
            down = pltpu.roll(block, 47, 0) - block
            right = pltpu.roll(block, 5 * LANE - 1, 1) - block
            power = power + down * down + right * right
            flows.append((down, right))
        inverse = lax.rsqrt(power)
        for channel in range(2):
            down, right = flows[channel]
            down = down * inverse
            right = right * inverse
            change = pltpu.roll(down, 1, 0) - down + pltpu.roll(right, 1, 1) - right
            out_ref[channel, pl.ds(base, 32), :] = tv_weight * change[8:40, LANE : 4 * LANE]
        return 0

    lax.fori_loop(0, 6, chunk, 0)


def variation(near, own, far):
    parts = (near, own, far)
    plan = [
        tuple((p[1], p[2], p[3:] + border) for p in part) for part, border in zip(parts, ((), (), ("beside",)))
    ]
    operands = [piece[0] for part in parts for piece in part]
    return pl.pallas_call(
        functools.partial(variation_kernel, *plan),
        out_shape=jax.ShapeDtypeStruct((2, 192, 3 * LANE), F32),
        in_specs=vmem(len(operands)),
        out_specs=pl.BlockSpec(memory_space=pltpu.VMEM),
        scratch_shapes=[pltpu.VMEM((2, 208, 5 * LANE), F32)],
        cost_estimate=COST,
        compiler_params=pltpu.CompilerParams(vmem_limit_bytes=VMEM_LIMIT),
        name="variation",
    )(*operands)


def totals_kernel(outs, extras, own_ref, near_ref, far_ref, *refs):
    added, out_refs = refs[: len(extras)], refs[len(extras) :]
    even = even_column()
    for (first, rows), out in zip(outs, out_refs):
        cuts = {first, first + rows}
        for at, count, _ in extras:
            cuts |= {c for c in (at, at + count) if first < c < first + rows}
        cuts = sorted(cuts)
        for a, b in zip(cuts, cuts[1:]):
            for channel in range(2):
                value = own_ref[channel, a:b, :]
                for (at, count, source), ref in zip(extras, added):
                    if at <= a and b <= at + count:
                        value = value + ref[channel, source + a - at : source + b - at, :]
                to = slice(a - first, b - first)
                one = near_ref[channel, a:b, :]
                other = kept(far_ref[channel, a:b, :], "beside")
                out[channel, to, :LANE] = value[:, :LANE] + jnp.where(even, other, one)
                out[channel, to, LANE : 2 * LANE] = value[:, LANE : 2 * LANE]
                out[channel, to, 2 * LANE :] = value[:, 2 * LANE :] + jnp.where(even, one, other)


def totals(own, near, far, outs, extras):
    plan = tuple((at, rows, source) for _, source, at, rows in extras)
    return pl.pallas_call(
        functools.partial(totals_kernel, outs, plan),
        out_shape=tuple(jax.ShapeDtypeStruct((2, rows, own.shape[2]), F32) for _, rows in outs),
        in_specs=vmem(3 + len(extras)),
        out_specs=tuple(vmem(len(outs))),
        cost_estimate=COST,
        compiler_params=pltpu.CompilerParams(vmem_limit_bytes=VMEM_LIMIT),
        name="totals",
    )(own, near, far, *[extra[0] for extra in extras])


def update_kernel(pieces, side, *refs):
    new, near, far = refs[-3:]
    even = even_column()
    ins = refs[:-3]
    row = 0
    for which, first, rows, grads, masked in pieces:
        for channel in range(2):
            total = None
            for grad, at in grads:
                term = ins[grad][channel, at : at + rows, :]
                if grad == len(ins) - 1:
                    term = kept(term, side)
                total = term if total is None else total + term
            value = ins[which][channel, first : first + rows, :] - step_size * total
            if masked:
                value = kept(value, side)
            new[channel, row : row + rows, :] = value
            near[channel, row : row + rows, :] = jnp.where(even, value[:, 2 * LANE :], value[:, :LANE])
            far[channel, row : row + rows, :] = jnp.where(even, value[:, :LANE], value[:, 2 * LANE :])
        row += rows


def update(operands, pieces, side):
    rows = sum(piece[2] for piece in pieces)
    shape = [jax.ShapeDtypeStruct((2, rows, width), F32) for width in (3 * LANE, LANE, LANE)]
    return pl.pallas_call(
        functools.partial(update_kernel, pieces, side),
        out_shape=tuple(shape),
        in_specs=vmem(len(operands)),
        out_specs=tuple(vmem(3)),
        cost_estimate=COST,
        compiler_params=pltpu.CompilerParams(vmem_limit_bytes=VMEM_LIMIT),
        name="update",
    )(*operands)


def near_kernel(own_ref, near_ref, out_ref):
    even = even_column()
    for channel in range(2):
        strip = near_ref[channel]
        out_ref[channel, :, :LANE] = own_ref[channel, :, :LANE] + jnp.where(even, 0.0, strip)
        out_ref[channel, :, LANE : 2 * LANE] = own_ref[channel, :, LANE : 2 * LANE]
        out_ref[channel, :, 2 * LANE :] = own_ref[channel, :, 2 * LANE :] + jnp.where(even, strip, 0.0)


def sums_near(own, near):
    return (
        pl.pallas_call(
            near_kernel,
            out_shape=jax.ShapeDtypeStruct(own.shape, F32),
            in_specs=vmem(2),
            out_specs=pl.BlockSpec(memory_space=pltpu.VMEM),
            cost_estimate=COST,
            compiler_params=pltpu.CompilerParams(vmem_limit_bytes=VMEM_LIMIT),
            name="sums_near",
        )(own, near),
    )


def finish_kernel(top_ref, bottom_ref, mid_ref, low_ref, above_ref, below_ref, corner_ref, out_ref):
    for channel in range(2):
        above = mid_ref[channel, :MARGIN, :] + kept(above_ref[channel], "above")
        out_ref[channel, :MARGIN, :] = top_ref[channel, MARGIN:, :] - step_size * above
        out_ref[channel, MARGIN:288, :] = bottom_ref[channel, :192, :] - step_size * mid_ref[channel, MARGIN:, :]
        base = bottom_ref[channel, 192:288, :] - step_size * (low_ref[channel] + kept(below_ref[channel], "below"))
        corner = step_size * kept(corner_ref[channel], "below", "beside")
        even = even_column()
        out_ref[channel, 288:, :LANE] = base[:, :LANE] - jnp.where(even, corner, 0.0)
        out_ref[channel, 288:, LANE : 2 * LANE] = base[:, LANE : 2 * LANE]
        out_ref[channel, 288:, 2 * LANE :] = base[:, 2 * LANE :] - jnp.where(even, 0.0, corner)


def finish(*operands):
    return pl.pallas_call(
        finish_kernel,
        out_shape=jax.ShapeDtypeStruct((2, 3 * LANE, 3 * LANE), F32),
        in_specs=vmem(len(operands)),
        out_specs=pl.BlockSpec(memory_space=pltpu.VMEM),
        cost_estimate=COST,
        compiler_params=pltpu.CompilerParams(vmem_limit_bytes=VMEM_LIMIT),
        name="finish",
    )(*operands)


def moved(block, axis, distance):
    count = lax.axis_size(axis)
    return lax.ppermute(block, axis, [(n, (n + distance) % count) for n in range(count)])


def to_near(block):
    rows, cols = lax.axis_size("row"), lax.axis_size("col")
    return lax.ppermute(block, ("row", "col"), [(r * cols + c, r * cols + (c ^ 1)) for r in range(rows) for c in range(cols)])


def to_far(block, ends=True):
    rows, cols = lax.axis_size("row"), lax.axis_size("col")
    route = []
    for r in range(rows):
        for c in range(cols):
            other = c - 1 if c % 2 == 0 else c + 1
            if ends or 0 <= other < cols:
                route.append((r * cols + c, r * cols + other % cols))
    return lax.ppermute(block, ("row", "col"), route)


def to_far_above(block):
    rows, cols = lax.axis_size("row"), lax.axis_size("col")
    route = []
    for r in range(rows):
        for c in range(cols):
            other = c - 1 if c % 2 == 0 else c + 1
            route.append((r * cols + c, (r - 1) % rows * cols + other % cols))
    return lax.ppermute(block, ("row", "col"), route)


def edges(block):
    width = block.shape[2]
    low, high = block[:, :, :LANE], block[:, :, width - LANE :]
    even = even_column()
    return jnp.where(even, high, low), jnp.where(even, low, high)


def on_device(table, twiddle, order, object_field, probe, amplitudes, offsets):
    tile = object_field.shape[1]
    last = tile - MARGIN
    band = 2 * MARGIN
    obj = object_field
    after = lax.optimization_barrier

    top = moved(obj[:, last:, :], "row", 1)
    near_strip, far_strip = edges(obj)
    far, near = to_far(far_strip), to_near(near_strip)
    held, top = after((obj, top))
    bottom = moved(held[:, :MARGIN, :], "row", -1)
    probes, amps = prepare(offsets, probe, amplitudes, order)
    consts = (offsets, table, twiddle, probes, amps)

    near_strip, far_strip = edges(top)
    top_b, top_a = to_far(far_strip), to_near(near_strip)
    own = [(top, 0, MARGIN, "above"), (obj, 0, last)]
    halves = ((0, band), (band, band))
    lo_o, lo_a, mid_o, mid_a = window(
        0, True, consts, [(top_a, 0, MARGIN, "above"), (near, 0, last)], own, [], [], halves
    )
    in_a = to_near(lo_a)
    lo_o, lo_b, mid_o, mid_b = window(
        0, False, consts, [(top_b, 0, MARGIN, "above"), (far, 0, last)], own, [(lo_o, 0), (mid_o, band)], [], halves
    )
    in_b = to_far(lo_b)
    bottom, lo_b = after((bottom, lo_b))
    near_strip, far_strip = edges(bottom)
    bot_b = to_far(far_strip)
    bot_a = to_near(near_strip)
    tv_top = variation(
        [(top_a, 88, 8, "above"), (near, 0, 200)],
        [(top, 88, 8, "above"), (obj, 0, 200)],
        [(top_b, 88, 8, "above"), (far, 0, 200)],
    )
    (top_sum,) = totals(lo_o, in_a, in_b, ((0, band),), [(tv_top, 0, MARGIN, MARGIN)])
    from_below = moved(top_sum, "row", -1)

    mid_o, top_sum = after((mid_o, top_sum))
    own = [(obj, MARGIN, last), (bottom, 0, MARGIN, "below")]
    whole = ((0, tile),)
    hi_o, hi_b = window(
        1, False, consts, [(far, MARGIN, last), (bot_b, 0, MARGIN, "below")], own, [(mid_o, 0)], [(mid_b, 0)], whole,
    )
    in_b = to_far(hi_b, ends=False)
    hi_o, hi_a = window(
        1, True, consts, [(near, MARGIN, last), (bot_a, 0, MARGIN, "below")], own, [(hi_o, 0)], [(mid_a, 0)], whole,
    )
    in_a = to_near(hi_a)
    tv_bottom = variation(
        [(near, 184, 200), (bot_a, 0, 8, "below")],
        [(obj, 184, 200), (bottom, 0, 8, "below")],
        [(far, 184, 200), (bot_b, 0, 8, "below")],
    )
    mid_sum, bot_sum = totals(
        hi_o, in_a, in_b, halves, [(tv_top, MARGIN, 0, MARGIN), (tv_bottom, 0, MARGIN, band)]
    )
    from_above = moved(bot_sum, "row", 1)

    low, near_strip, far_strip = update(
        (obj, bottom, mid_sum, bot_sum, from_below),
        (
            (0, MARGIN, band, ((2, 0),), False),
            (0, last, MARGIN, ((3, 0), (4, 0)), False),
            (1, 0, MARGIN, ((3, MARGIN), (4, MARGIN)), True),
        ),
        "below",
    )
    low_a, low_b = to_near(near_strip), to_far(far_strip, ends=False)
    own = [(low, 0, tile)]
    mid_o, mid_a, hi_o, hi_a = window(1, True, consts, [(low_a, 0, tile)], own, [], [], halves)
    in_a = to_near(hi_a)
    mid_o, mid_b, hi_o, hi_b = window(
        1, False, consts, [(low_b, 0, tile)], own, [(mid_o, 0), (hi_o, band)], [], halves
    )
    hi_in_b = to_far(hi_b)
    hi_in_a = in_a
    tv_bottom = variation([(low_a, 88, 208)], [(low, 88, 208)], [(low_b, 88, 208)])
    top, hi_b = after((top, hi_b))
    up, near_strip, far_strip = update(
        (top, obj, top_sum, from_above),
        (
            (0, 0, MARGIN, ((2, 0), (3, 0)), True),
            (1, 0, MARGIN, ((2, MARGIN), (3, MARGIN)), False),
        ),
        "above",
    )
    up_b, up_a = to_far(far_strip), to_near(near_strip)
    own = [(up, 0, band), (low, 0, band)]
    cut = ((0, MARGIN), (MARGIN, last))
    over_o, over_a, lo_o, lo_a = window(
        0, True, consts, [(up_a, 0, band), (low_a, 0, band)], own, [(mid_o, band)], [(mid_a, band)], cut
    )
    over_a, in_a = to_near(over_a), to_near(lo_a)
    lo_o, hi_o = after((lo_o, hi_o))
    low_sum, over = totals(
        hi_o, hi_in_a, hi_in_b, ((0, MARGIN), (MARGIN, MARGIN)), [(tv_bottom, MARGIN, 0, MARGIN)]
    )
    lo_o, over = after((lo_o, over))
    last_above = moved(over, "row", 1)
    over_o, over_b, lo_o, lo_b = window(
        0, False, consts, [(up_b, 0, band), (low_b, 0, band)], own, [(over_o, 0), (lo_o, MARGIN)], [(mid_b, band)], cut,
    )
    corner = to_far_above(over_b)
    (over,) = sums_near(over_o, over_a)
    last_below = moved(over, "row", -1)
    in_b = to_far(lo_b, ends=False)
    tv_top = variation(
        [(up_a, 88, 104), (low_a, 0, 104)], [(up, 88, 104), (low, 0, 104)], [(up_b, 88, 104), (low_b, 0, 104)]
    )
    (mid_sum,) = totals(lo_o, in_a, in_b, ((0, last),), [(tv_top, 0, 0, band), (tv_bottom, 0, band, MARGIN)])
    return finish(up, low, mid_sum, low_sum, last_above, last_below, corner)


def solution(mesh):
    table, twiddle, order = tables()
    body = jax.shard_map(
        on_device,
        mesh=mesh,
        in_specs=(P(), P(), P(), P(None, "row", "col"), P(), P("row", "col"), P("row", "col", None)),
        out_specs=P(None, "row", "col"),
        check_vma=False,
    )

    def step(object_field, probe, amplitudes, offsets):
        return body(table, twiddle, order, object_field, probe, amplitudes, offsets)

    return step
```

```python
import functools
import math

import jax
import jax.numpy as jnp
import numpy as np
from jax import lax
from jax.experimental import pallas as pl
from jax.experimental.pallas import tpu as pltpu
from jax.sharding import PartitionSpec as P


WIN = 256
HALF = 128
MARGIN = 96
LANE = 128
COST = pl.CostEstimate(flops=100_000, bytes_accessed=100_000, transcendentals=0)
VMEM_LIMIT = 24 * 1024 * 1024

step_size = 0.3
tv_weight = 0.2
tv_smooth = 0.1
amp_floor = 0.5

F32 = jnp.float32
BF16 = jnp.bfloat16


def tables():
    counter = np.arange(HALF)
    angle = (counter[:, None] * counter[None, :] % HALF) * (2.0 * math.pi / HALF)
    cosine = np.cos(angle) / math.sqrt(WIN)
    sine = np.sin(angle) / math.sqrt(WIN)
    first = np.block([[cosine, sine], [-sine, cosine]])
    second = np.block([[cosine, -sine], [sine, cosine]])
    parts = []
    for table in (first, second):
        table = table.astype(np.float32)
        high = table.astype(jnp.bfloat16)
        low = (table - high.astype(np.float32)).astype(jnp.bfloat16)
        parts += [high, low]
    turn = counter * (2.0 * math.pi / WIN)
    rows = np.stack([np.cos(turn), np.sin(turn)])
    by_row = np.broadcast_to(rows[:, :, None], (2, HALF, HALF))
    by_lane = np.broadcast_to(rows[:, None, :], (2, HALF, HALF))
    twiddle = np.concatenate([by_row, by_lane]).astype(np.float32)
    order = np.zeros((WIN, WIN), np.float32)
    for parity in range(2):
        order[2 * counter + parity, parity * HALF + counter] = 1.0
    return np.stack(parts), twiddle, order.astype(jnp.bfloat16)


def split(value):
    high = value.astype(BF16)
    return high, (value - high.astype(F32)).astype(BF16)


def has(side):
    if side == "above":
        return lax.axis_index("row") > 0
    if side == "below":
        return lax.axis_index("row") < lax.axis_size("row") - 1
    return (lax.axis_index("col") > 0) & (lax.axis_index("col") < lax.axis_size("col") - 1)


def even_column():
    return lax.axis_index("col") % 2 == 0


def kept(value, *sides):
    for side in sides:
        value = jnp.where(has(side), value, 0.0)
    return value


def mul(left, right):
    return jnp.dot(left, right, preferred_element_type=F32)


def vmem(count):
    return [pl.BlockSpec(memory_space=pltpu.VMEM)] * count


def prepare_kernel(off_ref, probe_ref, amp_ref, order_ref, probes_ref, amps_ref, parts_ref):
    order = order_ref[...]
    for i in range(2):
        for j in range(2):
            row = off_ref[i, j, 0]
            col = (off_ref[i, j, 1] + (32 if j == 0 else 224)) % WIN
            for channel in range(2):
                turned = pltpu.roll(probe_ref[channel], row, 0)
                probes_ref[2 * i + j, channel] = pltpu.roll(turned, col, 1)
            amp = amp_ref[i * WIN : (i + 1) * WIN, j * WIN : (j + 1) * WIN]
            high, rest = split(amp)
            middle, _ = split(amp - high.astype(F32) - rest.astype(F32))
            sorted_lanes = mul(high, order) + mul(rest, order) + mul(middle, order)
            for q in range(2):
                parts_ref[...] = sorted_lanes[:, q * HALF : (q + 1) * HALF]
                for p in range(2):
                    at = q * WIN + p * HALF
                    amps_ref[2 * i + j, at : at + HALF, :] = parts_ref[pl.ds(p, HALF, stride=2), :]


def prepare(offsets, probe, amplitudes, order):
    return pl.pallas_call(
        prepare_kernel,
        out_shape=(
            jax.ShapeDtypeStruct((4, 2, WIN, WIN), F32),
            jax.ShapeDtypeStruct((4, 2 * WIN, HALF), F32),
        ),
        in_specs=[pl.BlockSpec(memory_space=pltpu.SMEM)] + vmem(3),
        out_specs=tuple(vmem(2)),
        scratch_shapes=[pltpu.VMEM((WIN, HALF), F32)],
        cost_estimate=COST,
        compiler_params=pltpu.CompilerParams(vmem_limit_bytes=VMEM_LIMIT),
        name="prepare",
    )(offsets, probe, amplitudes, order)


def rows_of(pieces, refs, first, rows):
    found, at = [], 0
    for ref, (start, count, sides) in zip(refs, pieces):
        lo, hi = max(first, at), min(first + rows, at + count)
        if lo < hi:
            found.append((ref, start + lo - at, hi - lo, sides))
        at += count
    return found


def window_kernel(i, near, side, own, carried_own, carried_side, outs, *refs):
    off_ref, tab_ref, tw_ref, probes_ref, amps_ref = refs[:5]
    refs = refs[5:]
    side_refs, refs = refs[: len(side)], refs[len(side) :]
    own_refs, refs = refs[: len(own)], refs[len(own) :]
    sum_refs, refs = refs[: len(carried_own)], refs[len(carried_own) :]
    strip_refs, refs = refs[: len(carried_side)], refs[len(carried_side) :]
    out_refs, refs = refs[: 2 * len(outs)], refs[2 * len(outs) :]
    halves = [refs[n : n + 2] for n in range(0, 16, 2)]
    g_in, h_in, m_in, g_out = halves[0:2], halves[2:4], halves[4:6], halves[6:8]
    wide, tall, tall_back, wide_back = refs[16:18], refs[18:20], refs[20:22], refs[22:24]

    to_right = even_column() if near else jnp.logical_not(even_column())
    j = jnp.where(to_right, 1, 0)
    number = 2 * i + j
    row_start = off_ref[i, j, 0]
    col_start = off_ref[i, j, 1]
    row_iota = lax.broadcasted_iota(jnp.int32, (HALF, HALF), 0)
    lane_iota = lax.broadcasted_iota(jnp.int32, (HALF, HALF), 1)
    in_row = row_iota >= row_start
    sign = jnp.where(to_right, -1, 1)
    in_first = (
        sign * lane_iota >= jnp.where(to_right, 33 - col_start, 32 + col_start),
        lane_iota >= jnp.where(to_right, 96 + col_start, col_start - 96),
    )
    first_h, first_l, second_h, second_l = (tab_ref.at[n] for n in range(4))
    groups = (("strip", 1), (0, 2))

    def place(group):
        if group == "strip":
            return True, slice(0, LANE)
        return False, slice(group * LANE, (group + 1) * LANE)

    def load(channel, first, group):
        is_strip, lanes = place(group)
        pieces, sources = (side, side_refs) if is_strip else (own, own_refs)
        blocks = [
            kept(ref[channel, at : at + rows, lanes], *sides)
            for ref, at, rows, sides in rows_of(pieces, sources, first, HALF)
        ]
        return blocks[0] if len(blocks) == 1 else jnp.concatenate(blocks, axis=0)

    def emit(channel, first, group, value):
        is_strip, lanes = place(group)
        extra = (carried_side, strip_refs) if is_strip else (carried_own, sum_refs)
        which = 1 if is_strip else 0
        for n, (start, count) in enumerate(outs):
            lo, hi = max(first, start), min(first + HALF, start + count)
            if lo >= hi:
                continue
            cuts = sorted({lo, hi} | {c for at, rows in extra[0] for c in (at, at + rows) if lo < c < hi})
            for a, b in zip(cuts, cuts[1:]):
                part = value[a - first : b - first]
                for (at, rows), ref in zip(*extra):
                    if at <= a and b <= at + rows:
                        part = part + ref[channel, a - at : b - at, lanes]
                out_refs[2 * n + which][channel, a - start : b - start, lanes] = part

    def store_split(pair, rows, lanes, value):
        high, low = split(value)
        pair[0][rows, lanes] = high
        pair[1][rows, lanes] = low

    lo, hi = slice(0, HALF), slice(HALF, WIN)
    tw_c, tw_s = tw_ref[0], tw_ref[1]
    for cb in range(2):
        in_col = in_first[cb]
        first_group, second_group = groups[cb]
        field = []
        for rb in range(2):
            value = []
            for channel in range(2):
                at = rb * HALF
                picked = jnp.where(in_col, load(channel, at, first_group), load(channel, at, second_group))
                if rb == 0:
                    other = jnp.where(in_col, load(channel, WIN, first_group), load(channel, WIN, second_group))
                    picked = jnp.where(in_row, picked, other)
                value.append(picked)
            box = (slice(rb * HALF, (rb + 1) * HALF), slice(cb * LANE, (cb + 1) * LANE))
            p_re = probes_ref[(number, 0) + box]
            p_im = probes_ref[(number, 1) + box]
            field.append((p_re * value[0] - p_im * value[1], p_re * value[1] + p_im * value[0]))
        (re0, im0), (re1, im1) = field
        store_split(g_in[cb], lo, lo, re0 + re1)
        store_split(g_in[cb], hi, lo, im0 + im1)
        d_re = re0 - re1
        d_im = im0 - im1
        store_split(g_in[cb], lo, hi, d_re * tw_c + d_im * tw_s)
        store_split(g_in[cb], hi, hi, d_im * tw_c - d_re * tw_s)
        high, low = g_in[cb][0][...], g_in[cb][1][...]
        wide[cb][...] = mul(first_h[...], high) + mul(first_h[...], low) + mul(first_l[...], high)

    for p in range(2):
        tl_c, tl_s = tw_ref[2], tw_ref[3]
        cols = slice(p * HALF, (p + 1) * HALF)
        re0, re1 = wide[0][lo, cols], wide[1][lo, cols]
        im0, im1 = wide[0][hi, cols], wide[1][hi, cols]
        store_split(h_in[p], lo, lo, re0 + re1)
        store_split(h_in[p], lo, hi, im0 + im1)
        d_re = re0 - re1
        d_im = im0 - im1
        store_split(h_in[p], hi, lo, d_re * tl_c + d_im * tl_s)
        store_split(h_in[p], hi, hi, d_im * tl_c - d_re * tl_s)
        high, low = h_in[p][0][...], h_in[p][1][...]
        tall[p][...] = mul(high, second_h[...]) + mul(low, second_h[...]) + mul(high, second_l[...])

    for p in range(2):
        for q, rows in enumerate((lo, hi)):
            re, im = tall[p][rows, lo], tall[p][rows, hi]
            power = jnp.maximum(re * re + im * im, amp_floor * amp_floor)
            at = q * WIN + p * HALF
            keeping = 1.0 - amps_ref[number, at : at + HALF, :] * lax.rsqrt(power)
            store_split(m_in[p], rows, lo, re * keeping)
            store_split(m_in[p], rows, hi, im * keeping)
        high, low = m_in[p][0][...], m_in[p][1][...]
        tall_back[p][...] = mul(high, first_h[...]) + mul(low, first_h[...]) + mul(high, first_l[...])

    for p in range(2):
        tl_c, tl_s = tw_ref[2], tw_ref[3]
        u_re, u_im = tall_back[p][lo, lo], tall_back[p][lo, hi]
        v_re, v_im = tall_back[p][hi, lo], tall_back[p][hi, hi]
        w_re = v_re * tl_c - v_im * tl_s
        w_im = v_im * tl_c + v_re * tl_s
        store_split(g_out[p], lo, lo, u_re + w_re)
        store_split(g_out[p], lo, hi, u_re - w_re)
        store_split(g_out[p], hi, lo, u_im + w_im)
        store_split(g_out[p], hi, hi, u_im - w_im)
        high, low = g_out[p][0][...], g_out[p][1][...]
        wide_back[p][...] = mul(second_h[...], high) + mul(second_h[...], low) + mul(second_l[...], high)

    for cb in range(2):
        in_col = in_first[cb]
        first_group, second_group = groups[cb]
        cols = slice(cb * LANE, (cb + 1) * LANE)
        u_re, u_im = wide_back[0][lo, cols], wide_back[0][hi, cols]
        v_re, v_im = wide_back[1][lo, cols], wide_back[1][hi, cols]
        w_re = v_re * tw_c - v_im * tw_s
        w_im = v_im * tw_c + v_re * tw_s
        for rb in range(2):
            b_re = u_re + w_re if rb == 0 else u_re - w_re
            b_im = u_im + w_im if rb == 0 else u_im - w_im
            box = (slice(rb * HALF, (rb + 1) * HALF), cols)
            p_re = probes_ref[(number, 0) + box]
            p_im = probes_ref[(number, 1) + box]
            grads = (p_re * b_re + p_im * b_im, p_re * b_im - p_im * b_re)
            for channel in range(2):
                grad = grads[channel]
                targets = [(rb * HALF, grad)]
                if rb == 0:
                    targets = [(0, jnp.where(in_row, grad, 0.0)), (WIN, jnp.where(in_row, 0.0, grad))]
                for at, piece in targets:
                    emit(channel, at, first_group, jnp.where(in_col, piece, 0.0))
                    emit(channel, at, second_group, jnp.where(in_col, 0.0, piece))


def window(i, near, consts, side, own, carried_own, carried_side, outs):
    border = () if near else ("beside",)
    own_width = 3 * LANE
    shapes = []
    for _, rows in outs:
        shapes += [jax.ShapeDtypeStruct((2, rows, width), F32) for width in (own_width, LANE)]
    operands = [piece[0] for piece in list(side) + list(own) + list(carried_own) + list(carried_side)]
    kernel = functools.partial(
        window_kernel,
        i,
        near,
        tuple((p[1], p[2], p[3:] + border) for p in side),
        tuple((p[1], p[2], p[3:]) for p in own),
        tuple((at, array.shape[1]) for array, at in carried_own),
        tuple((at, array.shape[1]) for array, at in carried_side),
        outs,
    )
    return pl.pallas_call(
        kernel,
        out_shape=tuple(shapes),
        in_specs=[pl.BlockSpec(memory_space=pltpu.SMEM)] + vmem(4 + len(operands)),
        out_specs=tuple(vmem(len(shapes))),
        scratch_shapes=[pltpu.VMEM((WIN, WIN), BF16)] * 16 + [pltpu.VMEM((WIN, WIN), F32)] * 8,
        cost_estimate=COST,
        compiler_params=pltpu.CompilerParams(vmem_limit_bytes=VMEM_LIMIT),
    )(*consts, *operands)


def variation_kernel(near, own, far, *refs):
    reg = refs[-1]
    out_ref = refs[-2]
    near_refs, refs = refs[: len(near)], refs[len(near) :]
    own_refs, far_refs = refs[: len(own)], refs[len(own) : len(own) + len(far)]
    even = even_column()

    def block(pieces, sources, at, channel):
        first, rows, sides = pieces[at]
        return kept(sources[at][channel, first : first + rows, :], *sides)

    row = 0
    for n, (_, rows, _) in enumerate(own):
        for channel in range(2):
            span = slice(row, row + rows)
            one = block(near, near_refs, n, channel)
            other = block(far, far_refs, n, channel)
            reg[channel, span, LANE : 4 * LANE] = block(own, own_refs, n, channel)
            reg[channel, span, :LANE] = jnp.where(even, other, one)
            reg[channel, span, 4 * LANE :] = jnp.where(even, one, other)
        row += rows

    def chunk(step, _):
        base = pl.multiple_of(step * 32, 8)
        flows = []
        power = tv_smooth
        for channel in range(2):
            block = reg[channel, pl.ds(base, 48), :]
            down = pltpu.roll(block, 47, 0) - block
            right = pltpu.roll(block, 5 * LANE - 1, 1) - block
            power = power + down * down + right * right
            flows.append((down, right))
        inverse = lax.rsqrt(power)
        for channel in range(2):
            down, right = flows[channel]
            down = down * inverse
            right = right * inverse
            change = pltpu.roll(down, 1, 0) - down + pltpu.roll(right, 1, 1) - right
            out_ref[channel, pl.ds(base, 32), :] = tv_weight * change[8:40, LANE : 4 * LANE]
        return 0

    lax.fori_loop(0, 6, chunk, 0)


def variation(near, own, far):
    parts = (near, own, far)
    plan = [
        tuple((p[1], p[2], p[3:] + border) for p in part) for part, border in zip(parts, ((), (), ("beside",)))
    ]
    operands = [piece[0] for part in parts for piece in part]
    return pl.pallas_call(
        functools.partial(variation_kernel, *plan),
        out_shape=jax.ShapeDtypeStruct((2, 192, 3 * LANE), F32),
        in_specs=vmem(len(operands)),
        out_specs=pl.BlockSpec(memory_space=pltpu.VMEM),
        scratch_shapes=[pltpu.VMEM((2, 208, 5 * LANE), F32)],
        cost_estimate=COST,
        compiler_params=pltpu.CompilerParams(vmem_limit_bytes=VMEM_LIMIT),
        name="variation",
    )(*operands)


def totals_kernel(outs, extras, own_ref, near_ref, far_ref, *refs):
    added, out_refs = refs[: len(extras)], refs[len(extras) :]
    even = even_column()
    for (first, rows), out in zip(outs, out_refs):
        cuts = {first, first + rows}
        for at, count, _ in extras:
            cuts |= {c for c in (at, at + count) if first < c < first + rows}
        cuts = sorted(cuts)
        for a, b in zip(cuts, cuts[1:]):
            for channel in range(2):
                value = own_ref[channel, a:b, :]
                for (at, count, source), ref in zip(extras, added):
                    if at <= a and b <= at + count:
                        value = value + ref[channel, source + a - at : source + b - at, :]
                to = slice(a - first, b - first)
                one = near_ref[channel, a:b, :]
                other = kept(far_ref[channel, a:b, :], "beside")
                out[channel, to, :LANE] = value[:, :LANE] + jnp.where(even, other, one)
                out[channel, to, LANE : 2 * LANE] = value[:, LANE : 2 * LANE]
                out[channel, to, 2 * LANE :] = value[:, 2 * LANE :] + jnp.where(even, one, other)


def totals(own, near, far, outs, extras):
    plan = tuple((at, rows, source) for _, source, at, rows in extras)
    return pl.pallas_call(
        functools.partial(totals_kernel, outs, plan),
        out_shape=tuple(jax.ShapeDtypeStruct((2, rows, own.shape[2]), F32) for _, rows in outs),
        in_specs=vmem(3 + len(extras)),
        out_specs=tuple(vmem(len(outs))),
        cost_estimate=COST,
        compiler_params=pltpu.CompilerParams(vmem_limit_bytes=VMEM_LIMIT),
        name="totals",
    )(own, near, far, *[extra[0] for extra in extras])


def update_kernel(pieces, side, *refs):
    new, near, far = refs[-3:]
    even = even_column()
    ins = refs[:-3]
    row = 0
    for which, first, rows, grads, masked in pieces:
        for channel in range(2):
            total = None
            for grad, at in grads:
                term = ins[grad][channel, at : at + rows, :]
                if grad == len(ins) - 1:
                    term = kept(term, side)
                total = term if total is None else total + term
            value = ins[which][channel, first : first + rows, :] - step_size * total
            if masked:
                value = kept(value, side)
            new[channel, row : row + rows, :] = value
            near[channel, row : row + rows, :] = jnp.where(even, value[:, 2 * LANE :], value[:, :LANE])
            far[channel, row : row + rows, :] = jnp.where(even, value[:, :LANE], value[:, 2 * LANE :])
        row += rows


def update(operands, pieces, side):
    rows = sum(piece[2] for piece in pieces)
    shape = [jax.ShapeDtypeStruct((2, rows, width), F32) for width in (3 * LANE, LANE, LANE)]
    return pl.pallas_call(
        functools.partial(update_kernel, pieces, side),
        out_shape=tuple(shape),
        in_specs=vmem(len(operands)),
        out_specs=tuple(vmem(3)),
        cost_estimate=COST,
        compiler_params=pltpu.CompilerParams(vmem_limit_bytes=VMEM_LIMIT),
        name="update",
    )(*operands)


def near_kernel(own_ref, near_ref, out_ref):
    even = even_column()
    for channel in range(2):
        strip = near_ref[channel]
        out_ref[channel, :, :LANE] = own_ref[channel, :, :LANE] + jnp.where(even, 0.0, strip)
        out_ref[channel, :, LANE : 2 * LANE] = own_ref[channel, :, LANE : 2 * LANE]
        out_ref[channel, :, 2 * LANE :] = own_ref[channel, :, 2 * LANE :] + jnp.where(even, strip, 0.0)


def sums_near(own, near):
    return (
        pl.pallas_call(
            near_kernel,
            out_shape=jax.ShapeDtypeStruct(own.shape, F32),
            in_specs=vmem(2),
            out_specs=pl.BlockSpec(memory_space=pltpu.VMEM),
            cost_estimate=COST,
            compiler_params=pltpu.CompilerParams(vmem_limit_bytes=VMEM_LIMIT),
            name="sums_near",
        )(own, near),
    )


def finish_kernel(top_ref, bottom_ref, mid_ref, low_ref, above_ref, below_ref, corner_ref, out_ref):
    for channel in range(2):
        above = mid_ref[channel, :MARGIN, :] + kept(above_ref[channel], "above")
        out_ref[channel, :MARGIN, :] = top_ref[channel, MARGIN:, :] - step_size * above
        out_ref[channel, MARGIN:288, :] = bottom_ref[channel, :192, :] - step_size * mid_ref[channel, MARGIN:, :]
        base = bottom_ref[channel, 192:288, :] - step_size * (low_ref[channel] + kept(below_ref[channel], "below"))
        corner = step_size * kept(corner_ref[channel], "below", "beside")
        even = even_column()
        out_ref[channel, 288:, :LANE] = base[:, :LANE] - jnp.where(even, corner, 0.0)
        out_ref[channel, 288:, LANE : 2 * LANE] = base[:, LANE : 2 * LANE]
        out_ref[channel, 288:, 2 * LANE :] = base[:, 2 * LANE :] - jnp.where(even, 0.0, corner)


def finish(*operands):
    return pl.pallas_call(
        finish_kernel,
        out_shape=jax.ShapeDtypeStruct((2, 3 * LANE, 3 * LANE), F32),
        in_specs=vmem(len(operands)),
        out_specs=pl.BlockSpec(memory_space=pltpu.VMEM),
        cost_estimate=COST,
        compiler_params=pltpu.CompilerParams(vmem_limit_bytes=VMEM_LIMIT),
        name="finish",
    )(*operands)


def moved(block, axis, distance):
    count = lax.axis_size(axis)
    return lax.ppermute(block, axis, [(n, (n + distance) % count) for n in range(count)])


def to_near(block):
    rows, cols = lax.axis_size("row"), lax.axis_size("col")
    return lax.ppermute(block, ("row", "col"), [(r * cols + c, r * cols + (c ^ 1)) for r in range(rows) for c in range(cols)])


def to_far(block, ends=True):
    rows, cols = lax.axis_size("row"), lax.axis_size("col")
    route = []
    for r in range(rows):
        for c in range(cols):
            other = c - 1 if c % 2 == 0 else c + 1
            if ends or 0 <= other < cols:
                route.append((r * cols + c, r * cols + other % cols))
    return lax.ppermute(block, ("row", "col"), route)


def to_far_above(block):
    rows, cols = lax.axis_size("row"), lax.axis_size("col")
    route = []
    for r in range(rows):
        for c in range(cols):
            other = c - 1 if c % 2 == 0 else c + 1
            route.append((r * cols + c, (r - 1) % rows * cols + other % cols))
    return lax.ppermute(block, ("row", "col"), route)


def edges(block):
    width = block.shape[2]
    low, high = block[:, :, :LANE], block[:, :, width - LANE :]
    even = even_column()
    return jnp.where(even, high, low), jnp.where(even, low, high)


def on_device(table, twiddle, order, object_field, probe, amplitudes, offsets):
    tile = object_field.shape[1]
    last = tile - MARGIN
    band = 2 * MARGIN
    obj = object_field
    after = lax.optimization_barrier

    top = moved(obj[:, last:, :], "row", 1)
    near_strip, far_strip = edges(obj)
    far, near = to_far(far_strip), to_near(near_strip)
    up_rows, top = after((obj[:, :MARGIN, :], top))
    bottom = moved(up_rows, "row", -1)
    probes, amps = prepare(offsets, probe, amplitudes, order)
    consts = (offsets, table, twiddle, probes, amps)

    near_strip, far_strip = edges(top)
    top_b, top_a = to_far(far_strip), to_near(near_strip)
    own = [(top, 0, MARGIN, "above"), (obj, 0, last)]
    halves = ((0, band), (band, band))
    lo_o, lo_a, mid_o, mid_a = window(
        0, True, consts, [(top_a, 0, MARGIN, "above"), (near, 0, last)], own, [], [], halves
    )
    in_a = to_near(lo_a)
    lo_o, lo_b, mid_o, mid_b = window(
        0, False, consts, [(top_b, 0, MARGIN, "above"), (far, 0, last)], own, [(lo_o, 0), (mid_o, band)], [], halves
    )
    in_b = to_far(lo_b)
    bottom, lo_b = after((bottom, lo_b))
    near_strip, far_strip = edges(bottom)
    bot_b, bot_a = to_far(far_strip), to_near(near_strip)
    tv_top = variation(
        [(top_a, 88, 8, "above"), (near, 0, 200)],
        [(top, 88, 8, "above"), (obj, 0, 200)],
        [(top_b, 88, 8, "above"), (far, 0, 200)],
    )
    (top_sum,) = totals(lo_o, in_a, in_b, ((0, band),), [(tv_top, 0, MARGIN, MARGIN)])
    from_below = moved(top_sum, "row", -1)

    mid_o, top_sum = after((mid_o, top_sum))
    own = [(obj, MARGIN, last), (bottom, 0, MARGIN, "below")]
    whole = ((0, tile),)
    hi_o, hi_b = window(
        1, False, consts, [(far, MARGIN, last), (bot_b, 0, MARGIN, "below")], own, [(mid_o, 0)], [(mid_b, 0)], whole,
    )
    in_b = to_far(hi_b, ends=False)
    hi_o, hi_a = window(
        1, True, consts, [(near, MARGIN, last), (bot_a, 0, MARGIN, "below")], own, [(hi_o, 0)], [(mid_a, 0)], whole,
    )
    in_a = to_near(hi_a)
    tv_bottom = variation(
        [(near, 184, 200), (bot_a, 0, 8, "below")],
        [(obj, 184, 200), (bottom, 0, 8, "below")],
        [(far, 184, 200), (bot_b, 0, 8, "below")],
    )
    mid_sum, bot_sum = totals(
        hi_o, in_a, in_b, halves, [(tv_top, MARGIN, 0, MARGIN), (tv_bottom, 0, MARGIN, band)]
    )
    from_above = moved(bot_sum, "row", 1)

    low, near_strip, far_strip = update(
        (obj, bottom, mid_sum, bot_sum, from_below),
        (
            (0, MARGIN, band, ((2, 0),), False),
            (0, last, MARGIN, ((3, 0), (4, 0)), False),
            (1, 0, MARGIN, ((3, MARGIN), (4, MARGIN)), True),
        ),
        "below",
    )
    low_a, low_b = to_near(near_strip), to_far(far_strip, ends=False)
    own = [(low, 0, tile)]
    mid_o, mid_a, hi_o, hi_a = window(1, True, consts, [(low_a, 0, tile)], own, [], [], halves)
    in_a = to_near(hi_a)
    mid_o, mid_b, hi_o, hi_b = window(
        1, False, consts, [(low_b, 0, tile)], own, [(mid_o, 0), (hi_o, band)], [], halves
    )
    hi_in_b = to_far(hi_b)
    hi_in_a = in_a
    tv_bottom = variation([(low_a, 88, 208)], [(low, 88, 208)], [(low_b, 88, 208)])
    top, hi_b = after((top, hi_b))
    up, near_strip, far_strip = update(
        (top, obj, top_sum, from_above),
        (
            (0, 0, MARGIN, ((2, 0), (3, 0)), True),
            (1, 0, MARGIN, ((2, MARGIN), (3, MARGIN)), False),
        ),
        "above",
    )
    up_b, up_a = to_far(far_strip), to_near(near_strip)
    own = [(up, 0, band), (low, 0, band)]
    cut = ((0, MARGIN), (MARGIN, last))
    over_o, over_a, lo_o, lo_a = window(
        0, True, consts, [(up_a, 0, band), (low_a, 0, band)], own, [(mid_o, band)], [(mid_a, band)], cut
    )
    over_a, in_a = to_near(over_a), to_near(lo_a)
    lo_o, hi_o = after((lo_o, hi_o))
    low_sum, over = totals(
        hi_o, hi_in_a, hi_in_b, ((0, MARGIN), (MARGIN, MARGIN)), [(tv_bottom, MARGIN, 0, MARGIN)]
    )
    lo_o, over = after((lo_o, over))
    last_above = moved(over, "row", 1)
    over_o, over_b, lo_o, lo_b = window(
        0, False, consts, [(up_b, 0, band), (low_b, 0, band)], own, [(over_o, 0), (lo_o, MARGIN)], [(mid_b, band)], cut,
    )
    corner = to_far_above(over_b)
    (over,) = sums_near(over_o, over_a)
    last_below = moved(over, "row", -1)
    in_b = to_far(lo_b)
    tv_top = variation(
        [(up_a, 88, 104), (low_a, 0, 104)], [(up, 88, 104), (low, 0, 104)], [(up_b, 88, 104), (low_b, 0, 104)]
    )
    (mid_sum,) = totals(lo_o, in_a, in_b, ((0, last),), [(tv_top, 0, 0, band), (tv_bottom, 0, band, MARGIN)])
    return finish(up, low, mid_sum, low_sum, last_above, last_below, corner)


def solution(mesh):
    table, twiddle, order = tables()
    body = jax.shard_map(
        on_device,
        mesh=mesh,
        in_specs=(P(), P(), P(), P(None, "row", "col"), P(), P("row", "col"), P("row", "col", None)),
        out_specs=P(None, "row", "col"),
        check_vma=False,
    )

    def step(object_field, probe, amplitudes, offsets):
        return body(table, twiddle, order, object_field, probe, amplitudes, offsets)

    return step
```
